32 devices in a mesh: seq: 4 (over x, core), ctx: 4 (over z), fsdp: 2 (over y).
Axes of the slice: x: 2, y: 2, z: 4, core: 2. Of those that a mesh axis runs over, the one named last changes fastest.
Arguments:
- hidden_in: bfloat16 [8, 512, 768], P(('seq', 'fsdp'), 'ctx'), may hold values from -6 to 6
- encoder_states: bfloat16 [8, 64, 768], P(('seq', 'fsdp'), 'ctx'), may hold values from -6 to 6
- out_grad: bfloat16 [8, 512, 768], P(('seq', 'fsdp'), 'ctx'), may hold values from -6 to 6
- bucket_index: int32 [512], replicated, may hold values from 0 to 31, as said below
- bias_table: float32 [32, 12], replicated, may hold values from -5 to 5
- self_gain: bfloat16 [768], P(('ctx', 'fsdp')), may hold values from 0.099609375 to 1.8984375
- self_query: bfloat16 [768, 768], P(('ctx', 'fsdp')), may hold values from -0.02734375 to 0.02734375
- self_key: bfloat16 [768, 768], P(('ctx', 'fsdp')), may hold values from -0.21875 to 0.21875
- self_value: bfloat16 [768, 768], P(('ctx', 'fsdp')), may hold values from -0.21875 to 0.21875
- self_output: bfloat16 [768, 768], P(('ctx', 'fsdp')), may hold values from -1.5 to 1.5
- cross_gain: bfloat16 [768], P(('ctx', 'fsdp')), may hold values from 0.099609375 to 1.8984375
- cross_query: bfloat16 [768, 768], P(('ctx', 'fsdp')), may hold values from -0.02734375 to 0.02734375
- cross_key: bfloat16 [768, 768], P(('ctx', 'fsdp')), may hold values from -0.21875 to 0.21875
- cross_value: bfloat16 [768, 768], P(('ctx', 'fsdp')), may hold values from -0.21875 to 0.21875
- cross_output: bfloat16 [768, 768], P(('ctx', 'fsdp')), may hold values from -1.5 to 1.5
- feed_gain: bfloat16 [768], P(('ctx', 'fsdp')), may hold values from 0.099609375 to 1.8984375
- gate_weight: bfloat16 [768, 2048], P(('ctx', 'fsdp')), may hold values from -0.21875 to 0.21875
- linear_weight: bfloat16 [768, 2048], P(('ctx', 'fsdp')), may hold values from -0.21875 to 0.21875
- down_weight: bfloat16 [2048, 768], P(('ctx', 'fsdp')), may hold values from -0.125 to 0.125
Outputs:
- layer_out: bfloat16 [8, 512, 768], P(('seq', 'fsdp'), 'ctx')
- input_grad: float32 [8, 512, 768], P(('seq', 'fsdp'), 'ctx')
- encoder_grad: float32 [8, 64, 768], P(('seq', 'fsdp'), 'ctx')
- grad_bias_table: float32 [32, 12], replicated
- grad_self_gain: float32 [768], P(('ctx', 'fsdp'))
- grad_self_query: float32 [768, 768], P(('ctx', 'fsdp'))
- grad_self_key: float32 [768, 768], P(('ctx', 'fsdp'))
- grad_self_value: float32 [768, 768], P(('ctx', 'fsdp'))
- grad_self_output: float32 [768, 768], P(('ctx', 'fsdp'))
- grad_cross_gain: float32 [768], P(('ctx', 'fsdp'))
- grad_cross_query: float32 [768, 768], P(('ctx', 'fsdp'))
- grad_cross_key: float32 [768, 768], P(('ctx', 'fsdp'))
- grad_cross_value: float32 [768, 768], P(('ctx', 'fsdp'))
- grad_cross_output: float32 [768, 768], P(('ctx', 'fsdp'))
- grad_feed_gain: float32 [768], P(('ctx', 'fsdp'))
- grad_gate_weight: float32 [768, 2048], P(('ctx', 'fsdp'))
- grad_linear_weight: float32 [768, 2048], P(('ctx', 'fsdp'))
- grad_down_weight: float32 [2048, 768], P(('ctx', 'fsdp'))
The draws below stay inside these ranges and needn't reach their ends.
Inputs may be any that keep to these rules, and one draw needn't show every extreme that they name: bucket_index[d] is the bucket of a key that lies d positions before its query; it is 0 at d = 0 and never falls as d grows.
All inputs are finite; a program needn't handle non-finite values.
Results may differ from the reference program's by a relative error of at most 0.025.
Values may be sent and summed in bfloat16 or wider, within the bound.
A program may use at most 256 MiB of HBM per device.

```python
import math
import jax
import jax.numpy as jnp
from jax import lax

D = 768
HEADS = 12
FF = 2048
BUCKETS = 32
HEAD = 64
LEN = 512
ENC = 64
SEQS = 8


def draw_bucket_index(key, part):
    source = jax.random.fold_in(key, 5303)
    increments = jax.random.randint(source, (LEN - 1,), 0, 3).astype(jnp.int32)
    running = jnp.concatenate([jnp.zeros((1,), jnp.int32), jnp.cumsum(increments).astype(jnp.int32)])
    capped = jnp.minimum(running, BUCKETS - 1).astype(jnp.int32)
    distance = jnp.arange(LEN, dtype=jnp.int32)
    return jnp.where(distance == LEN - 1, BUCKETS - 1, capped).astype(jnp.int32)


def level_of(own_key, extent, shards, least, high):
    factor_of = 1.0
    for axis_at, blocks in shards:
        heights = jax.random.uniform(jax.random.fold_in(jax.random.fold_in(own_key, 6), axis_at), (blocks,), jnp.float32, least / len(shards), high / len(shards))
        factor_of = factor_of * jnp.repeat(jnp.exp(heights), extent[axis_at] // blocks).reshape((-1,) + (1,) * (len(extent) - 1 - axis_at))
    return factor_of


def gaussian(own_key, dims, deviation, reach, split=(), kind=jnp.bfloat16):
    factor_of = level_of(own_key, dims, split, -0.22, 0.18) if split else 1.0
    drawn = jax.random.normal(own_key, dims, jnp.float32) * deviation * factor_of
    return jnp.minimum(jnp.maximum(drawn, -reach), reach).astype(kind)


def setup_inputs(seed: int = 0) -> dict:
    splits = jax.random.split(jax.random.key(seed), 20)
    return {
        "hidden_in": gaussian(splits[0], (SEQS, LEN, D), 1.0, 6.0, ((0, 8), (1, 4))),
        "encoder_states": gaussian(splits[1], (SEQS, ENC, D), 1.0, 6.0, ((0, 8), (1, 4))),
        "out_grad": gaussian(splits[2], (SEQS, LEN, D), 1.0, 6.0, ((0, 8), (1, 4))),
        "bucket_index": draw_bucket_index(jax.random.fold_in(splits[19], 71), 0),
        "bias_table": gaussian(splits[4], (BUCKETS, HEADS), 1.0, 5.0, (), jnp.float32),
        "self_gain": jnp.clip(1.0 + 0.18 * jax.random.normal(splits[5], (D,), jnp.float32), 0.099609375, 1.8984375).astype(jnp.bfloat16),
        "self_query": gaussian(splits[6], (D, D), (D * HEAD) ** -0.5, 0.02734375, ((0, 8),)),
        "self_key": gaussian(splits[7], (D, D), D ** -0.5, 0.21875, ((0, 8),)),
        "self_value": gaussian(splits[8], (D, D), D ** -0.5, 0.21875, ((0, 8),)),
        "self_output": gaussian(splits[9], (D, D), 16 ** -0.5, 1.5, ((0, 8),)),
        "cross_gain": jnp.clip(1.0 + 0.18 * jax.random.normal(splits[10], (D,), jnp.float32), 0.099609375, 1.8984375).astype(jnp.bfloat16),
        "cross_query": gaussian(splits[11], (D, D), (D * HEAD) ** -0.5, 0.02734375, ((0, 8),)),
        "cross_key": gaussian(splits[12], (D, D), D ** -0.5, 0.21875, ((0, 8),)),
        "cross_value": gaussian(splits[13], (D, D), D ** -0.5, 0.21875, ((0, 8),)),
        "cross_output": gaussian(splits[14], (D, D), 16 ** -0.5, 1.5, ((0, 8),)),
        "feed_gain": jnp.clip(1.0 + 0.18 * jax.random.normal(splits[15], (D,), jnp.float32), 0.099609375, 1.8984375).astype(jnp.bfloat16),
        "gate_weight": gaussian(splits[16], (D, FF), D ** -0.5, 0.21875, ((0, 8),)),
        "linear_weight": gaussian(splits[17], (D, FF), D ** -0.5, 0.21875, ((0, 8),)),
        "down_weight": gaussian(splits[18], (FF, D), FF ** -0.5, 0.125, ((0, 8),)),
    }


EPSILON = 1e-06
NEGATIVE = -1e+30
HIGHEST = lax.Precision.HIGHEST

def to_bf16(values):
    return lax.optimization_barrier(values.astype(jnp.bfloat16))

def product(left, right):
    return jnp.dot(left, right, preferred_element_type=jnp.float32)

def row_contract(left, right):
    return jnp.dot(left.T, right, preferred_element_type=jnp.float32)

def col_contract(left, right):
    return jnp.dot(left, right.T, preferred_element_type=jnp.float32)

def norm_forward(values, gain):
    inverse = lax.rsqrt(lax.optimization_barrier(jnp.mean(values * values, axis=-1, keepdims=True)) + EPSILON)
    normed = values * inverse
    return (to_bf16(normed * gain.astype(jnp.float32)), normed, inverse)

def norm_backward(upstream, normed, inverse, gain):
    grad_gain = lax.optimization_barrier(jnp.sum(upstream * normed, axis=0))
    grad_normed = upstream * gain.astype(jnp.float32)
    grad_values = inverse * (grad_normed - normed * lax.optimization_barrier(jnp.mean(grad_normed * normed, axis=-1, keepdims=True)))
    return (grad_values, grad_gain)

def geglu(gate_pre, linear_pre):
    return jax.nn.gelu(gate_pre, approximate=True) * linear_pre

def split_heads(values):
    return values.astype(jnp.float32).reshape(values.shape[0], HEADS, HEAD)

def attend_forward(query, keys, values, extra, allowed):
    scores = jnp.einsum('qhe,khe->hqk', split_heads(query), split_heads(keys)) + extra
    scores = jnp.where(allowed, scores, NEGATIVE)
    top = lax.optimization_barrier(jnp.max(scores, axis=-1, keepdims=True))
    weights = jnp.where(allowed, jnp.exp(scores - top), 0.0)
    total = lax.optimization_barrier(jnp.sum(weights, axis=-1, keepdims=True))
    mixed = jnp.einsum('hqk,khe->qhe', to_bf16(weights).astype(jnp.float32), split_heads(values))
    result = to_bf16((mixed / jnp.transpose(total, (1, 0, 2))).reshape(query.shape[0], D))
    return (result, (top + jnp.log(total))[:, :, 0])

def attend_backward(query, keys, values, extra, allowed, lse, output, grad_output):
    split_grad = split_heads(grad_output)
    delta = lax.optimization_barrier(jnp.sum(split_grad * split_heads(output), axis=-1)).T
    scores = jnp.einsum('qhe,khe->hqk', split_heads(query), split_heads(keys)) + extra
    scores = jnp.where(allowed, scores, NEGATIVE)
    probs = jnp.where(allowed, jnp.exp(scores - lse[:, :, None]), 0.0)
    grad_probs = jnp.einsum('qhe,khe->hqk', split_grad, split_heads(values))
    grad_scores = probs * (grad_probs - delta[:, :, None])
    rounded = to_bf16(grad_scores).astype(jnp.float32)
    grad_query = jnp.einsum('hqk,khe->qhe', rounded, split_heads(keys)).reshape(query.shape[0], D)
    grad_keys = jnp.einsum('hqk,qhe->khe', rounded, split_heads(query)).reshape(keys.shape[0], D)
    grad_values = jnp.einsum('hqk,qhe->khe', to_bf16(probs).astype(jnp.float32), split_grad).reshape(keys.shape[0], D)
    return (grad_query, grad_keys, grad_values, grad_scores)

def sequence_pass(hidden_row, encoder_row, grad_row, params, bias_dist):
    self_gain, self_query, self_key, self_value, self_output, cross_gain, cross_query, cross_key, cross_value, cross_output, feed_gain, gate_weight, linear_weight, down_weight = params
    block_size = math.gcd(LEN, 512)
    block_count = LEN // block_size
    positions = jnp.arange(LEN, dtype=jnp.int32)
    numbers = jnp.arange(block_count, dtype=jnp.int32)

    def self_layout(number):
        offset = (number * block_size + jnp.arange(block_size, dtype=jnp.int32))[:, None] - positions[None, :]
        distance = jnp.clip(offset, 0, LEN - 1)
        return (jnp.take(bias_dist, distance, axis=1), (offset >= 0)[None], distance)

    def rows_of(values, number):
        return lax.dynamic_slice_in_dim(values, number * block_size, block_size, 0)
    start_x = hidden_row.astype(jnp.float32)
    norm_one, normed_one, inverse_one = norm_forward(start_x, self_gain)
    query = to_bf16(product(norm_one, self_query))
    keys = to_bf16(product(norm_one, self_key))
    values = to_bf16(product(norm_one, self_value))

    def self_forward(carried, number):
        extra, allowed, distance = self_layout(number)
        return (carried, attend_forward(rows_of(query, number), keys, values, extra, allowed))
    _, (attn, self_lse) = lax.scan(self_forward, None, numbers)
    attn = attn.reshape(LEN, D)
    after_self = start_x + product(attn, self_output)
    norm_two, normed_two, inverse_two = norm_forward(after_self, cross_gain)
    cross_q = to_bf16(product(norm_two, cross_query))
    cross_keys = to_bf16(product(encoder_row, cross_key))
    cross_values = to_bf16(product(encoder_row, cross_value))

    def cross_forward(carried, number):
        return (carried, attend_forward(rows_of(cross_q, number), cross_keys, cross_values, 0.0, True))
    _, (cattn, cross_lse) = lax.scan(cross_forward, None, numbers)
    cattn = cattn.reshape(LEN, D)
    after_cross = after_self + product(cattn, cross_output)
    norm_three, normed_three, inverse_three = norm_forward(after_cross, feed_gain)
    gate_pre = product(norm_three, gate_weight)
    linear_pre = product(norm_three, linear_weight)
    middle = to_bf16(geglu(gate_pre, linear_pre))
    layer_row = (after_cross + product(middle, down_weight)).astype(jnp.bfloat16)
    grad_down = row_contract(middle, grad_row)
    grad_middle = col_contract(grad_row, down_weight)
    _, pull_back = jax.vjp(geglu, gate_pre, linear_pre)
    grad_gate_pre, grad_linear_pre = pull_back(grad_middle)
    gate_round = to_bf16(grad_gate_pre)
    linear_round = to_bf16(grad_linear_pre)
    grad_gate = row_contract(norm_three, gate_round)
    grad_linear = row_contract(norm_three, linear_round)
    back_three, grad_feed_gain = norm_backward(col_contract(gate_round, gate_weight) + col_contract(linear_round, linear_weight), normed_three, inverse_three, feed_gain)
    grad_after_cross = grad_row.astype(jnp.float32) + back_three
    cross_round = to_bf16(grad_after_cross)
    grad_cross_output = row_contract(cattn, cross_round)
    grad_cattn = to_bf16(col_contract(cross_round, cross_output))

    def cross_backward(carried, number):
        grad_query, grad_keys, grad_values, _ = attend_backward(rows_of(cross_q, number), cross_keys, cross_values, 0.0, True, cross_lse[number], rows_of(cattn, number), rows_of(grad_cattn, number))
        return ((carried[0] + grad_keys, carried[1] + grad_values), grad_query)
    empty_enc = jnp.zeros((ENC, D), jnp.float32)
    (cross_key_sum, cross_value_sum), grad_cq = lax.scan(cross_backward, (empty_enc, empty_enc), numbers)
    grad_cq = to_bf16(grad_cq.reshape(LEN, D))
    cross_key_round = to_bf16(cross_key_sum)
    cross_value_round = to_bf16(cross_value_sum)
    grad_cross_query = row_contract(norm_two, grad_cq)
    grad_cross_key = row_contract(encoder_row, cross_key_round)
    grad_cross_value = row_contract(encoder_row, cross_value_round)
    encoder_grad_row = col_contract(cross_key_round, cross_key) + col_contract(cross_value_round, cross_value)
    back_two, grad_cross_gain = norm_backward(col_contract(grad_cq, cross_query), normed_two, inverse_two, cross_gain)
    grad_after_self = grad_after_cross + back_two
    self_round = to_bf16(grad_after_self)
    grad_self_output = row_contract(attn, self_round)
    grad_attn = to_bf16(col_contract(self_round, self_output))

    def self_backward(carried, number):
        extra, allowed, distance = self_layout(number)
        grad_query, grad_keys, grad_values, grad_scores = attend_backward(rows_of(query, number), keys, values, extra, allowed, self_lse[number], rows_of(attn, number), rows_of(grad_attn, number))
        grad_dist = jax.ops.segment_sum(grad_scores.reshape(HEADS, -1).T, distance.reshape(-1), num_segments=LEN)
        return ((carried[0] + grad_keys, carried[1] + grad_values, carried[2] + grad_dist), grad_query)
    empty_seq = jnp.zeros((LEN, D), jnp.float32)
    (key_sum, value_sum, dist_sum), grad_q = lax.scan(self_backward, (empty_seq, empty_seq, jnp.zeros((LEN, HEADS), jnp.float32)), numbers)
    grad_q = to_bf16(grad_q.reshape(LEN, D))
    grad_k = to_bf16(key_sum)
    grad_v = to_bf16(value_sum)
    grad_self_query = row_contract(norm_one, grad_q)
    grad_self_key = row_contract(norm_one, grad_k)
    grad_self_value = row_contract(norm_one, grad_v)
    upstream_one = col_contract(grad_q, self_query) + col_contract(grad_k, self_key) + col_contract(grad_v, self_value)
    back_one, grad_self_gain = norm_backward(upstream_one, normed_one, inverse_one, self_gain)
    input_row = grad_after_self + back_one
    grads = (grad_self_gain, grad_self_query, grad_self_key, grad_self_value, grad_self_output, grad_cross_gain, grad_cross_query, grad_cross_key, grad_cross_value, grad_cross_output, grad_feed_gain, grad_gate, grad_linear, grad_down)
    return (layer_row, input_row, encoder_grad_row, grads, dist_sum)

def reference(hidden_in, encoder_states, out_grad, bucket_index, bias_table, self_gain, self_query, self_key, self_value, self_output, cross_gain, cross_query, cross_key, cross_value, cross_output, feed_gain, gate_weight, linear_weight, down_weight):
    params = (self_gain, self_query, self_key, self_value, self_output, cross_gain, cross_query, cross_key, cross_value, cross_output, feed_gain, gate_weight, linear_weight, down_weight)
    onehot = (bucket_index[:, None] == jnp.arange(BUCKETS, dtype=jnp.int32)[None, :]).astype(jnp.float32)
    bias_dist = jnp.dot(onehot, bias_table, precision=HIGHEST).T
    empty_grads = tuple((jnp.zeros(member.shape, jnp.float32) for member in params))

    def per_sequence(totals, inputs):
        hidden_row, encoder_row, grad_row = inputs
        layer_row, input_row, encoder_grad_row, grads, dist_sum = sequence_pass(hidden_row, encoder_row, grad_row, params, bias_dist)
        sums = tuple((running_sum + new_grad for running_sum, new_grad in zip(totals[0], grads)))
        return ((sums, totals[1] + dist_sum), (layer_row, input_row, encoder_grad_row))
    (grads, grad_dist), (layer_out, input_grad, encoder_grad) = lax.scan(per_sequence, (empty_grads, jnp.zeros((LEN, HEADS), jnp.float32)), (hidden_in, encoder_states, out_grad))
    grad_table = jnp.dot(onehot.T, grad_dist, precision=HIGHEST)
    return (layer_out, input_grad, encoder_grad, grad_table, grads[0], grads[1], grads[2], grads[3], grads[4], grads[5], grads[6], grads[7], grads[8], grads[9], grads[10], grads[11], grads[12], grads[13])
```

```python
from functools import partial
import math

import jax
import jax.numpy as jnp
from jax import lax
from jax.experimental import pallas as pl
from jax.experimental.pallas import tpu as pltpu
from jax.sharding import PartitionSpec as P

EPSILON = 1e-06
NEGATIVE = -1e30
HIGHEST = lax.Precision.HIGHEST


LANES = 128
MESH = pl.DeviceIdType.MESH


def place():
    seq = lax.axis_index("seq")
    return seq // 2, seq % 2, lax.axis_index("ctx"), lax.axis_index("fsdp")


def device_at(side, core, depth, row):
    return (side * 2 + core, depth, row)


def greet(partners):
    barrier = pltpu.get_barrier_semaphore()
    for partner in partners:
        pl.semaphore_signal(barrier, inc=1, device_id=partner, device_id_type=MESH)
    pl.semaphore_wait(barrier, len(partners))


def remote(source, target, send_sem, recv_sem, device):
    return pltpu.make_async_remote_copy(
        src_ref=source,
        dst_ref=target,
        send_sem=send_sem,
        recv_sem=recv_sem,
        device_id=device,
        device_id_type=MESH,
    )


class Gather:
    def __init__(self, depth_count, piece, chunk_count, sems):
        self.count = depth_count
        self.piece = piece
        self.chunks = chunk_count
        (self.z_send, self.z_recv, self.y_send, self.y_recv, self.x_send, self.x_recv,
         self.c_send, self.c_recv, self.d_send, self.d_recv) = sems
        side, core, depth, row = place()
        self.side, self.core, self.depth, self.row = side, core, depth, row
        self.to_y = device_at(side, core, depth, 1 - row)
        self.to_x = device_at(1 - side, core, depth, row)
        self.to_core = device_at(side, 1 - core, depth, row)
        self.first = 2 * core
        self.other_first = 2 * (1 - core)

    @staticmethod
    def semaphores(chunks, count):
        slots = 2 * count - 1
        shapes = [(chunks, 2 * (count - 1))] * 2 + [(chunks, slots)] * 4
        shapes += [(chunks, 2 * (count - 1))] * 2 + [(chunks, slots)] * 2
        return [pltpu.SemaphoreType.DMA(shape) for shape in shapes]

    def slot_of(self, way, far):
        return 0 if far == 0 else 1 + way * (self.count - 1) + far - 1

    def at_depth(self, way, far):
        return self.depth + far if way == 0 else self.depth - far

    def valid(self, way, far):
        return self.depth + far <= self.count - 1 if way == 0 else self.depth - far >= 0

    def steps(self):
        return [(way, far) for far in range(1, self.count) for way in (0, 1)]

    def z_copy(self, chunk, way, far):
        index = way * (self.count - 1) + far
        held = self.piece(chunk, self.at_depth(way, far), self.row, self.first, 2)
        target = device_at(self.side, self.core, self.depth - 1 if way == 0 else self.depth + 1, self.row)
        return remote(held, held, self.z_send.at[chunk, index], self.z_recv.at[chunk, index], target)

    def z_arrival(self, chunk, way, far):
        index = way * (self.count - 1) + far - 1
        held = self.piece(chunk, self.at_depth(way, far), self.row, self.first, 2)
        return remote(held, held, self.z_send.at[chunk, index], self.z_recv.at[chunk, index], self.to_y)

    def can_send(self, way):
        return self.depth > 0 if way == 0 else self.depth < self.count - 1

    def y_copy(self, chunk, way, far):
        slot = self.slot_of(way, far)
        held = self.piece(chunk, self.at_depth(way, far), self.row, self.first + self.side, 1)
        return remote(held, held, self.y_send.at[chunk, slot], self.y_recv.at[chunk, slot], self.to_y)

    def y_arrival(self, chunk, way, far):
        slot = self.slot_of(way, far)
        held = self.piece(chunk, self.at_depth(way, far), 1 - self.row, self.first + self.side, 1)
        return remote(held, held, self.y_send.at[chunk, slot], self.y_recv.at[chunk, slot], self.to_y)

    def x_copy(self, chunk, way, far):
        slot = self.slot_of(way, far)
        held = self.piece(chunk, self.at_depth(way, far), 1 - self.row, self.first + self.side, 1)
        return remote(held, held, self.x_send.at[chunk, slot], self.x_recv.at[chunk, slot], self.to_x)

    def x_arrival(self, chunk, way, far):
        slot = self.slot_of(way, far)
        held = self.piece(chunk, self.at_depth(way, far), 1 - self.row, self.first + 1 - self.side, 1)
        return remote(held, held, self.x_send.at[chunk, slot], self.x_recv.at[chunk, slot], self.to_x)

    def c_copy(self, chunk, way, far):
        index = way * (self.count - 1) + far - 1
        held = self.piece(chunk, self.at_depth(way, far), self.row, self.first, 2)
        return remote(held, held, self.c_send.at[chunk, index], self.c_recv.at[chunk, index], self.to_core)

    def c_arrival(self, chunk, way, far):
        index = way * (self.count - 1) + far - 1
        held = self.piece(chunk, self.at_depth(way, far), self.row, self.other_first, 2)
        return remote(held, held, self.c_send.at[chunk, index], self.c_recv.at[chunk, index], self.to_core)

    def d_copy(self, chunk, way, far):
        slot = self.slot_of(way, far)
        held = self.piece(chunk, self.at_depth(way, far), 1 - self.row, self.first, 2)
        return remote(held, held, self.d_send.at[chunk, slot], self.d_recv.at[chunk, slot], self.to_core)

    def d_arrival(self, chunk, way, far):
        slot = self.slot_of(way, far)
        held = self.piece(chunk, self.at_depth(way, far), 1 - self.row, self.other_first, 2)
        return remote(held, held, self.d_send.at[chunk, slot], self.d_recv.at[chunk, slot], self.to_core)

    def begin(self, chunk):
        for way in (0, 1):
            @pl.when(self.can_send(way))
            def _():
                self.z_copy(chunk, way, 0).start()
        self.y_copy(chunk, 0, 0).start()

    def z_phase(self, chunk):
        for way, far in self.steps():
            @pl.when(self.valid(way, far))
            def _():
                self.z_arrival(chunk, way, far).wait_recv()
                if far < self.count - 1:
                    @pl.when(self.can_send(way))
                    def _():
                        self.z_copy(chunk, way, far).start()
                self.y_copy(chunk, way, far).start()
                self.c_copy(chunk, way, far).start()

    def y_phase(self, chunk):
        for way, far in [(0, 0)] + self.steps():
            @pl.when(self.valid(way, far))
            def _():
                self.y_arrival(chunk, way, far).wait_recv()
                self.x_copy(chunk, way, far).start()

    def x_phase(self, chunk):
        for way, far in [(0, 0)] + self.steps():
            @pl.when(self.valid(way, far))
            def _():
                self.x_arrival(chunk, way, far).wait_recv()
                self.d_copy(chunk, way, far).start()

    def finish(self, chunk):
        for way, far in [(0, 0)] + self.steps():
            @pl.when(self.valid(way, far))
            def _():
                if far:
                    self.c_arrival(chunk, way, far).wait_recv()
                self.d_arrival(chunk, way, far).wait_recv()

    def drain(self, chunk):
        for way in (0, 1):
            @pl.when(self.can_send(way))
            def _():
                self.z_copy(chunk, way, 0).wait_send()
        for way, far in [(0, 0)] + self.steps():
            @pl.when(self.valid(way, far))
            def _():
                if 0 < far < self.count - 1:
                    @pl.when(self.can_send(way))
                    def _():
                        self.z_copy(chunk, way, far).wait_send()
                self.y_copy(chunk, way, far).wait_send()
                self.x_copy(chunk, way, far).wait_send()
                self.d_copy(chunk, way, far).wait_send()
                if far:
                    self.c_copy(chunk, way, far).wait_send()


def gather_kernel(count, *refs):
    squares = refs[:8]
    gate, linear, down, gains = refs[8:12]
    packed, gates, linears, downs, all_gains = refs[12:17]
    own_sem, gain_send, gain_recv = refs[17:20]
    wide = gates.shape[-1]
    side, core, depth, row = place()

    def piece(chunk, at_depth, at_row, first, number):
        parts = pl.ds(first, number)
        if chunk < 2:
            return packed.at[chunk, parts, at_depth, at_row]
        if chunk < 4:
            return (gates, linears)[chunk - 2].at[parts, at_depth, at_row]
        return downs.at[at_depth, at_row, parts]

    local = [[], [], [], [], []]
    for number, member in enumerate(squares):
        local[number // 4].append((member, packed.at[number // 4, number % 4, depth, row]))
    for at, member, whole in ((2, gate, gates), (3, linear, linears)):
        for number in range(4):
            local[at].append((member.at[:, pl.ds(number * wide, wide)], whole.at[number, depth, row]))
    local[4].append((down, downs.at[depth, row]))
    local[0].append((gains, all_gains.at[depth, row]))
    copies = [
        [pltpu.make_async_copy(source, target, own_sem.at[at, number])
         for number, (source, target) in enumerate(group)]
        for at, group in enumerate(local)
    ]
    for group in copies:
        for copy in group:
            copy.start()
    work = Gather(count, piece, 5, refs[20:])
    mates = []
    for far in range(count):
        for flip in (0, 1):
            if far or flip:
                mates.append((lax.rem(depth + far, count), row if flip == 0 else 1 - row))
    greet([device_at(side, core, *mate) for mate in mates] + [work.to_x, work.to_core])
    for chunk in range(5):
        for copy in copies[chunk]:
            copy.wait()
        work.begin(chunk)
    sends = [
        remote(all_gains.at[depth, row], all_gains.at[depth, row], gain_send.at[number],
               gain_recv.at[number], device_at(side, core, *mate))
        for number, mate in enumerate(mates)
    ]
    for copy in sends:
        copy.start()
    for chunk in range(7):
        if chunk < 5:
            work.z_phase(chunk)
        if 1 <= chunk < 6:
            work.y_phase(chunk - 1)
        if 2 <= chunk:
            work.x_phase(chunk - 2)
    for copy in sends:
        copy.wait_send()
    for far in range(count):
        for flip in (0, 1):
            if far or flip:
                number = far * 2 + flip - 1
                source = (lax.rem(depth + count - far, count), row if flip == 0 else 1 - row)
                held = all_gains.at[source[0], source[1]]
                remote(held, held, gain_send.at[number], gain_recv.at[number], work.to_core).wait_recv()
    for chunk in range(5):
        work.finish(chunk)
        work.drain(chunk)


def gather_weights(squares, gate, linear, down, gains):
    count = lax.axis_size("ctx")
    rows, features = squares[0].shape
    wide = gate.shape[1] // 4
    tall = down.shape[0] // 4
    kind = squares[0].dtype
    chunks = 5
    return pl.pallas_call(
        partial(gather_kernel, count),
        out_shape=(
            jax.ShapeDtypeStruct((2, 4, count, 2, rows, features), kind),
            jax.ShapeDtypeStruct((4, count, 2, rows, wide), kind),
            jax.ShapeDtypeStruct((4, count, 2, rows, wide), kind),
            jax.ShapeDtypeStruct((count, 2, 4, tall, features), kind),
            jax.ShapeDtypeStruct((count, 2) + gains.shape, kind),
        ),
        in_specs=[pl.BlockSpec(memory_space=pl.ANY)] * 12,
        out_specs=[pl.BlockSpec(memory_space=pl.ANY)] * 5,
        scratch_shapes=[
            pltpu.SemaphoreType.DMA((chunks, 5)),
            pltpu.SemaphoreType.DMA((2 * count - 1,)),
            pltpu.SemaphoreType.DMA((2 * count - 1,)),
            *Gather.semaphores(chunks, count),
        ],
        compiler_params=pltpu.CompilerParams(collective_id=0, has_side_effects=True),
        name="gather_weights",
    )(*squares, gate, linear, down.reshape(4, tall, features), gains)


def add_into(target, source, index_of, steps):
    def body(number, carry):
        at, other = index_of(number)
        target[at] = target[at] + source[other]
        return carry

    lax.fori_loop(0, steps, body, 0)


class Scatter:
    def __init__(self, count, source, buffers, out, sems, chunk):
        self.count, self.source, self.out = count, source, out
        self.total, self.from_core, self.from_x, self.from_y, self.from_z, self.last = buffers
        self.own_sem, self.sends, self.recvs = sems
        self.chunk = chunk
        side, core, depth, row = place()
        self.side, self.core, self.depth, self.row = side, core, depth, row
        self.to_y = device_at(side, core, depth, 1 - row)
        self.to_x = device_at(1 - side, core, depth, row)
        self.to_core = device_at(side, 1 - core, depth, row)

    @staticmethod
    def buffers(count, rows, columns):
        kind = jnp.bfloat16
        return [
            pltpu.VMEM((2, count, 2, rows, columns), kind),
            pltpu.VMEM((2, count, 2, rows, columns), kind),
            pltpu.VMEM((count, rows, columns), kind),
            pltpu.VMEM((count, rows, columns), kind),
            pltpu.VMEM((2, count - 1, 2, rows, columns), kind),
            pltpu.VMEM((2, rows, columns), kind),
        ]

    @staticmethod
    def semaphores(chunks, count):
        slots = 6 + 2 * (count - 1)
        return [
            pltpu.SemaphoreType.DMA((chunks, 2)),
            pltpu.SemaphoreType.DMA((chunks, slots)),
            pltpu.SemaphoreType.DMA((chunks, slots)),
        ]

    def link(self, source, target, slot, device):
        return remote(source, target, self.sends.at[self.chunk, slot], self.recvs.at[self.chunk, slot], device)

    def own_copy(self, part):
        return pltpu.make_async_copy(
            self.source(2 * self.core + part), self.total.at[part], self.own_sem.at[self.chunk, part]
        )

    def core_copy(self, part):
        return self.link(self.source(2 * (1 - self.core) + part), self.from_core.at[part], part, self.to_core)

    def x_copy(self):
        return self.link(self.total.at[1 - self.side, :, 1 - self.row], self.from_x, 2, self.to_x)

    def y_copy(self):
        return self.link(self.total.at[self.side, :, 1 - self.row], self.from_y, 3, self.to_y)

    def last_copy(self):
        return self.link(self.total.at[:, self.depth, self.row], self.last, 4, self.to_x)

    def out_copy(self):
        half = self.out.at[pl.ds(2 * self.core, 2)]
        return self.link(half, half, 5, self.to_core)

    def out_arrival(self):
        half = self.out.at[pl.ds(2 * (1 - self.core), 2)]
        return self.link(half, half, 5, self.to_core)

    def z_copy(self, way, far):
        at = self.depth - far if way == 0 else self.depth + far
        target = device_at(self.side, self.core, self.depth - 1 if way == 0 else self.depth + 1, self.row)
        return self.link(
            self.total.at[:, at, self.row], self.from_z.at[way, far - 1], 6 + way * (self.count - 1) + far - 1, target
        )

    def z_arrival(self, way, far):
        held = self.from_z.at[way, far]
        return self.link(held, held, 6 + way * (self.count - 1) + far, self.to_y)

    def begin(self):
        for part in (0, 1):
            self.core_copy(part).start()
            self.own_copy(part).start()

    def core_phase(self):
        for part in (0, 1):
            self.own_copy(part).wait()
            self.core_copy(part).wait_recv()
        side, row = self.side, self.row
        for step, (part, at_row) in enumerate(
            ((1 - side, 1 - row), (side, 1 - row), (side, row), (1 - side, row))
        ):
            add_into(
                self.total, self.from_core,
                lambda number: ((part, number, at_row), (part, number, at_row)),
                self.count,
            )
            if step == 0:
                self.x_copy().start()

    def x_phase(self):
        self.x_copy().wait_recv()
        side, row = self.side, self.row
        add_into(self.total, self.from_x, lambda number: ((side, number, 1 - row), number), self.count)
        self.y_copy().start()

    def y_phase(self):
        self.y_copy().wait_recv()
        side, row = self.side, self.row
        add_into(self.total, self.from_y, lambda number: ((side, number, row), number), self.count)

    def z_phase(self):
        row = self.row
        for far in range(self.count - 1, 0, -1):
            for way in (0, 1):
                at = self.depth - far if way == 0 else self.depth + far
                valid = at >= 0 if way == 0 else at <= self.count - 1
                inner = self.depth < self.count - 1 if way == 0 else self.depth > 0

                @pl.when(valid)
                def _():
                    if far < self.count - 1:
                        @pl.when(inner)
                        def _():
                            self.z_arrival(way, far).wait_recv()
                            add_into(
                                self.total, self.from_z,
                                lambda part: ((part, at, row), (way, far, part)), 2,
                            )
                    self.z_copy(way, far).start()
        for way in (0, 1):
            inner = self.depth < self.count - 1 if way == 0 else self.depth > 0

            @pl.when(inner)
            def _():
                self.z_arrival(way, 0).wait_recv()
                add_into(
                    self.total, self.from_z, lambda part: ((part, self.depth, row), (way, 0, part)), 2
                )
        self.last_copy().start()

    def last_phase(self):
        self.last_copy().wait_recv()
        core, depth, row = self.core, self.depth, self.row

        def body(part, carry):
            self.out[2 * core + part] = self.total[part, depth, row] + self.last[part]
            return carry

        lax.fori_loop(0, 2, body, 0)
        self.out_copy().start()

    def finish(self):
        self.out_arrival().wait_recv()
        for part in (0, 1):
            self.core_copy(part).wait_send()
        self.x_copy().wait_send()
        self.y_copy().wait_send()
        self.last_copy().wait_send()
        self.out_copy().wait_send()
        for far in range(1, self.count):
            for way in (0, 1):
                at = self.depth - far if way == 0 else self.depth + far

                @pl.when(at >= 0 if way == 0 else at <= self.count - 1)
                def _():
                    self.z_copy(way, far).wait_send()


class SmallSum:
    def __init__(self, count, held, landing, depth_held, out, sends, recvs):
        self.count, self.held, self.landing, self.depth_held, self.out = count, held, landing, depth_held, out
        self.sends, self.recvs = sends, recvs
        side, core, depth, row = place()
        self.side, self.core, self.depth, self.row = side, core, depth, row
        self.partners = [
            device_at(side, 1 - core, depth, row),
            device_at(1 - side, core, depth, row),
            device_at(side, core, depth, 1 - row),
        ]

    @staticmethod
    def scratch(count, shape):
        return [
            pltpu.VMEM((3,) + shape, jnp.float32),
            pltpu.VMEM((3,) + shape, jnp.float32),
            pltpu.VMEM((count,) + shape, jnp.float32),
            pltpu.SemaphoreType.DMA((3 + count,)),
            pltpu.SemaphoreType.DMA((3 + count,)),
        ]

    def copy(self, level):
        return remote(
            self.held.at[level], self.landing.at[level], self.sends.at[level], self.recvs.at[level], self.partners[level]
        )

    def z_copy(self, at):
        return remote(
            self.depth_held.at[self.depth], self.depth_held.at[self.depth], self.sends.at[3 + at],
            self.recvs.at[3 + self.depth], device_at(self.side, self.core, at, self.row),
        )

    def begin(self, value):
        self.held[0] = value
        self.copy(0).start()

    def level(self, level):
        self.copy(level).wait_recv()
        summed = self.held[level] + self.landing[level]
        if level < 2:
            self.held[level + 1] = summed
            self.copy(level + 1).start()
        else:
            self.depth_held[self.depth] = summed
            for at in range(self.count):
                @pl.when(self.depth != at)
                def _():
                    self.z_copy(at).start()

    def finish(self):
        for at in range(self.count):
            @pl.when(self.depth != at)
            def _():
                held = self.depth_held.at[at]
                remote(held, held, self.sends.at[3 + at], self.recvs.at[3 + at], self.partners[0]).wait_recv()
        summed = self.depth_held[0]
        for at in range(1, self.count):
            summed = summed + self.depth_held[at]
        self.out[...] = summed
        for level in range(3):
            self.copy(level).wait_send()
        for at in range(self.count):
            @pl.when(self.depth != at)
            def _():
                self.z_copy(at).wait_send()


def scatter_kernel(count, *refs):
    packed, gates, linears, downs, small = refs[:5]
    outs, small_out = refs[5:10], refs[10]
    refs = refs[11:]
    buffers = [refs[6 * chunk : 6 * chunk + 6] for chunk in range(5)]
    refs = refs[30:]
    sems, refs = refs[:3], refs[3:]
    sources = [
        lambda part: packed.at[0, part],
        lambda part: packed.at[1, part],
        lambda part: gates.at[part],
        lambda part: linears.at[part],
        lambda part: downs.at[:, :, part],
    ]
    work = [
        Scatter(count, sources[chunk], buffers[chunk], outs[chunk], sems, chunk) for chunk in range(5)
    ]
    summing = SmallSum(count, refs[0], refs[1], refs[2], small_out, refs[3], refs[4])
    side, core, depth, row = place()
    mates = [device_at(side, core, lax.rem(depth + far, count), row) for far in range(1, count)]
    greet(mates + summing.partners)
    summing.begin(small[...])
    order = (4, 2, 3, 1, 0)
    for chunk in order:
        work[chunk].begin()
    phases = ["core_phase", "x_phase", "y_phase", "z_phase", "last_phase"]
    for step in range(len(order) + len(phases) - 1):
        for number, name in reversed(list(enumerate(phases))):
            if 0 <= step - number < len(order):
                getattr(work[order[step - number]], name)()
        if step < 3:
            summing.level(step)
    summing.finish()
    for chunk in order:
        work[chunk].finish()


def scatter_gradients(packed, gates, linears, downs, small):
    count = lax.axis_size("ctx")
    rows, features = packed.shape[-2:]
    wide = gates.shape[-1]
    tall = downs.shape[-2]
    kind = packed.dtype
    vmem = pl.BlockSpec(memory_space=pltpu.VMEM)
    sizes = [(rows, features), (rows, features), (rows, wide), (rows, wide), (tall, features)]
    return pl.pallas_call(
        partial(scatter_kernel, count),
        out_shape=tuple(jax.ShapeDtypeStruct((4,) + size, kind) for size in sizes)
        + (jax.ShapeDtypeStruct(small.shape, small.dtype),),
        in_specs=[pl.BlockSpec(memory_space=pl.ANY)] * 4 + [vmem],
        out_specs=[vmem] * 6,
        scratch_shapes=[
            *(buffer for size in sizes for buffer in Scatter.buffers(count, *size)),
            *Scatter.semaphores(5, count),
            *SmallSum.scratch(count, small.shape),
        ],
        compiler_params=pltpu.CompilerParams(
            collective_id=1, has_side_effects=True, vmem_limit_bytes=48 << 20
        ),
        name="scatter_gradients",
    )(packed, gates, linears, downs, small)


def fold_rows(rows, height):
    count = -(-rows.shape[-2] // height)
    short = count * height - rows.shape[-2]
    padding = [(0, 0)] * (rows.ndim - 2) + [(0, short), (0, 0)]
    padded = jnp.pad(rows, padding)
    return jnp.concatenate(
        [padded[..., number * height : (number + 1) * height, :] for number in range(count)],
        axis=-1,
    )


def unfold_rows(columns, row_count, features):
    count = columns.shape[-1] // features
    stacked = jnp.concatenate(
        [columns[..., number * features : (number + 1) * features] for number in range(count)],
        axis=-2,
    )
    return stacked[..., :row_count, :]


def gain_columns(gains, dtype):
    columns = jnp.stack([member.astype(dtype) for member in gains], axis=1)
    return jnp.pad(columns, ((0, 0), (0, LANES - columns.shape[1])))


def product(left, right):
    return jnp.dot(left, right, preferred_element_type=jnp.float32)


def row_contract(left, right):
    return lax.dot_general(
        left, right, (((0,), (0,)), ((), ())), preferred_element_type=jnp.float32
    )


def col_contract(left, right):
    return lax.dot_general(
        left, right, (((1,), (1,)), ((), ())), preferred_element_type=jnp.float32
    )


def norm_forward(values, gain):
    inverse = lax.rsqrt(jnp.mean(values * values, axis=-1, keepdims=True) + EPSILON)
    normed = values * inverse
    return ((normed * gain.astype(jnp.float32)).astype(jnp.bfloat16), normed, inverse)


def norm_backward(upstream, normed, inverse, gain):
    grad_gain = jnp.sum(upstream * normed, axis=0)
    grad_normed = upstream * gain.astype(jnp.float32)
    grad_values = inverse * (
        grad_normed - normed * jnp.mean(grad_normed * normed, axis=-1, keepdims=True)
    )
    return (grad_values, grad_gain)


def geglu(gate_pre, linear_pre):
    return jax.nn.gelu(gate_pre, approximate=True) * linear_pre


def by_heads(values, head_count):
    return values.reshape(values.shape[0], head_count, values.shape[1] // head_count)


def band_onehot(bucket_rev, buckets, query_rows, key_rows, query_first, key_first):
    length = bucket_rev.shape[0] // 2
    offset_first = query_first - key_first
    upper_band = lax.dynamic_slice_in_dim(bucket_rev, length - 1 - offset_first, key_rows, 0)
    lower_band = lax.dynamic_slice_in_dim(
        bucket_rev, length - offset_first - query_rows, query_rows - 1, 0
    )
    slots = jnp.concatenate([upper_band, jnp.full((1,), -1, jnp.int32), lower_band])
    return (slots[:, None] == jnp.arange(buckets, dtype=jnp.int32)[None, :]).astype(jnp.float32)


def spread_band(band, query_rows, key_rows):
    head_count, width = band.shape
    tiled = jnp.broadcast_to(band[:, None, :], (head_count, query_rows, width)).reshape(
        head_count, query_rows * width
    )
    return tiled[:, : query_rows * (width - 1)].reshape(head_count, query_rows, width - 1)[
        :, :, :key_rows
    ]


def fold_band(grad_scores, width):
    head_count, query_rows, key_rows = grad_scores.shape
    padded = jnp.pad(grad_scores, ((0, 0), (0, 0), (0, width - 1 - key_rows))).reshape(
        head_count, query_rows * (width - 1)
    )
    padded = jnp.pad(padded, ((0, 0), (0, query_rows)))
    return jnp.sum(padded.reshape(head_count, query_rows, width), axis=1)


def self_scores(query, key_block, query_first, key_first, bucket_rev, bias_table):
    head_count = bias_table.shape[1]
    query_rows = query.shape[0]
    key_rows = key_block.shape[0]
    scores = jnp.einsum(
        "qhe,khe->hqk",
        by_heads(query, head_count),
        by_heads(key_block, head_count),
        preferred_element_type=jnp.float32,
    )
    offset = (query_first + jnp.arange(query_rows, dtype=jnp.int32))[:, None] - (
        key_first + jnp.arange(key_rows, dtype=jnp.int32)
    )[None, :]
    allowed = offset >= 0
    onehot = band_onehot(
        bucket_rev, bias_table.shape[0], query_rows, key_rows, query_first, key_first
    )
    band = jnp.dot(onehot, bias_table, precision=HIGHEST).T
    scores = jnp.where(allowed[None], scores + spread_band(band, query_rows, key_rows), NEGATIVE)
    return (scores, allowed, onehot)


def table_terms(grad_scores, onehot):
    band_grad = fold_band(grad_scores, onehot.shape[0])
    return jnp.dot(onehot.T, band_grad.T, precision=HIGHEST)


def fold_blocks(block_step, running, arrays, first_row):
    piece_rows = arrays[0].shape[0]
    block_size = math.gcd(piece_rows, 512) if piece_rows > 512 else piece_rows
    if block_size == piece_rows:
        return block_step(running, arrays, first_row)
    block_count = piece_rows // block_size
    stacked = tuple(
        (member.reshape((block_count, block_size) + member.shape[1:]) for member in arrays)
    )

    def scan_block(state_now, scanned):
        number, blocks = scanned
        return (block_step(state_now, blocks, first_row + number * block_size), None)

    result, _ = lax.scan(scan_block, running, (jnp.arange(block_count, dtype=jnp.int32), stacked))
    return result


def forward_step(running, blocks, key_first, query, query_first, bucket_rev, bias_table):
    top, total, mixed = running
    key_block, value_block = blocks
    head_count = bias_table.shape[1]
    scores, allowed, _ = self_scores(
        query, key_block, query_first, key_first, bucket_rev, bias_table
    )
    new_top = jnp.maximum(top, jnp.max(scores, axis=-1))
    weights = jnp.where(allowed[None], jnp.exp(scores - new_top[:, :, None]), 0.0)
    rescale = jnp.exp(top - new_top)
    total = total * rescale + jnp.sum(weights, axis=-1)
    update = jnp.einsum(
        "hqk,khe->qhe",
        weights.astype(jnp.bfloat16),
        by_heads(value_block, head_count),
        preferred_element_type=jnp.float32,
    )
    mixed = mixed * rescale.T[:, :, None] + update
    return (new_top, total, mixed)


def backward_core(
    query,
    grad_attn,
    lse_rows,
    delta_rows,
    key_block,
    value_block,
    query_first,
    key_first,
    bucket_rev,
    bias_table,
):
    head_count = bias_table.shape[1]
    scores, allowed, onehot = self_scores(
        query, key_block, query_first, key_first, bucket_rev, bias_table
    )
    probs = jnp.where(allowed[None], jnp.exp(scores - lse_rows.T[:, :, None]), 0.0)
    grad_probs = jnp.einsum(
        "qhe,khe->hqk",
        by_heads(grad_attn, head_count),
        by_heads(value_block, head_count),
        preferred_element_type=jnp.float32,
    )
    grad_scores = probs * (grad_probs - delta_rows.T[:, :, None])
    return (probs, grad_scores, onehot)


def partial_step(
    running,
    blocks,
    key_first,
    query,
    grad_attn,
    lse_rows,
    delta_rows,
    query_first,
    bucket_rev,
    bias_table,
):
    grad_query, grad_keys, grad_values, table_part = running
    key_block, value_block = blocks
    head_count = bias_table.shape[1]
    probs, grad_scores, onehot = backward_core(
        query,
        grad_attn,
        lse_rows,
        delta_rows,
        key_block,
        value_block,
        query_first,
        key_first,
        bucket_rev,
        bias_table,
    )
    rounded = grad_scores.astype(jnp.bfloat16)
    grad_query = grad_query + jnp.einsum(
        "hqk,khe->qhe", rounded, by_heads(key_block, head_count), preferred_element_type=jnp.float32
    )
    key_part = jnp.einsum(
        "hqk,qhe->khe", rounded, by_heads(query, head_count), preferred_element_type=jnp.float32
    ).reshape(key_block.shape[0], -1)
    value_part = jnp.einsum(
        "hqk,qhe->khe",
        probs.astype(jnp.bfloat16),
        by_heads(grad_attn, head_count),
        preferred_element_type=jnp.float32,
    ).reshape(key_block.shape[0], -1)
    grad_keys = lax.dynamic_update_slice_in_dim(grad_keys, key_part, key_first, 0)
    grad_values = lax.dynamic_update_slice_in_dim(grad_values, value_part, key_first, 0)
    table_part = table_part + table_terms(grad_scores, onehot)
    return (grad_query, grad_keys, grad_values, table_part)


def plain_forward(query, keys, values, head_count):
    scores = jnp.einsum(
        "qhe,khe->hqk",
        by_heads(query, head_count),
        by_heads(keys, head_count),
        preferred_element_type=jnp.float32,
    )
    top = jnp.max(scores, axis=-1, keepdims=True)
    weights = jnp.exp(scores - top)
    total = jnp.sum(weights, axis=-1, keepdims=True)
    mixed = jnp.einsum(
        "hqk,khe->qhe",
        weights.astype(jnp.bfloat16),
        by_heads(values, head_count),
        preferred_element_type=jnp.float32,
    )
    result = (
        (mixed / jnp.transpose(total, (1, 0, 2))).reshape(query.shape[0], -1).astype(jnp.bfloat16)
    )
    return (result, (top + jnp.log(total))[:, :, 0])


def plain_backward(query, keys, values, lse, output, grad_output, head_count):
    split_grad = by_heads(grad_output, head_count)
    delta = jnp.sum(
        split_grad.astype(jnp.float32) * by_heads(output, head_count).astype(jnp.float32), axis=-1
    ).T
    scores = jnp.einsum(
        "qhe,khe->hqk",
        by_heads(query, head_count),
        by_heads(keys, head_count),
        preferred_element_type=jnp.float32,
    )
    probs = jnp.exp(scores - lse[:, :, None])
    grad_probs = jnp.einsum(
        "qhe,khe->hqk", split_grad, by_heads(values, head_count), preferred_element_type=jnp.float32
    )
    rounded = (probs * (grad_probs - delta[:, :, None])).astype(jnp.bfloat16)
    grad_query = jnp.einsum(
        "hqk,khe->qhe", rounded, by_heads(keys, head_count), preferred_element_type=jnp.float32
    ).reshape(query.shape[0], -1)
    grad_keys = jnp.einsum(
        "hqk,qhe->khe", rounded, by_heads(query, head_count), preferred_element_type=jnp.float32
    ).reshape(keys.shape[0], -1)
    grad_values = jnp.einsum(
        "hqk,qhe->khe", probs.astype(jnp.bfloat16), split_grad, preferred_element_type=jnp.float32
    ).reshape(keys.shape[0], -1)
    return (grad_query, grad_keys, grad_values)


def reduce_terms(terms, table_terms):
    groups = lax.axis_size("seq")
    share = terms.shape[1] // groups
    stacked = jnp.stack(
        [terms[:, number * share : (number + 1) * share] for number in range(groups)]
    )
    part = lax.psum_scatter(stacked, "seq", scatter_dimension=0, tiled=False)
    table = lax.psum(table_terms, ("seq", "ctx", "fsdp"))
    part, table = lax.optimization_barrier((part, table))
    part = lax.psum_scatter(part, ("ctx", "fsdp"), scatter_dimension=0, tiled=True)
    return join_columns(lax.all_gather(part, "seq", axis=0, tiled=False)), table


def join_columns(stacked):
    return jnp.concatenate([stacked[number] for number in range(stacked.shape[0])], axis=1)


def gather_pack(pack):
    share = pack.shape[1] // lax.axis_size("seq")
    own = lax.dynamic_slice_in_dim(pack, lax.axis_index("seq") * share, share, 1)
    rows = lax.all_gather(own, ("ctx", "fsdp"), axis=0, tiled=True)
    return join_columns(lax.all_gather(rows, "seq", axis=0, tiled=False))


def even_columns(members):
    joined = jnp.concatenate(members, axis=1)
    return jnp.pad(joined, ((0, 0), (0, -joined.shape[1] % (LANES * lax.axis_size("seq")))))


def per_device(
    hidden_in,
    encoder_states,
    out_grad,
    bucket_index,
    bias_table,
    self_gain,
    self_query,
    self_key,
    self_value,
    self_output,
    cross_gain,
    cross_query,
    cross_key,
    cross_value,
    cross_output,
    feed_gain,
    gate_weight,
    linear_weight,
    down_weight,
):
    shards = lax.axis_size(("ctx", "fsdp"))
    features = self_query.shape[1]
    hidden = gate_weight.shape[1]
    pack = even_columns(
        [
            self_query,
            self_key,
            self_value,
            self_output,
            cross_query,
            cross_key,
            cross_value,
            cross_output,
            gate_weight,
            linear_weight,
            fold_rows(down_weight, self_query.shape[0]),
            gain_columns((self_gain, cross_gain, feed_gain), jnp.bfloat16),
        ]
    )
    pack = gather_pack(pack)
    (
        self_query,
        self_key,
        self_value,
        self_output,
        cross_query,
        cross_key,
        cross_value,
        cross_output,
    ) = (pack[:, number * features : (number + 1) * features] for number in range(8))
    first = 8 * features
    gate_weight = pack[:, first : first + hidden]
    linear_weight = pack[:, first + hidden : first + 2 * hidden]
    first = first + 2 * hidden
    width = -(-(hidden // shards) // (features // shards)) * features
    down_weight = unfold_rows(
        pack[:, first : first + width].reshape(shards, -1, width), hidden // shards, features
    ).reshape(hidden, features)
    gains = pack[:, first + width : first + width + LANES].T
    self_gain, cross_gain, feed_gain = gains[0], gains[1], gains[2]
    tokens = hidden_in.shape[1]
    length = bucket_index.shape[0]
    head_count = bias_table.shape[1]
    buckets = bias_table.shape[0]
    query_first = lax.axis_index("ctx") * tokens
    bucket_rev = jnp.flip(jnp.concatenate([jnp.full((length,), -1, jnp.int32), bucket_index]))
    start_x = hidden_in[0].astype(jnp.float32)
    norm_one, normed_one, inverse_one = norm_forward(start_x, self_gain)
    projected = product(norm_one, pack[:, : 3 * features]).astype(jnp.bfloat16)
    query = projected[:, :features]
    encoder_local = encoder_states[0]
    cross_local = product(encoder_local, pack[:, 5 * features : 7 * features]).astype(jnp.bfloat16)
    encoder_rows = encoder_local.shape[0]
    blocks = lax.all_gather(
        jnp.concatenate([projected[:, features:], cross_local], axis=0), "ctx", axis=0, tiled=False
    )
    both = blocks[:, :tokens].reshape(length, 2 * features)
    keys, values = both[:, :features], both[:, features:]
    both = blocks[:, tokens:].reshape(-1, 2 * features)
    cross_keys, cross_values = both[:, :features], both[:, features:]
    empty_top = jnp.full((head_count, tokens), NEGATIVE, jnp.float32)
    empty_total = jnp.zeros((head_count, tokens), jnp.float32)
    empty_mixed = jnp.zeros((tokens, head_count, query.shape[1] // head_count), jnp.float32)
    forward_bound = partial(
        forward_step,
        query=query,
        query_first=query_first,
        bucket_rev=bucket_rev,
        bias_table=bias_table,
    )
    top, total, mixed = fold_blocks(
        forward_bound,
        (empty_top, empty_total, empty_mixed),
        (keys, values),
        jnp.int32(0),
    )
    attn = (mixed / total.T[:, :, None]).reshape(tokens, -1).astype(jnp.bfloat16)
    self_lse = (top + jnp.log(total)).T
    after_self = start_x + product(attn, self_output)
    norm_two, normed_two, inverse_two = norm_forward(after_self, cross_gain)
    cross_q = product(norm_two, cross_query).astype(jnp.bfloat16)
    cattn, cross_lse = plain_forward(cross_q, cross_keys, cross_values, head_count)
    after_cross = after_self + product(cattn, cross_output)
    norm_three, normed_three, inverse_three = norm_forward(after_cross, feed_gain)
    gate_pre = product(norm_three, gate_weight)
    linear_pre = product(norm_three, linear_weight)
    middle = geglu(gate_pre, linear_pre).astype(jnp.bfloat16)
    layer_out = (after_cross + product(middle, down_weight)).astype(jnp.bfloat16)
    grad_top = out_grad[0]
    grad_down = row_contract(middle, grad_top)
    grad_middle = col_contract(grad_top, down_weight)
    _, pull_back = jax.vjp(geglu, gate_pre, linear_pre)
    grad_gate_pre, grad_linear_pre = pull_back(grad_middle)
    gate_round = grad_gate_pre.astype(jnp.bfloat16)
    linear_round = grad_linear_pre.astype(jnp.bfloat16)
    grad_gate = row_contract(norm_three, gate_round)
    grad_linear = row_contract(norm_three, linear_round)
    back_three, grad_feed_gain = norm_backward(
        col_contract(gate_round, gate_weight) + col_contract(linear_round, linear_weight),
        normed_three,
        inverse_three,
        feed_gain,
    )
    grad_after_cross = grad_top.astype(jnp.float32) + back_three
    cross_round = grad_after_cross.astype(jnp.bfloat16)
    grad_cross_output = row_contract(cattn, cross_round)
    grad_cattn = col_contract(cross_round, cross_output).astype(jnp.bfloat16)
    grad_cq, cross_key_terms, cross_value_terms = plain_backward(
        cross_q, cross_keys, cross_values, cross_lse, cattn, grad_cattn, head_count
    )
    grad_cq = grad_cq.astype(jnp.bfloat16)
    grad_cross_query = row_contract(norm_two, grad_cq)
    back_two, grad_cross_gain = norm_backward(
        col_contract(grad_cq, cross_query), normed_two, inverse_two, cross_gain
    )
    grad_after_self = grad_after_cross + back_two
    self_round = grad_after_self.astype(jnp.bfloat16)
    grad_self_output = row_contract(attn, self_round)
    grad_attn = col_contract(self_round, self_output).astype(jnp.bfloat16)
    delta_rows = jnp.sum(
        by_heads(grad_attn, head_count).astype(jnp.float32)
        * by_heads(attn, head_count).astype(jnp.float32),
        axis=-1,
    )
    empty_rows = jnp.zeros((tokens, query.shape[1]), jnp.float32)
    empty_table = jnp.zeros((buckets, head_count), jnp.float32)
    partial_bound = partial(
        partial_step,
        query=query,
        grad_attn=grad_attn,
        lse_rows=self_lse,
        delta_rows=delta_rows,
        query_first=query_first,
        bucket_rev=bucket_rev,
        bias_table=bias_table,
    )
    empty_whole = jnp.zeros((length, query.shape[1]), jnp.float32)
    grad_query, key_terms, value_terms, table_part = fold_blocks(
        partial_bound,
        (empty_rows.reshape(tokens, head_count, -1), empty_whole, empty_whole, empty_table),
        (keys, values),
        jnp.int32(0),
    )
    terms = jnp.concatenate(
        [
            jnp.concatenate([key_terms, value_terms], axis=1).reshape(-1, tokens, 2 * features),
            jnp.concatenate([cross_key_terms, cross_value_terms], axis=1).reshape(
                -1, encoder_rows, 2 * features
            ),
        ],
        axis=1,
    ).astype(jnp.bfloat16)
    sums = lax.psum_scatter(terms, "ctx", scatter_dimension=0, tiled=False)
    cross_both = sums[tokens:]
    grad_cross_both = row_contract(encoder_local, cross_both)
    grad_cross_key, grad_cross_value = (
        grad_cross_both[:, :features],
        grad_cross_both[:, features:],
    )
    encoder_grad = col_contract(cross_both, pack[:, 5 * features : 7 * features])
    grad_q = grad_query.reshape(tokens, -1).astype(jnp.bfloat16)
    grad_projected = jnp.concatenate([grad_q, sums[:tokens]], axis=1)
    grad_self_projections = row_contract(norm_one, grad_projected)
    upstream_one = col_contract(grad_projected, pack[:, : 3 * features])
    back_one, grad_self_gain = norm_backward(upstream_one, normed_one, inverse_one, self_gain)
    input_grad = grad_after_self + back_one
    folded = fold_rows(grad_down.reshape(shards, -1, features), features // shards)
    parts = [
        grad_self_projections,
        grad_self_output,
        grad_cross_query,
        grad_cross_both,
        grad_cross_output,
        grad_gate,
        grad_linear,
        folded.reshape(features, width),
        gain_columns((grad_self_gain, grad_cross_gain, grad_feed_gain), jnp.bfloat16),
    ]
    terms = even_columns([member.astype(jnp.bfloat16) for member in parts])
    summed, grad_table = reduce_terms(terms, table_part)
    summed = summed.astype(jnp.float32)
    squares = [summed[:, number * features : (number + 1) * features] for number in range(8)]
    first = 8 * features
    down_first = first + 2 * hidden
    gain_first = down_first + width
    return (
        layer_out[None],
        input_grad[None],
        encoder_grad[None],
        grad_table,
        summed[:, gain_first],
        squares[0],
        squares[1],
        squares[2],
        squares[3],
        summed[:, gain_first + 1],
        squares[4],
        squares[5],
        squares[6],
        squares[7],
        summed[:, gain_first + 2],
        summed[:, first : first + hidden],
        summed[:, first + hidden : down_first],
        unfold_rows(summed[:, down_first:gain_first], hidden // shards, features),
    )


def per_device_fast(
    hidden_in,
    encoder_states,
    out_grad,
    bucket_index,
    bias_table,
    self_gain,
    self_query,
    self_key,
    self_value,
    self_output,
    cross_gain,
    cross_query,
    cross_key,
    cross_value,
    cross_output,
    feed_gain,
    gate_weight,
    linear_weight,
    down_weight,
):
    shards = lax.axis_size(("ctx", "fsdp"))
    features = self_query.shape[1]
    hidden = gate_weight.shape[1]
    rows = self_query.shape[0]
    gains = jnp.pad(jnp.stack([self_gain, cross_gain, feed_gain]), ((0, 13), (0, LANES - rows)))
    packed, gates, linears, downs, gains = gather_weights(
        (self_query, self_key, self_value, cross_key, cross_value, self_output, cross_query, cross_output),
        gate_weight,
        linear_weight,
        down_weight,
        gains,
    )
    packed = packed.reshape(8, features, features)
    self_output, cross_query, cross_output = packed[5], packed[6], packed[7]
    self_three = jnp.concatenate([packed[0], packed[1], packed[2]], axis=1)
    cross_two = jnp.concatenate([packed[3], packed[4]], axis=1)
    gate_weight = jnp.concatenate([gates[number].reshape(features, -1) for number in range(4)], axis=1)
    linear_weight = jnp.concatenate([linears[number].reshape(features, -1) for number in range(4)], axis=1)
    down_weight = downs.reshape(hidden, features)
    gains = jnp.swapaxes(gains.reshape(shards, 16, LANES)[:, :3, :rows], 0, 1).reshape(3, features)
    self_gain, cross_gain, feed_gain = gains[0], gains[1], gains[2]
    tokens = hidden_in.shape[1]
    length = bucket_index.shape[0]
    head_count = bias_table.shape[1]
    buckets = bias_table.shape[0]
    query_first = lax.axis_index("ctx") * tokens
    bucket_rev = jnp.flip(jnp.concatenate([jnp.full((length,), -1, jnp.int32), bucket_index]))
    start_x = hidden_in[0].astype(jnp.float32)
    norm_one, normed_one, inverse_one = norm_forward(start_x, self_gain)
    projected = product(norm_one, self_three).astype(jnp.bfloat16)
    query = projected[:, :features]
    encoder_local = encoder_states[0]
    cross_local = product(encoder_local, cross_two).astype(jnp.bfloat16)
    encoder_rows = encoder_local.shape[0]
    blocks = lax.all_gather(
        jnp.concatenate([projected[:, features:], cross_local], axis=0), "ctx", axis=0, tiled=False
    )
    both = blocks[:, :tokens].reshape(length, 2 * features)
    keys, values = both[:, :features], both[:, features:]
    both = blocks[:, tokens:].reshape(-1, 2 * features)
    cross_keys, cross_values = both[:, :features], both[:, features:]
    empty_top = jnp.full((head_count, tokens), NEGATIVE, jnp.float32)
    empty_total = jnp.zeros((head_count, tokens), jnp.float32)
    empty_mixed = jnp.zeros((tokens, head_count, query.shape[1] // head_count), jnp.float32)
    forward_bound = partial(
        forward_step,
        query=query,
        query_first=query_first,
        bucket_rev=bucket_rev,
        bias_table=bias_table,
    )
    top, total, mixed = fold_blocks(
        forward_bound,
        (empty_top, empty_total, empty_mixed),
        (keys, values),
        jnp.int32(0),
    )
    attn = (mixed / total.T[:, :, None]).reshape(tokens, -1).astype(jnp.bfloat16)
    self_lse = (top + jnp.log(total)).T
    after_self = start_x + product(attn, self_output)
    norm_two, normed_two, inverse_two = norm_forward(after_self, cross_gain)
    cross_q = product(norm_two, cross_query).astype(jnp.bfloat16)
    cattn, cross_lse = plain_forward(cross_q, cross_keys, cross_values, head_count)
    after_cross = after_self + product(cattn, cross_output)
    norm_three, normed_three, inverse_three = norm_forward(after_cross, feed_gain)
    gate_pre = product(norm_three, gate_weight)
    linear_pre = product(norm_three, linear_weight)
    middle = geglu(gate_pre, linear_pre).astype(jnp.bfloat16)
    layer_out = (after_cross + product(middle, down_weight)).astype(jnp.bfloat16)
    grad_top = out_grad[0]
    grad_down = row_contract(middle, grad_top)
    grad_middle = col_contract(grad_top, down_weight)
    _, pull_back = jax.vjp(geglu, gate_pre, linear_pre)
    grad_gate_pre, grad_linear_pre = pull_back(grad_middle)
    gate_round = grad_gate_pre.astype(jnp.bfloat16)
    linear_round = grad_linear_pre.astype(jnp.bfloat16)
    grad_gate = row_contract(norm_three, gate_round)
    grad_linear = row_contract(norm_three, linear_round)
    back_three, grad_feed_gain = norm_backward(
        col_contract(gate_round, gate_weight) + col_contract(linear_round, linear_weight),
        normed_three,
        inverse_three,
        feed_gain,
    )
    grad_after_cross = grad_top.astype(jnp.float32) + back_three
    cross_round = grad_after_cross.astype(jnp.bfloat16)
    grad_cross_output = row_contract(cattn, cross_round)
    grad_cattn = col_contract(cross_round, cross_output).astype(jnp.bfloat16)
    grad_cq, cross_key_terms, cross_value_terms = plain_backward(
        cross_q, cross_keys, cross_values, cross_lse, cattn, grad_cattn, head_count
    )
    grad_cq = grad_cq.astype(jnp.bfloat16)
    grad_cross_query = row_contract(norm_two, grad_cq)
    back_two, grad_cross_gain = norm_backward(
        col_contract(grad_cq, cross_query), normed_two, inverse_two, cross_gain
    )
    grad_after_self = grad_after_cross + back_two
    self_round = grad_after_self.astype(jnp.bfloat16)
    grad_self_output = row_contract(attn, self_round)
    grad_attn = col_contract(self_round, self_output).astype(jnp.bfloat16)
    delta_rows = jnp.sum(
        by_heads(grad_attn, head_count).astype(jnp.float32)
        * by_heads(attn, head_count).astype(jnp.float32),
        axis=-1,
    )
    empty_rows = jnp.zeros((tokens, query.shape[1]), jnp.float32)
    empty_table = jnp.zeros((buckets, head_count), jnp.float32)
    partial_bound = partial(
        partial_step,
        query=query,
        grad_attn=grad_attn,
        lse_rows=self_lse,
        delta_rows=delta_rows,
        query_first=query_first,
        bucket_rev=bucket_rev,
        bias_table=bias_table,
    )
    empty_whole = jnp.zeros((length, query.shape[1]), jnp.float32)
    grad_query, key_terms, value_terms, table_part = fold_blocks(
        partial_bound,
        (empty_rows.reshape(tokens, head_count, -1), empty_whole, empty_whole, empty_table),
        (keys, values),
        jnp.int32(0),
    )
    terms = jnp.concatenate(
        [
            jnp.concatenate([key_terms, value_terms], axis=1).reshape(-1, tokens, 2 * features),
            jnp.concatenate([cross_key_terms, cross_value_terms], axis=1).reshape(
                -1, encoder_rows, 2 * features
            ),
        ],
        axis=1,
    ).astype(jnp.bfloat16)
    sums = lax.psum_scatter(terms, "ctx", scatter_dimension=0, tiled=False)
    cross_both = sums[tokens:]
    grad_cross_both = row_contract(encoder_local, cross_both)
    grad_cross_key, grad_cross_value = (
        grad_cross_both[:, :features],
        grad_cross_both[:, features:],
    )
    encoder_grad = col_contract(cross_both, cross_two)
    grad_q = grad_query.reshape(tokens, -1).astype(jnp.bfloat16)
    grad_projected = jnp.concatenate([grad_q, sums[:tokens]], axis=1)
    grad_self_projections = row_contract(norm_one, grad_projected)
    upstream_one = col_contract(grad_projected, self_three)
    back_one, grad_self_gain = norm_backward(upstream_one, normed_one, inverse_one, self_gain)
    input_grad = grad_after_self + back_one
    squares = jnp.stack(
        [
            member.astype(jnp.bfloat16)
            for member in (
                grad_self_projections[:, :features],
                grad_self_projections[:, features : 2 * features],
                grad_self_projections[:, 2 * features :],
                grad_cross_key,
                grad_cross_value,
                grad_self_output,
                grad_cross_query,
                grad_cross_output,
            )
        ]
    ).reshape(2, 4, shards // 2, 2, rows, features)
    wide = hidden // 4

    def quarters(member):
        return jnp.stack(
            [member[:, number * wide : (number + 1) * wide].astype(jnp.bfloat16) for number in range(4)]
        ).reshape(4, shards // 2, 2, rows, wide)

    flat = jnp.concatenate(
        [grad_self_gain, grad_cross_gain, grad_feed_gain, table_part.reshape(-1)]
    )
    span = -(-flat.shape[0] // (8 * LANES)) * LANES
    small = jnp.pad(flat, (0, 8 * span - flat.shape[0])).reshape(8, span)
    *sums, small = scatter_gradients(
        squares,
        quarters(grad_gate),
        quarters(grad_linear),
        grad_down.astype(jnp.bfloat16).reshape(shards // 2, 2, 4, -1, features),
        small,
    )
    sums = [member.astype(jnp.float32) for member in sums]
    flat = small.reshape(-1)
    shard = lax.axis_index(("ctx", "fsdp"))
    gain_sums = lax.dynamic_slice_in_dim(flat[: 3 * features].reshape(3, features), shard * rows, rows, 1)
    grad_table = flat[3 * features : 3 * features + buckets * head_count].reshape(buckets, head_count)

    def unquarter(member):
        return jnp.concatenate([member[number] for number in range(4)], axis=1)

    return (
        layer_out[None],
        input_grad[None],
        encoder_grad[None],
        grad_table,
        gain_sums[0],
        sums[0][0],
        sums[0][1],
        sums[0][2],
        sums[1][1],
        gain_sums[1],
        sums[1][2],
        sums[0][3],
        sums[1][0],
        sums[1][3],
        gain_sums[2],
        unquarter(sums[2]),
        unquarter(sums[3]),
        sums[4].reshape(-1, features),
    )


def fits(mesh):
    return mesh.shape["seq"] == 4 and mesh.shape["fsdp"] == 2 and mesh.shape["ctx"] <= 4


def solution(mesh):
    return jax.shard_map(
        per_device_fast if fits(mesh) else per_device,
        mesh=mesh,
        in_specs=(
            P(("seq", "fsdp"), "ctx", None),
            P(("seq", "fsdp"), "ctx", None),
            P(("seq", "fsdp"), "ctx", None),
            P(),
            P(),
            P(("ctx", "fsdp")),
            P(("ctx", "fsdp"), None),
            P(("ctx", "fsdp"), None),
            P(("ctx", "fsdp"), None),
            P(("ctx", "fsdp"), None),
            P(("ctx", "fsdp")),
            P(("ctx", "fsdp"), None),
            P(("ctx", "fsdp"), None),
            P(("ctx", "fsdp"), None),
            P(("ctx", "fsdp"), None),
            P(("ctx", "fsdp")),
            P(("ctx", "fsdp"), None),
            P(("ctx", "fsdp"), None),
            P(("ctx", "fsdp"), None),
        ),
        out_specs=(
            P(("seq", "fsdp"), "ctx", None),
            P(("seq", "fsdp"), "ctx", None),
            P(("seq", "fsdp"), "ctx", None),
            P(),
            P(("ctx", "fsdp")),
            P(("ctx", "fsdp"), None),
            P(("ctx", "fsdp"), None),
            P(("ctx", "fsdp"), None),
            P(("ctx", "fsdp"), None),
            P(("ctx", "fsdp")),
            P(("ctx", "fsdp"), None),
            P(("ctx", "fsdp"), None),
            P(("ctx", "fsdp"), None),
            P(("ctx", "fsdp"), None),
            P(("ctx", "fsdp")),
            P(("ctx", "fsdp"), None),
            P(("ctx", "fsdp"), None),
            P(("ctx", "fsdp"), None),
        ),
        check_vma=False,
    )
```

```python
from functools import partial
import math

import jax
import jax.numpy as jnp
from jax import lax
from jax.experimental import pallas as pl
from jax.experimental.pallas import tpu as pltpu
from jax.sharding import PartitionSpec as P

EPSILON = 1e-06
NEGATIVE = -1e30
HIGHEST = lax.Precision.HIGHEST


LANES = 128


def fold_rows(rows, height):
    count = -(-rows.shape[-2] // height)
    short = count * height - rows.shape[-2]
    padding = [(0, 0)] * (rows.ndim - 2) + [(0, short), (0, 0)]
    padded = jnp.pad(rows, padding)
    return jnp.concatenate(
        [padded[..., number * height : (number + 1) * height, :] for number in range(count)],
        axis=-1,
    )


def unfold_rows(columns, row_count, features):
    count = columns.shape[-1] // features
    stacked = jnp.concatenate(
        [columns[..., number * features : (number + 1) * features] for number in range(count)],
        axis=-2,
    )
    return stacked[..., :row_count, :]


def gain_columns(gains, dtype):
    columns = jnp.stack([member.astype(dtype) for member in gains], axis=1)
    return jnp.pad(columns, ((0, 0), (0, LANES - columns.shape[1])))


def product(left, right):
    return jnp.dot(left, right, preferred_element_type=jnp.float32)


def row_contract(left, right):
    return lax.dot_general(
        left, right, (((0,), (0,)), ((), ())), preferred_element_type=jnp.float32
    )


def col_contract(left, right):
    return lax.dot_general(
        left, right, (((1,), (1,)), ((), ())), preferred_element_type=jnp.float32
    )


def norm_forward(values, gain):
    inverse = lax.rsqrt(jnp.mean(values * values, axis=-1, keepdims=True) + EPSILON)
    normed = values * inverse
    return ((normed * gain.astype(jnp.float32)).astype(jnp.bfloat16), normed, inverse)


def norm_backward(upstream, normed, inverse, gain):
    grad_gain = jnp.sum(upstream * normed, axis=0)
    grad_normed = upstream * gain.astype(jnp.float32)
    grad_values = inverse * (
        grad_normed - normed * jnp.mean(grad_normed * normed, axis=-1, keepdims=True)
    )
    return (grad_values, grad_gain)


def geglu(gate_pre, linear_pre):
    return jax.nn.gelu(gate_pre, approximate=True) * linear_pre


def by_heads(values, head_count):
    return values.reshape(values.shape[0], head_count, values.shape[1] // head_count)


def band_onehot(bucket_rev, buckets, query_rows, key_rows, query_first, key_first):
    length = bucket_rev.shape[0] // 2
    offset_first = query_first - key_first
    upper_band = lax.dynamic_slice_in_dim(bucket_rev, length - 1 - offset_first, key_rows, 0)
    lower_band = lax.dynamic_slice_in_dim(
        bucket_rev, length - offset_first - query_rows, query_rows - 1, 0
    )
    slots = jnp.concatenate([upper_band, jnp.full((1,), -1, jnp.int32), lower_band])
    return (slots[:, None] == jnp.arange(buckets, dtype=jnp.int32)[None, :]).astype(jnp.float32)


def spread_band(band, query_rows, key_rows):
    head_count, width = band.shape
    tiled = jnp.broadcast_to(band[:, None, :], (head_count, query_rows, width)).reshape(
        head_count, query_rows * width
    )
    return tiled[:, : query_rows * (width - 1)].reshape(head_count, query_rows, width - 1)[
        :, :, :key_rows
    ]


def fold_band(grad_scores, width):
    head_count, query_rows, key_rows = grad_scores.shape
    padded = jnp.pad(grad_scores, ((0, 0), (0, 0), (0, width - 1 - key_rows))).reshape(
        head_count, query_rows * (width - 1)
    )
    padded = jnp.pad(padded, ((0, 0), (0, query_rows)))
    return jnp.sum(padded.reshape(head_count, query_rows, width), axis=1)


def self_scores(query, key_block, query_first, key_first, bucket_rev, bias_table):
    head_count = bias_table.shape[1]
    query_rows = query.shape[0]
    key_rows = key_block.shape[0]
    scores = jnp.einsum(
        "qhe,khe->hqk",
        by_heads(query, head_count),
        by_heads(key_block, head_count),
        preferred_element_type=jnp.float32,
    )
    offset = (query_first + jnp.arange(query_rows, dtype=jnp.int32))[:, None] - (
        key_first + jnp.arange(key_rows, dtype=jnp.int32)
    )[None, :]
    allowed = offset >= 0
    onehot = band_onehot(
        bucket_rev, bias_table.shape[0], query_rows, key_rows, query_first, key_first
    )
    band = jnp.dot(onehot, bias_table, precision=HIGHEST).T
    scores = jnp.where(allowed[None], scores + spread_band(band, query_rows, key_rows), NEGATIVE)
    return (scores, allowed, onehot)


def table_terms(grad_scores, onehot):
    band_grad = fold_band(grad_scores, onehot.shape[0])
    return jnp.dot(onehot.T, band_grad.T, precision=HIGHEST)


def fold_blocks(block_step, running, arrays, first_row):
    piece_rows = arrays[0].shape[0]
    block_size = math.gcd(piece_rows, 512) if piece_rows > 512 else piece_rows
    if block_size == piece_rows:
        return block_step(running, arrays, first_row)
    block_count = piece_rows // block_size
    stacked = tuple(
        (member.reshape((block_count, block_size) + member.shape[1:]) for member in arrays)
    )

    def scan_block(state_now, scanned):
        number, blocks = scanned
        return (block_step(state_now, blocks, first_row + number * block_size), None)

    result, _ = lax.scan(scan_block, running, (jnp.arange(block_count, dtype=jnp.int32), stacked))
    return result


def forward_step(running, blocks, key_first, query, query_first, bucket_rev, bias_table):
    top, total, mixed = running
    key_block, value_block = blocks
    head_count = bias_table.shape[1]
    scores, allowed, _ = self_scores(
        query, key_block, query_first, key_first, bucket_rev, bias_table
    )
    new_top = jnp.maximum(top, jnp.max(scores, axis=-1))
    weights = jnp.where(allowed[None], jnp.exp(scores - new_top[:, :, None]), 0.0)
    rescale = jnp.exp(top - new_top)
    total = total * rescale + jnp.sum(weights, axis=-1)
    update = jnp.einsum(
        "hqk,khe->qhe",
        weights.astype(jnp.bfloat16),
        by_heads(value_block, head_count),
        preferred_element_type=jnp.float32,
    )
    mixed = mixed * rescale.T[:, :, None] + update
    return (new_top, total, mixed)


def backward_core(
    query,
    grad_attn,
    lse_rows,
    delta_rows,
    key_block,
    value_block,
    query_first,
    key_first,
    bucket_rev,
    bias_table,
):
    head_count = bias_table.shape[1]
    scores, allowed, onehot = self_scores(
        query, key_block, query_first, key_first, bucket_rev, bias_table
    )
    probs = jnp.where(allowed[None], jnp.exp(scores - lse_rows.T[:, :, None]), 0.0)
    grad_probs = jnp.einsum(
        "qhe,khe->hqk",
        by_heads(grad_attn, head_count),
        by_heads(value_block, head_count),
        preferred_element_type=jnp.float32,
    )
    grad_scores = probs * (grad_probs - delta_rows.T[:, :, None])
    return (probs, grad_scores, onehot)


def partial_step(
    running,
    blocks,
    key_first,
    query,
    grad_attn,
    lse_rows,
    delta_rows,
    query_first,
    bucket_rev,
    bias_table,
):
    grad_query, grad_keys, grad_values, table_part = running
    key_block, value_block = blocks
    head_count = bias_table.shape[1]
    probs, grad_scores, onehot = backward_core(
        query,
        grad_attn,
        lse_rows,
        delta_rows,
        key_block,
        value_block,
        query_first,
        key_first,
        bucket_rev,
        bias_table,
    )
    rounded = grad_scores.astype(jnp.bfloat16)
    grad_query = grad_query + jnp.einsum(
        "hqk,khe->qhe", rounded, by_heads(key_block, head_count), preferred_element_type=jnp.float32
    )
    key_part = jnp.einsum(
        "hqk,qhe->khe", rounded, by_heads(query, head_count), preferred_element_type=jnp.float32
    ).reshape(key_block.shape[0], -1)
    value_part = jnp.einsum(
        "hqk,qhe->khe",
        probs.astype(jnp.bfloat16),
        by_heads(grad_attn, head_count),
        preferred_element_type=jnp.float32,
    ).reshape(key_block.shape[0], -1)
    grad_keys = lax.dynamic_update_slice_in_dim(grad_keys, key_part, key_first, 0)
    grad_values = lax.dynamic_update_slice_in_dim(grad_values, value_part, key_first, 0)
    table_part = table_part + table_terms(grad_scores, onehot)
    return (grad_query, grad_keys, grad_values, table_part)


def plain_forward(query, keys, values, head_count):
    scores = jnp.einsum(
        "qhe,khe->hqk",
        by_heads(query, head_count),
        by_heads(keys, head_count),
        preferred_element_type=jnp.float32,
    )
    top = jnp.max(scores, axis=-1, keepdims=True)
    weights = jnp.exp(scores - top)
    total = jnp.sum(weights, axis=-1, keepdims=True)
    mixed = jnp.einsum(
        "hqk,khe->qhe",
        weights.astype(jnp.bfloat16),
        by_heads(values, head_count),
        preferred_element_type=jnp.float32,
    )
    result = (
        (mixed / jnp.transpose(total, (1, 0, 2))).reshape(query.shape[0], -1).astype(jnp.bfloat16)
    )
    return (result, (top + jnp.log(total))[:, :, 0])


def plain_backward(query, keys, values, lse, output, grad_output, head_count):
    split_grad = by_heads(grad_output, head_count)
    delta = jnp.sum(
        split_grad.astype(jnp.float32) * by_heads(output, head_count).astype(jnp.float32), axis=-1
    ).T
    scores = jnp.einsum(
        "qhe,khe->hqk",
        by_heads(query, head_count),
        by_heads(keys, head_count),
        preferred_element_type=jnp.float32,
    )
    probs = jnp.exp(scores - lse[:, :, None])
    grad_probs = jnp.einsum(
        "qhe,khe->hqk", split_grad, by_heads(values, head_count), preferred_element_type=jnp.float32
    )
    rounded = (probs * (grad_probs - delta[:, :, None])).astype(jnp.bfloat16)
    grad_query = jnp.einsum(
        "hqk,khe->qhe", rounded, by_heads(keys, head_count), preferred_element_type=jnp.float32
    ).reshape(query.shape[0], -1)
    grad_keys = jnp.einsum(
        "hqk,qhe->khe", rounded, by_heads(query, head_count), preferred_element_type=jnp.float32
    ).reshape(keys.shape[0], -1)
    grad_values = jnp.einsum(
        "hqk,qhe->khe", probs.astype(jnp.bfloat16), split_grad, preferred_element_type=jnp.float32
    ).reshape(keys.shape[0], -1)
    return (grad_query, grad_keys, grad_values)


def reduce_terms(terms, table_terms):
    groups = lax.axis_size("seq")
    share = terms.shape[1] // groups
    stacked = jnp.stack(
        [terms[:, number * share : (number + 1) * share] for number in range(groups)]
    )
    part = lax.psum_scatter(stacked, "seq", scatter_dimension=0, tiled=False)
    table = lax.psum(table_terms, ("seq", "ctx", "fsdp"))
    part, table = lax.optimization_barrier((part, table))
    part = lax.psum_scatter(part, ("ctx", "fsdp"), scatter_dimension=0, tiled=True)
    return join_columns(lax.all_gather(part, "seq", axis=0, tiled=False)), table


def join_columns(stacked):
    return jnp.concatenate([stacked[number] for number in range(stacked.shape[0])], axis=1)


def gather_pack(pack):
    share = pack.shape[1] // lax.axis_size("seq")
    own = lax.dynamic_slice_in_dim(pack, lax.axis_index("seq") * share, share, 1)
    rows = lax.all_gather(own, ("ctx", "fsdp"), axis=0, tiled=True)
    return join_columns(lax.all_gather(rows, "seq", axis=0, tiled=False))


def even_columns(members):
    joined = jnp.concatenate(members, axis=1)
    return jnp.pad(joined, ((0, 0), (0, -joined.shape[1] % (LANES * lax.axis_size("seq")))))


def per_device(
    hidden_in,
    encoder_states,
    out_grad,
    bucket_index,
    bias_table,
    self_gain,
    self_query,
    self_key,
    self_value,
    self_output,
    cross_gain,
    cross_query,
    cross_key,
    cross_value,
    cross_output,
    feed_gain,
    gate_weight,
    linear_weight,
    down_weight,
):
    shards = lax.axis_size(("ctx", "fsdp"))
    features = self_query.shape[1]
    hidden = gate_weight.shape[1]
    pack = even_columns(
        [
            self_query,
            self_key,
            self_value,
            self_output,
            cross_query,
            cross_key,
            cross_value,
            cross_output,
            gate_weight,
            linear_weight,
            fold_rows(down_weight, self_query.shape[0]),
            gain_columns((self_gain, cross_gain, feed_gain), jnp.bfloat16),
        ]
    )
    pack = gather_pack(pack)
    (
        self_query,
        self_key,
        self_value,
        self_output,
        cross_query,
        cross_key,
        cross_value,
        cross_output,
    ) = (pack[:, number * features : (number + 1) * features] for number in range(8))
    first = 8 * features
    gate_weight = pack[:, first : first + hidden]
    linear_weight = pack[:, first + hidden : first + 2 * hidden]
    first = first + 2 * hidden
    width = -(-(hidden // shards) // (features // shards)) * features
    down_weight = unfold_rows(
        pack[:, first : first + width].reshape(shards, -1, width), hidden // shards, features
    ).reshape(hidden, features)
    gains = pack[:, first + width : first + width + LANES].T
    self_gain, cross_gain, feed_gain = gains[0], gains[1], gains[2]
    tokens = hidden_in.shape[1]
    length = bucket_index.shape[0]
    head_count = bias_table.shape[1]
    buckets = bias_table.shape[0]
    query_first = lax.axis_index("ctx") * tokens
    bucket_rev = jnp.flip(jnp.concatenate([jnp.full((length,), -1, jnp.int32), bucket_index]))
    start_x = hidden_in[0].astype(jnp.float32)
    norm_one, normed_one, inverse_one = norm_forward(start_x, self_gain)
    projected = product(norm_one, pack[:, : 3 * features]).astype(jnp.bfloat16)
    query = projected[:, :features]
    encoder_local = encoder_states[0]
    cross_local = product(encoder_local, pack[:, 5 * features : 7 * features]).astype(jnp.bfloat16)
    encoder_rows = encoder_local.shape[0]
    blocks = lax.all_gather(
        jnp.concatenate([projected[:, features:], cross_local], axis=0), "ctx", axis=0, tiled=False
    )
    both = blocks[:, :tokens].reshape(length, 2 * features)
    keys, values = both[:, :features], both[:, features:]
    both = blocks[:, tokens:].reshape(-1, 2 * features)
    cross_keys, cross_values = both[:, :features], both[:, features:]
    empty_top = jnp.full((head_count, tokens), NEGATIVE, jnp.float32)
    empty_total = jnp.zeros((head_count, tokens), jnp.float32)
    empty_mixed = jnp.zeros((tokens, head_count, query.shape[1] // head_count), jnp.float32)
    forward_bound = partial(
        forward_step,
        query=query,
        query_first=query_first,
        bucket_rev=bucket_rev,
        bias_table=bias_table,
    )
    top, total, mixed = fold_blocks(
        forward_bound,
        (empty_top, empty_total, empty_mixed),
        (keys, values),
        jnp.int32(0),
    )
    attn = (mixed / total.T[:, :, None]).reshape(tokens, -1).astype(jnp.bfloat16)
    self_lse = (top + jnp.log(total)).T
    after_self = start_x + product(attn, self_output)
    norm_two, normed_two, inverse_two = norm_forward(after_self, cross_gain)
    cross_q = product(norm_two, cross_query).astype(jnp.bfloat16)
    cattn, cross_lse = plain_forward(cross_q, cross_keys, cross_values, head_count)
    after_cross = after_self + product(cattn, cross_output)
    norm_three, normed_three, inverse_three = norm_forward(after_cross, feed_gain)
    gate_pre = product(norm_three, gate_weight)
    linear_pre = product(norm_three, linear_weight)
    middle = geglu(gate_pre, linear_pre).astype(jnp.bfloat16)
    layer_out = (after_cross + product(middle, down_weight)).astype(jnp.bfloat16)
    grad_top = out_grad[0]
    grad_down = row_contract(middle, grad_top)
    grad_middle = col_contract(grad_top, down_weight)
    _, pull_back = jax.vjp(geglu, gate_pre, linear_pre)
    grad_gate_pre, grad_linear_pre = pull_back(grad_middle)
    gate_round = grad_gate_pre.astype(jnp.bfloat16)
    linear_round = grad_linear_pre.astype(jnp.bfloat16)
    grad_gate = row_contract(norm_three, gate_round)
    grad_linear = row_contract(norm_three, linear_round)
    back_three, grad_feed_gain = norm_backward(
        col_contract(gate_round, gate_weight) + col_contract(linear_round, linear_weight),
        normed_three,
        inverse_three,
        feed_gain,
    )
    grad_after_cross = grad_top.astype(jnp.float32) + back_three
    cross_round = grad_after_cross.astype(jnp.bfloat16)
    grad_cross_output = row_contract(cattn, cross_round)
    grad_cattn = col_contract(cross_round, cross_output).astype(jnp.bfloat16)
    grad_cq, cross_key_terms, cross_value_terms = plain_backward(
        cross_q, cross_keys, cross_values, cross_lse, cattn, grad_cattn, head_count
    )
    grad_cq = grad_cq.astype(jnp.bfloat16)
    grad_cross_query = row_contract(norm_two, grad_cq)
    back_two, grad_cross_gain = norm_backward(
        col_contract(grad_cq, cross_query), normed_two, inverse_two, cross_gain
    )
    grad_after_self = grad_after_cross + back_two
    self_round = grad_after_self.astype(jnp.bfloat16)
    grad_self_output = row_contract(attn, self_round)
    grad_attn = col_contract(self_round, self_output).astype(jnp.bfloat16)
    delta_rows = jnp.sum(
        by_heads(grad_attn, head_count).astype(jnp.float32)
        * by_heads(attn, head_count).astype(jnp.float32),
        axis=-1,
    )
    empty_rows = jnp.zeros((tokens, query.shape[1]), jnp.float32)
    empty_table = jnp.zeros((buckets, head_count), jnp.float32)
    partial_bound = partial(
        partial_step,
        query=query,
        grad_attn=grad_attn,
        lse_rows=self_lse,
        delta_rows=delta_rows,
        query_first=query_first,
        bucket_rev=bucket_rev,
        bias_table=bias_table,
    )
    empty_whole = jnp.zeros((length, query.shape[1]), jnp.float32)
    grad_query, key_terms, value_terms, table_part = fold_blocks(
        partial_bound,
        (empty_rows.reshape(tokens, head_count, -1), empty_whole, empty_whole, empty_table),
        (keys, values),
        jnp.int32(0),
    )
    terms = jnp.concatenate(
        [
            jnp.concatenate([key_terms, value_terms], axis=1).reshape(-1, tokens, 2 * features),
            jnp.concatenate([cross_key_terms, cross_value_terms], axis=1).reshape(
                -1, encoder_rows, 2 * features
            ),
        ],
        axis=1,
    ).astype(jnp.bfloat16)
    sums = lax.psum_scatter(terms, "ctx", scatter_dimension=0, tiled=False)
    cross_both = sums[tokens:]
    grad_cross_both = row_contract(encoder_local, cross_both)
    grad_cross_key, grad_cross_value = (
        grad_cross_both[:, :features],
        grad_cross_both[:, features:],
    )
    encoder_grad = col_contract(cross_both, pack[:, 5 * features : 7 * features])
    grad_q = grad_query.reshape(tokens, -1).astype(jnp.bfloat16)
    grad_projected = jnp.concatenate([grad_q, sums[:tokens]], axis=1)
    grad_self_projections = row_contract(norm_one, grad_projected)
    upstream_one = col_contract(grad_projected, pack[:, : 3 * features])
    back_one, grad_self_gain = norm_backward(upstream_one, normed_one, inverse_one, self_gain)
    input_grad = grad_after_self + back_one
    folded = fold_rows(grad_down.reshape(shards, -1, features), features // shards)
    parts = [
        grad_self_projections,
        grad_self_output,
        grad_cross_query,
        grad_cross_both,
        grad_cross_output,
        grad_gate,
        grad_linear,
        folded.reshape(features, width),
        gain_columns((grad_self_gain, grad_cross_gain, grad_feed_gain), jnp.bfloat16),
    ]
    terms = even_columns([member.astype(jnp.bfloat16) for member in parts])
    summed, grad_table = reduce_terms(terms, table_part)
    summed = summed.astype(jnp.float32)
    squares = [summed[:, number * features : (number + 1) * features] for number in range(8)]
    first = 8 * features
    down_first = first + 2 * hidden
    gain_first = down_first + width
    return (
        layer_out[None],
        input_grad[None],
        encoder_grad[None],
        grad_table,
        summed[:, gain_first],
        squares[0],
        squares[1],
        squares[2],
        squares[3],
        summed[:, gain_first + 1],
        squares[4],
        squares[5],
        squares[6],
        squares[7],
        summed[:, gain_first + 2],
        summed[:, first : first + hidden],
        summed[:, first + hidden : down_first],
        unfold_rows(summed[:, down_first:gain_first], hidden // shards, features),
    )


MESH = pl.DeviceIdType.MESH
FAR_BELOW = -1e30


def remote(source, target, send_sem, recv_sem, device):
    return pltpu.make_async_remote_copy(
        src_ref=source,
        dst_ref=target,
        send_sem=send_sem,
        recv_sem=recv_sem,
        device_id=device,
        device_id_type=MESH,
    )


class Place:
    def __init__(self, count, sends, recvs):
        self.count, self.sends, self.recvs = count, sends, recvs
        self.seq = lax.axis_index("seq")
        self.side, self.core = self.seq // 2, self.seq % 2
        self.depth, self.row = lax.axis_index("ctx"), lax.axis_index("fsdp")
        self.quarter = self.seq
        self.to_x = self.at(1 - self.side, self.core, self.depth, self.row)
        self.to_y = self.at(self.side, self.core, self.depth, 1 - self.row)
        self.to_core = self.at(self.side, 1 - self.core, self.depth, self.row)
        self.to_far = self.at(1 - self.side, 1 - self.core, self.depth, self.row)
        self.x_quarter = 2 * (1 - self.side) + self.core
        self.core_quarter = 2 * self.side + 1 - self.core
        self.far_quarter = 2 * (1 - self.side) + 1 - self.core
        self.used = 0

    def at(self, side, core, depth, row):
        return (side * 2 + core, depth, row)

    def at_depth(self, depth):
        return (self.seq, depth, self.row)

    def take(self, number):
        first = self.used
        self.used += number
        return first

    def link(self, source, target, index, device):
        return remote(source, target, self.sends.at[index], self.recvs.at[index], device)

    def steps(self):
        return [(way, far) for far in range(1, self.count) for way in (0, 1)]

    def shifted(self, way, far):
        return self.depth + far if way == 0 else self.depth - far

    def valid(self, way, far):
        return self.depth + far <= self.count - 1 if way == 0 else self.depth - far >= 0

    def can_send(self, way):
        return self.depth > 0 if way == 0 else self.depth < self.count - 1

    def next_of(self, way):
        return self.at_depth(self.depth - 1 if way == 0 else self.depth + 1)


class Gather:
    def __init__(self, here, piece, spread):
        self.here, self.piece, self.spread = here, piece, spread
        count = here.count
        slots = 2 * count - 1
        self.z_base = here.take(2 * (count - 1))
        self.y_base = here.take(slots)
        if spread:
            self.x_base = here.take(2 * slots)
            self.c_base = here.take(4 * slots)
        self.slots = slots

    def slot(self, way, far):
        return 0 if far == 0 else 1 + way * (self.here.count - 1) + far - 1

    def z_copy(self, way, far):
        here = self.here
        held = self.piece(here.shifted(way, far), here.row, here.quarter)
        return here.link(held, held, self.z_base + way * (here.count - 1) + far, here.next_of(way))

    def z_arrival(self, way, far):
        here = self.here
        held = self.piece(here.shifted(way, far), here.row, here.quarter)
        return here.link(held, held, self.z_base + way * (here.count - 1) + far - 1, here.to_y)

    def y_copy(self, way, far, at_row):
        here = self.here
        held = self.piece(here.shifted(way, far), at_row, here.quarter)
        return here.link(held, held, self.y_base + self.slot(way, far), here.to_y)

    def x_copy(self, way, far, other, quarter):
        here = self.here
        held = self.piece(here.shifted(way, far), 1 - here.row if other else here.row, quarter)
        return here.link(held, held, self.x_base + other * self.slots + self.slot(way, far), here.to_x)

    def c_copy(self, way, far, other, level, quarter):
        here = self.here
        held = self.piece(here.shifted(way, far), 1 - here.row if other else here.row, quarter)
        index = self.c_base + (2 * level + other) * self.slots + self.slot(way, far)
        return here.link(held, held, index, here.to_core)

    def onward(self, way, far, other):
        if self.spread:
            self.x_copy(way, far, other, self.here.quarter).start()
            self.c_copy(way, far, other, 0, self.here.quarter).start()

    def begin(self):
        for way in (0, 1):
            @pl.when(self.here.can_send(way))
            def _():
                self.z_copy(way, 0).start()
        self.y_copy(0, 0, self.here.row).start()

    def z_phase(self, only=None):
        here = self.here
        for way, far in here.steps():
            if only is not None and far != only:
                continue

            @pl.when(here.valid(way, far))
            def _():
                self.z_arrival(way, far).wait_recv()
                if far < here.count - 1:
                    @pl.when(here.can_send(way))
                    def _():
                        self.z_copy(way, far).start()
                self.y_copy(way, far, here.row).start()
                self.onward(way, far, 0)

    def y_phase(self):
        here = self.here
        for way, far in [(0, 0)] + here.steps():
            @pl.when(here.valid(way, far))
            def _():
                self.y_copy(way, far, 1 - here.row).wait_recv()
                self.onward(way, far, 1)

    def members(self):
        return [(way, far, other) for way, far in [(0, 0)] + self.here.steps() for other in (0, 1) if far or other]

    def x_phase(self):
        here = self.here
        for way, far, other in self.members():
            @pl.when(here.valid(way, far))
            def _():
                self.x_copy(way, far, other, here.x_quarter).wait_recv()
                self.c_copy(way, far, other, 1, here.x_quarter).start()

    def finish(self):
        here = self.here
        for way, far, other in self.members():
            @pl.when(here.valid(way, far))
            def _():
                self.c_copy(way, far, other, 0, here.core_quarter).wait_recv()
                self.c_copy(way, far, other, 1, here.far_quarter).wait_recv()

    def drain(self):
        here = self.here
        for way in (0, 1):
            for far in range(here.count - 1):
                @pl.when(jnp.logical_and(here.valid(way, far), here.can_send(way)))
                def _():
                    self.z_copy(way, far).wait_send()
        for way, far in [(0, 0)] + here.steps():
            @pl.when(here.valid(way, far))
            def _():
                self.y_copy(way, far, here.row).wait_send()
        if self.spread:
            for way, far, other in self.members():
                @pl.when(here.valid(way, far))
                def _():
                    self.x_copy(way, far, other, here.quarter).wait_send()
                    self.c_copy(way, far, other, 0, here.quarter).wait_send()
                    self.c_copy(way, far, other, 1, here.x_quarter).wait_send()


class Scatter:
    def __init__(self, here, total, height, from_y, from_z, out):
        self.here, self.total, self.height, self.out = here, total, height, out
        self.from_y, self.from_z = from_y, from_z
        count = here.count
        self.y_base = here.take(count)
        self.z_base = here.take(2 * (count - 1))
        self.out_base = here.take(3)

    def block(self, depth, row):
        first = pl.multiple_of((depth * 2 + row) * self.height, self.height)
        return self.total.at[pl.ds(first, self.height), :]

    def y_copy(self, depth):
        here = self.here
        return here.link(self.block(depth, 1 - here.row), self.from_y.at[depth], self.y_base + depth, here.to_y)

    def y_begin(self):
        for depth in range(self.here.count):
            self.y_copy(depth).start()

    def y_phase(self):
        here = self.here
        for depth in range(here.count):
            self.y_copy(depth).wait_recv()
            block = self.block(depth, here.row)
            block[...] = block[...] + self.from_y[depth]

    def z_copy(self, way, far):
        here = self.here
        at = here.depth - far if way == 0 else here.depth + far
        index = self.z_base + way * (here.count - 1) + far - 1
        return here.link(self.block(at, here.row), self.from_z.at[way, far - 1], index, here.next_of(way))

    def z_add(self, way, far):
        here = self.here
        held = self.from_z.at[way, far]
        here.link(held, held, self.z_base + way * (here.count - 1) + far, here.to_y).wait_recv()
        at = here.depth - far if way == 0 else here.depth + far
        block = self.block(at, here.row)
        block[...] = block[...] + held[...]

    def reaches(self, way, far):
        here = self.here
        return here.depth - far >= 0 if way == 0 else here.depth + far <= here.count - 1

    def z_phase(self):
        here = self.here
        for far in range(here.count - 1, 0, -1):
            for way in (0, 1):
                inner = here.depth < here.count - 1 if way == 0 else here.depth > 0

                @pl.when(self.reaches(way, far))
                def _():
                    if far < here.count - 1:
                        @pl.when(inner)
                        def _():
                            self.z_add(way, far)
                    self.z_copy(way, far).start()
        for way in (0, 1):
            @pl.when(here.depth < here.count - 1 if way == 0 else here.depth > 0)
            def _():
                self.z_add(way, 0)
        self.out(here.quarter)[...] = self.block(here.depth, here.row)[...]
        self.out_copy(0).start()
        self.out_copy(1).start()

    def out_copy(self, level, quarter=None):
        here = self.here
        quarter = (here.quarter, here.quarter, here.x_quarter)[level] if quarter is None else quarter
        held = self.out(quarter)
        return here.link(held, held, self.out_base + level, here.to_x if level == 0 else here.to_core)

    def out_phase(self):
        self.out_copy(0, self.here.x_quarter).wait_recv()
        self.out_copy(2).start()

    def finish(self):
        here = self.here
        self.out_copy(1, here.core_quarter).wait_recv()
        self.out_copy(2, here.far_quarter).wait_recv()
        for level in range(3):
            self.out_copy(level).wait_send()
        for depth in range(here.count):
            self.y_copy(depth).wait_send()
        for far in range(1, here.count):
            for way in (0, 1):
                @pl.when(self.reaches(way, far))
                def _():
                    self.z_copy(way, far).wait_send()


class SmallSum:
    def __init__(self, here, held, landing, depth_held):
        self.here, self.held, self.landing, self.depth_held = here, held, landing, depth_held
        self.base = here.take(3 + here.count)
        self.partners = [here.to_core, here.to_x, here.to_y]

    def copy(self, level):
        return self.here.link(self.held.at[level], self.landing.at[level], self.base + level, self.partners[level])

    def z_copy(self, at):
        here = self.here
        held = self.depth_held.at[here.depth]
        return remote(
            held, held, here.sends.at[self.base + 3 + at], here.recvs.at[self.base + 3 + here.depth], here.at_depth(at)
        )

    def begin(self):
        self.copy(0).start()

    def level(self, level):
        here = self.here
        self.copy(level).wait_recv()
        summed = self.held[level] + self.landing[level]
        if level < 2:
            self.held[level + 1] = summed
            self.copy(level + 1).start()
        else:
            self.depth_held[here.depth] = summed
            for at in range(here.count):
                @pl.when(here.depth != at)
                def _():
                    self.z_copy(at).start()

    def finish(self):
        here = self.here
        for at in range(here.count):
            @pl.when(here.depth != at)
            def _():
                held = self.depth_held.at[at]
                here.link(held, held, self.base + 3 + at, here.to_y).wait_recv()
        summed = self.depth_held[0]
        for at in range(1, here.count):
            summed = summed + self.depth_held[at]
        for level in range(3):
            self.copy(level).wait_send()
        for at in range(here.count):
            @pl.when(here.depth != at)
            def _():
                self.z_copy(at).wait_send()
        return summed


class Swap:
    def __init__(self, here, source, target):
        self.here, self.source, self.target = here, source, target
        self.base = here.take(here.count)

    def copy(self, at):
        here = self.here
        return remote(
            self.source(at), self.target(here.depth), here.sends.at[self.base + at],
            here.recvs.at[self.base + here.depth], here.at_depth(at),
        )

    def each(self, step):
        for at in range(self.here.count):
            @pl.when(self.here.depth != at)
            def _():
                step(at)

    def begin(self):
        self.each(lambda at: self.copy(at).start())

    def arrive(self):
        def wait(at):
            held = self.target(at)
            self.here.link(held, held, self.base + at, self.here.to_y).wait_recv()

        self.each(wait)

    def drain(self):
        self.each(lambda at: self.copy(at).wait_send())


class SeqGather:
    def __init__(self, here, held):
        self.here, self.held = here, held
        self.base = here.take(3)

    def copy(self, level, index=None):
        here = self.here
        index = (here.quarter, here.quarter, here.x_quarter)[level] if index is None else index
        held = self.held.at[index]
        return here.link(held, held, self.base + level, here.to_x if level == 0 else here.to_core)

    def begin(self):
        self.copy(0).start()
        self.copy(1).start()

    def relay(self):
        self.copy(0, self.here.x_quarter).wait_recv()
        self.copy(2).start()

    def arrive(self):
        self.copy(1, self.here.core_quarter).wait_recv()
        self.copy(2, self.here.far_quarter).wait_recv()

    def drain(self):
        for level in range(3):
            self.copy(level).wait_send()


class SeqSum:
    def __init__(self, here, held, landing):
        self.here, self.held, self.landing = here, held, landing
        self.base = here.take(3)

    def copy(self, level):
        here = self.here
        index = (here.far_quarter, here.core_quarter, here.x_quarter)[level]
        return here.link(
            self.held.at[index], self.landing.at[level], self.base + level, here.to_x if level == 2 else here.to_core
        )

    def begin(self):
        self.copy(0).start()
        self.copy(1).start()

    def relay(self):
        here = self.here
        self.copy(0).wait_recv()
        self.held[here.x_quarter] = self.held[here.x_quarter] + self.landing[0]
        self.copy(2).start()

    def arrive(self):
        here = self.here
        self.copy(1).wait_recv()
        self.copy(2).wait_recv()
        own = self.held[here.quarter].astype(jnp.float32)
        return own + self.landing[1].astype(jnp.float32) + self.landing[2].astype(jnp.float32)

    def drain(self):
        for level in range(3):
            self.copy(level).wait_send()


class SeqSwap:
    def __init__(self, here, heights, landing):
        self.here, self.heights, self.landing = here, heights, landing
        self.base = here.take(4)

    def held(self, member, source):
        return self.landing.at[source, pl.ds(0, self.heights[member]), :]

    def copy(self, member, block):
        here = self.here
        return remote(
            block, self.held(member, here.seq), here.sends.at[self.base + member], here.recvs.at[self.base + here.seq],
            (member, here.depth, here.row),
        )

    def begin(self, member, block):
        here = self.here

        @pl.when(here.seq != member)
        def _():
            self.copy(member, block).start()

        @pl.when(here.seq == member)
        def _():
            self.held(member, here.seq)[...] = block[...]

    def arrive(self):
        here = self.here
        for member in range(4):
            @pl.when(here.seq == member)
            def _():
                for source in range(4):
                    if source != member:
                        held = self.held(member, source)
                        here.link(held, held, self.base + source, here.to_core).wait_recv()

    def drain(self):
        here = self.here
        for member in range(4):
            @pl.when(here.seq != member)
            def _():
                held = self.held(member, member)
                here.link(held, held, self.base + member, here.to_core).wait_send()


def tiles(total, width, body):
    def step(number, carry):
        body(pl.ds(pl.multiple_of(number * width, width), width))
        return carry

    lax.fori_loop(0, total // width, step, 0)


def times(left, right, left_dim, right_dim):
    return lax.dot_general(
        left, right, (((left_dim,), (right_dim,)), ((), ())), preferred_element_type=jnp.float32
    )


def normed_of(values):
    inverse = lax.rsqrt(jnp.mean(values * values, axis=-1, keepdims=True) + EPSILON)
    return values * inverse, inverse


def norm_back(upstream, values, gain):
    normed, inverse = normed_of(values)
    grad_gain = jnp.sum(upstream * normed, axis=0, keepdims=True)
    grad_normed = upstream * gain
    mean = jnp.mean(grad_normed * normed, axis=-1, keepdims=True)
    return inverse * (grad_normed - normed * mean), grad_gain


BF = jnp.bfloat16
F32 = jnp.float32


class Names:
    pass


def layer_kernel(sizes, names, *refs):
    r = Names()
    for name, ref in zip(names, refs):
        setattr(r, name, ref)
    count, tokens, features, enc, heads, quarter, rows, tall = sizes
    head = features // heads
    mine = heads // count
    width = mine * head
    length = count * tokens
    states = count * enc
    here = Place(count, r.sends, r.recvs)
    seq, depth, row = here.seq, here.depth, here.row

    own = pl.multiple_of((depth * 2 + row) * rows, rows)
    own_tall = pl.multiple_of((depth * 2 + row) * tall, tall)
    squares = [getattr(r, f"square{number}") for number in range(8)]
    local = [
        pltpu.make_async_copy(squares[number], r.weights.at[number, pl.ds(own, rows), :], r.local.at[number])
        for number in range(8)
    ]
    local.append(
        pltpu.make_async_copy(
            r.down.at[pl.ds(pl.multiple_of(seq * tall, tall), tall), :], r.down_quarter.at[pl.ds(own_tall, tall), :],
            r.local.at[8],
        )
    )
    for copy in local:
        copy.start()

    def weight_piece(chunk):
        return lambda at, at_row, quarter_at: r.weights.at[
            4 * chunk + quarter_at, pl.ds(pl.multiple_of((at * 2 + at_row) * rows, rows), rows), :
        ]

    def quarter_piece(whole, height):
        return lambda at, at_row, quarter_at: whole.at[
            pl.ds(pl.multiple_of((at * 2 + at_row) * height, height), height), :
        ]

    gathers = [
        Gather(here, weight_piece(0), True),
        Gather(here, weight_piece(1), True),
        Gather(here, quarter_piece(r.gate_quarter, rows), False),
        Gather(here, quarter_piece(r.linear_quarter, rows), False),
        Gather(here, quarter_piece(r.down_quarter, tall), False),
    ]
    mates = []
    for far in range(count):
        for flip in (0, 1):
            if far or flip:
                mates.append((lax.rem(depth + far, count), row if flip == 0 else 1 - row))
    partners = [(seq,) + mate for mate in mates] + [here.to_x, here.to_core, here.to_far]
    barrier = pltpu.get_barrier_semaphore()
    for partner in partners:
        pl.semaphore_signal(barrier, inc=1, device_id=partner, device_id_type=MESH)
    pl.semaphore_wait(barrier, len(partners))

    gain_base = here.take(2 * count - 1)
    r.all_gains[depth * 2 + row] = r.gains[...]
    gain_sends = [
        here.link(r.all_gains.at[depth * 2 + row], r.all_gains.at[depth * 2 + row], gain_base + number, (seq,) + mate)
        for number, mate in enumerate(mates)
    ]
    for copy in gain_sends:
        copy.start()
    for number in range(4):
        local[number].wait()
    gathers[0].begin()
    for number in range(4, 9):
        local[number].wait()

    r.grads_in[seq] = r.out_grad[...]
    grads_in = SeqGather(here, r.grads_in)
    long = (tokens,) * 3 + (enc,)
    lefts = [SeqSwap(here, long, r.left.at[0]), SeqSwap(here, long[::-1], r.left.at[1])]
    rights = [SeqSwap(here, long, r.right.at[0]), SeqSwap(here, long[::-1], r.right.at[1])]

    for at in range(4):
        @pl.when(seq == at)
        def _():
            for source, whole in ((r.gate, r.gate_quarter), (r.linear, r.linear_quarter)):
                span = 4 * tall
                whole[pl.ds(own, rows), :] = jnp.concatenate(
                    [source[:, number * span + at * tall : number * span + (at + 1) * tall] for number in range(2 * count)],
                    axis=1,
                )

    key_at = lax.broadcasted_iota(jnp.int32, (tokens, length), 0)
    query_at = lax.broadcasted_iota(jnp.int32, (tokens, length), 1)
    for number in range(mine):
        strip = jnp.broadcast_to(r.bias[number : number + 1, :], (tokens, length))
        step = 1
        while step < tokens:
            strip = jnp.where((key_at // step) % 2 == 1, pltpu.roll(strip, step, 1), strip)
            step *= 2
        r.strip[number] = jnp.where(query_at >= key_at, strip, FAR_BELOW)

    gathers[0].z_phase()
    gathers[1].begin()
    gathers[0].y_phase()

    for far in range(count):
        for flip in (0, 1):
            if far or flip:
                source = lax.rem(depth + count - far, count) * 2 + (row if flip == 0 else 1 - row)
                held = r.all_gains.at[source]
                here.link(held, held, gain_base + far * 2 + flip - 1, here.to_core).wait_recv()
    lane = lax.broadcasted_iota(jnp.int32, (LANES, features), 0)
    column = lax.broadcasted_iota(jnp.int32, (LANES, features), 1)
    gain_rows = jnp.zeros((16, features), F32)
    for number in range(2 * count):
        select = jnp.logical_and(column - number * rows == lane, lane < rows)
        gain_rows = gain_rows + times(r.all_gains[number], select.astype(F32).astype(BF), 1, 0)
    r.gain_rows[...] = gain_rows

    def gain(number):
        return r.gain_rows[number : number + 1, :]

    x0 = r.hidden[...].astype(F32)
    h1 = (normed_of(x0)[0] * gain(0)).astype(BF)
    r.h1[...] = h1

    gathers[1].z_phase()
    gathers[0].x_phase()
    gathers[0].finish()

    for number in range(3):
        def project(at, number=number):
            r.qkv_t[number, at, :] = times(r.h1[...], r.weights[number, :, at], 1, 0).astype(BF).T

        tiles(features, 256, project)

    def head_rows(at):
        return pl.ds(pl.multiple_of(at * width, width), width)

    def token_lanes(at):
        return pl.ds(pl.multiple_of(at * tokens, tokens), tokens)

    def own_block(target, source):
        target[...] = source[...]

    qkv = Swap(
        here, lambda at: r.qkv_t.at[:, head_rows(at), :], lambda at: r.qkv_h.at[:, :, token_lanes(at)]
    )
    qkv.begin()
    own_block(r.qkv_h.at[:, :, token_lanes(depth)], r.qkv_t.at[:, head_rows(depth), :])

    gathers[1].y_phase()
    grads_in.begin()
    for chunk in (2, 3, 4):
        gathers[chunk].begin()
    gathers[1].x_phase()
    for chunk in (2, 3, 4):
        gathers[chunk].z_phase(1)
    gathers[1].finish()
    for member in range(3):
        lefts[0].begin(member, r.h1)
    lefts[0].begin(3, r.encoder)
    lefts[1].begin(0, r.encoder)

    for number in range(2):
        def project(at, number=number):
            r.cross_kv[number, pl.ds(pl.multiple_of(depth * enc, enc), enc), at] = times(
                r.encoder[...], r.weights[3 + number, :, at], 1, 0
            ).astype(BF)

        tiles(features, 256, project)

    def enc_rows(at):
        return pl.ds(pl.multiple_of(at * enc, enc), enc)

    own_kv = r.cross_kv.at[:, enc_rows(depth), :]
    cross = Swap(here, lambda at: own_kv, lambda at: r.cross_kv.at[:, enc_rows(at), :])
    cross.begin()

    for chunk in (2, 3, 4):
        gathers[chunk].z_phase(2)
    qkv.arrive()

    def block_scores(number, block):
        keys = (block + 1) * tokens
        at = pl.ds(pl.multiple_of(number * head, head), head)
        query = r.qkv_h[0, at, block * tokens : keys]
        scores = times(r.qkv_h[1, at, :keys], query, 0, 0)
        bias = jnp.concatenate(
            [r.strip[number, :, (block - key) * tokens : (block - key + 1) * tokens] for key in range(block + 1)], axis=0
        )
        return scores + bias, at, keys, query

    def self_forward(number, carry):
        for block in range(count):
            scores, at, keys, _ = block_scores(number, block)
            top = jnp.max(scores, axis=0, keepdims=True)
            weights = jnp.exp(scores - top)
            total = jnp.sum(weights, axis=0, keepdims=True)
            mixed = times(r.qkv_h[2, at, :keys], weights.astype(BF), 1, 0)
            span = slice(block * tokens, keys)
            r.attn_h[at, span] = (mixed / total).astype(BF)
            r.lse[number, :, span] = top + jnp.log(total)
        return carry

    lax.fori_loop(0, mine, self_forward, 0)
    attn = Swap(here, lambda at: r.attn_h.at[:, token_lanes(at)], lambda at: r.attn_t.at[head_rows(at), :])
    attn.begin()
    own_block(r.attn_t.at[head_rows(depth), :], r.attn_h.at[:, token_lanes(depth)])

    for far in range(3, count):
        for chunk in (2, 3, 4):
            gathers[chunk].z_phase(far)
    grads_in.relay()
    cross.arrive()
    for number in range(2):
        r.cross_t[number] = r.cross_kv[number].T
    attn.arrive()
    r.attn[...] = r.attn_t[...].T
    lefts[1].begin(1, r.attn)

    def after(at):
        r.x1[:, at] = r.hidden[:, at].astype(F32) + times(r.attn[...], r.weights[5, :, at], 1, 0)

    tiles(features, 256, after)
    h2 = (normed_of(r.x1[...])[0] * gain(1)).astype(BF)
    r.h2[...] = h2
    lefts[1].begin(2, r.h2)

    def project(at):
        r.cq_t[at, :] = times(r.h2[...], r.weights[6, :, at], 1, 0).astype(BF).T

    tiles(features, 256, project)

    def head_at(number):
        return pl.ds(pl.multiple_of(number * head, head), head)

    def cross_forward(number, carry):
        at = head_at(number)
        scores = times(r.cross_t[0, at, :], r.cq_t[at, :], 0, 0)
        top = jnp.max(scores, axis=0, keepdims=True)
        weights = jnp.exp(scores - top)
        total = jnp.sum(weights, axis=0, keepdims=True)
        mixed = times(r.cross_t[1, at, :], weights.astype(BF), 1, 0)
        r.cattn_t[at, :] = (mixed / total).astype(BF)
        r.clse[number] = top + jnp.log(total)
        return carry

    lax.fori_loop(0, heads, cross_forward, 0)
    r.cattn[...] = r.cattn_t[...].T
    lefts[1].begin(3, r.cattn)

    def after(at):
        r.x2[:, at] = r.x1[:, at] + times(r.cattn[...], r.weights[7, :, at], 1, 0)

    tiles(features, 256, after)
    r.h3[seq] = (normed_of(r.x2[...])[0] * gain(2)).astype(BF)
    h3 = SeqGather(here, r.h3)
    h3.begin()
    gathers[2].y_phase()
    gathers[3].y_phase()
    h3.relay()
    gathers[4].y_phase()
    grads_in.arrive()
    h3.arrive()

    group = 4 * tokens
    hidden_rows = r.h3[...].reshape(group, features)
    grad_rows = r.grads_in[...].reshape(group, features)
    root = math.sqrt(2.0 / math.pi)

    def feed(at):
        gate = times(hidden_rows, r.gate_quarter[:, at], 1, 0)
        linear = times(hidden_rows, r.linear_quarter[:, at], 1, 0)
        grad = times(grad_rows, r.down_quarter[at, :], 1, 1)
        square = gate * gate
        bent = jnp.tanh(root * gate * (1.0 + 0.044715 * square))
        half = 0.5 * (1.0 + bent)
        curve = gate * half
        slope = half + 0.5 * gate * (1.0 - bent * bent) * (root * (1.0 + 3 * 0.044715 * square))
        r.middle[:, at] = (curve * linear).astype(BF)
        r.grad_gate[:, at] = (grad * linear * slope).astype(BF)
        r.grad_linear[:, at] = (grad * curve).astype(BF)

    tiles(quarter, 256, feed)

    def back(at):
        upstream = times(r.grad_gate[...], r.gate_quarter[at, :], 1, 1) + times(
            r.grad_linear[...], r.linear_quarter[at, :], 1, 1
        )
        r.gh3[:, :, at] = upstream.reshape(4, tokens, -1).astype(BF)

    tiles(features, 256, back)
    gh3 = SeqSum(here, r.gh3, r.gh3_in)
    gh3.begin()

    def forth(at):
        r.lout[:, :, at] = times(r.middle[...], r.down_quarter[:, at], 1, 0).reshape(4, tokens, -1).astype(BF)

    tiles(features, 256, forth)
    lout = SeqSum(here, r.lout, r.lout_in)
    gh3.relay()
    lout.begin()

    def down_terms(at):
        r.down_terms[at, :] = times(r.middle[:, at], grad_rows, 0, 0).astype(BF)

    tiles(quarter, 256, down_terms)
    feeds = [
        Scatter(here, r.down_terms, tall, r.down_y, r.down_z, lambda q: r.out_down.at[q]),
        Scatter(here, r.gate_terms, rows, r.gate_y, r.gate_z, lambda q: r.out_gate.at[q]),
        Scatter(here, r.linear_terms, rows, r.linear_y, r.linear_z, lambda q: r.out_linear.at[q]),
    ]
    feeds[0].y_begin()

    def gate_terms(at):
        r.gate_terms[at, :] = times(hidden_of(at), r.grad_gate[...], 0, 0).astype(BF)

    def linear_terms(at):
        r.linear_terms[at, :] = times(hidden_of(at), r.grad_linear[...], 0, 0).astype(BF)

    def hidden_of(at):
        return r.h3[:, :, at].reshape(group, -1)

    tiles(features, 256, gate_terms)
    feeds[1].y_begin()
    lout.relay()
    tiles(features, 256, linear_terms)
    feeds[2].y_begin()

    grad_x2, gain_three = norm_back(gh3.arrive(), r.x2[...], gain(2))
    grad_x2 = r.out_grad[...].astype(F32) + grad_x2
    r.gx[...] = grad_x2
    rounded = grad_x2.astype(BF)
    r.rounded[...] = rounded
    rights[1].begin(3, r.rounded)

    def pull(at):
        r.grad_t[at, :] = times(r.rounded[...], r.weights[7, at, :], 1, 1).astype(BF).T

    tiles(features, 256, pull)

    def cross_backward(number, carry):
        at = head_at(number)
        grad = r.grad_t[at, :]
        delta = jnp.sum(grad.astype(F32) * r.cattn_t[at, :].astype(F32), axis=0, keepdims=True)
        query, keys = r.cq_t[at, :], r.cross_t[0, at, :]
        probs = jnp.exp(times(keys, query, 0, 0) - r.clse[number])
        terms = (probs * (times(r.cross_t[1, at, :], grad, 0, 0) - delta)).astype(BF)
        r.gq_t[at, :] = times(keys, terms, 1, 0).astype(BF)
        r.cross_terms_t[0, at, :] = times(query, terms, 1, 1)
        r.cross_terms_t[1, at, :] = times(grad, probs.astype(BF), 1, 1)
        return carry

    lax.fori_loop(0, heads, cross_backward, 0)
    for number in range(2):
        r.cross_terms[number] = r.cross_terms_t[number].T.astype(BF)
    cross_terms = Swap(here, lambda at: r.cross_terms.at[:, enc_rows(at), :], lambda at: r.cross_in.at[at])
    cross_terms.begin()
    r.cross_in[depth] = r.cross_terms[:, enc_rows(depth), :]
    r.gq[...] = r.gq_t[...].T
    rights[1].begin(2, r.gq)

    spread = [
        Scatter(
            here, r.terms.at[chunk], rows, r.terms_y.at[chunk], r.terms_z.at[chunk],
            lambda q, chunk=chunk: r.out_squares.at[4 * chunk + q],
        )
        for chunk in range(2)
    ]

    def square_terms(chunk):
        lefts[chunk].arrive()
        rights[chunk].arrive()
        heights = lefts[chunk].heights
        short = heights.index(enc)
        for which, height in ((seq != short, tokens), (seq == short, enc)):
            @pl.when(which)
            def _():
                def body(at):
                    left = r.left[chunk, :, :height, at].reshape(4 * height, -1)
                    right = r.right[chunk, :, :height, :].reshape(4 * height, features)
                    r.terms[chunk, at, :] = times(left, right, 0, 0).astype(BF)

                tiles(features, 256, body)

        spread[chunk].y_begin()

    feeds[0].y_phase()
    feeds[0].z_phase()

    def pull(at):
        r.up[:, at] = times(r.gq[...], r.weights[6, at, :], 1, 1)

    tiles(features, 256, pull)
    grad_x1, gain_two = norm_back(r.up[...], r.x1[...], gain(1))
    grad_x1 = r.gx[...] + grad_x1
    r.gx[...] = grad_x1
    r.rounded_one[...] = grad_x1.astype(BF)
    rights[1].begin(1, r.rounded_one)

    def pull(at):
        r.grad_t[at, :] = times(r.rounded_one[...], r.weights[5, at, :], 1, 1).astype(BF).T

    tiles(features, 256, pull)
    grad_attn = Swap(here, lambda at: r.grad_t.at[head_rows(at), :], lambda at: r.grad_h.at[:, token_lanes(at)])
    grad_attn.begin()
    own_block(r.grad_h.at[:, token_lanes(depth)], r.grad_t.at[head_rows(depth), :])

    feeds[1].y_phase()
    feeds[1].z_phase()
    cross_terms.arrive()
    summed = r.cross_in[0].astype(F32)
    for at in range(1, count):
        summed = summed + r.cross_in[at].astype(F32)
    r.cross_sum[...] = summed.astype(BF)
    rights[0].begin(3, r.cross_sum.at[0])
    rights[1].begin(0, r.cross_sum.at[1])
    square_terms(1)
    feeds[2].y_phase()
    feeds[2].z_phase()
    r.layer_out[...] = (r.x2[...] + lout.arrive()).astype(BF)

    def encoder_back(at):
        r.encoder_grad[:, at] = times(r.cross_sum[0], r.weights[3, at, :], 1, 1) + times(
            r.cross_sum[1], r.weights[4, at, :], 1, 1
        )

    tiles(features, 256, encoder_back)
    for work in feeds:
        work.out_phase()

    grad_attn.arrive()

    def self_backward(number, carry):
        at = head_at(number)
        r.dkv[...] = jnp.zeros_like(r.dkv)
        r.strip_sum[...] = jnp.zeros_like(r.strip_sum)
        for block in range(count):
            scores, _, keys, query = block_scores(number, block)
            span = slice(block * tokens, keys)
            grad = r.grad_h[at, span]
            delta = jnp.sum(grad.astype(F32) * r.attn_h[at, span].astype(F32), axis=0, keepdims=True)
            probs = jnp.exp(scores - r.lse[number, :, span])
            grad_scores = probs * (times(r.qkv_h[2, at, :keys], grad, 0, 0) - delta)
            terms = grad_scores.astype(BF)
            r.dqkv_h[0, at, span] = times(r.qkv_h[1, at, :keys], terms, 1, 0).astype(BF)
            r.dkv[0, :, :keys] += times(query, terms, 1, 1)
            r.dkv[1, :, :keys] += times(grad, probs.astype(BF), 1, 1)
            for key in range(block + 1):
                lanes = slice((block - key) * tokens, (block - key + 1) * tokens)
                r.strip_sum[:, lanes] += grad_scores[key * tokens : (key + 1) * tokens, :]
        r.dqkv_h[1, at, :] = r.dkv[0].astype(BF)
        r.dqkv_h[2, at, :] = r.dkv[1].astype(BF)
        strip = r.strip_sum[...]
        step = 1
        while step < tokens:
            strip = jnp.where((key_at // step) % 2 == 1, pltpu.roll(strip, length - step, 1), strip)
            step *= 2
        r.small[0, pl.ds(mine * depth + number, 1), :length] = jnp.sum(strip, axis=0, keepdims=True)
        return carry

    r.small[0] = jnp.zeros(r.small.shape[1:], F32)
    lax.fori_loop(0, mine, self_backward, 0)
    dqkv = Swap(
        here, lambda at: r.dqkv_h.at[:, :, token_lanes(at)], lambda at: r.dqkv_t.at[:, head_rows(at), :]
    )
    dqkv.begin()
    own_block(r.dqkv_t.at[:, head_rows(depth), :], r.dqkv_h.at[:, :, token_lanes(depth)])
    spread[1].y_phase()
    spread[1].z_phase()
    for work in feeds:
        work.finish()
    dqkv.arrive()
    for number in range(3):
        r.dqkv[number] = r.dqkv_t[number].T
        rights[0].begin(number, r.dqkv.at[number])

    def pull(at):
        r.up[:, at] = (
            times(r.dqkv[0], r.weights[0, at, :], 1, 1)
            + times(r.dqkv[1], r.weights[1, at, :], 1, 1)
            + times(r.dqkv[2], r.weights[2, at, :], 1, 1)
        )

    tiles(features, 256, pull)
    grad_x0, gain_one = norm_back(r.up[...], r.hidden[...].astype(F32), gain(0))
    r.input_grad[...] = r.gx[...] + grad_x0
    for number, value in enumerate((gain_one, gain_two, gain_three)):
        r.small[0, heads + number : heads + number + 1, :] = value
    small = SmallSum(here, r.small, r.small_in, r.small_depth)
    small.begin()
    spread[1].out_phase()
    square_terms(0)
    small.level(0)
    small.level(1)
    small.level(2)
    spread[0].y_phase()
    spread[0].z_phase()
    r.small_out[...] = small.finish()
    for work in gathers:
        work.drain()
    for copy in gain_sends:
        copy.wait_send()
    for work in (*lefts, *rights, qkv, attn, cross, cross_terms, grad_attn, dqkv, h3, grads_in, gh3, lout):
        work.drain()
    spread[0].out_phase()
    spread[1].finish()
    spread[0].finish()
    for source, whole in ((r.out_gate, r.whole_gate), (r.out_linear, r.whole_linear)):
        held = [source[at] for at in range(4)]
        whole[...] = jnp.concatenate(
            [held[at][:, number * tall : (number + 1) * tall] for number in range(2 * count) for at in range(4)], axis=1
        )


def run_layer(hidden, encoder, out_grad, bias, squares, gate, linear, down, gains):
    count = lax.axis_size("ctx")
    tokens, features = hidden.shape
    enc = encoder.shape[0]
    rows, hidden_units = gate.shape
    heads = features // 64
    quarter = hidden_units // 4
    tall = down.shape[0] // 4
    length, states = count * tokens, count * enc
    mine = heads // count
    width = features // count
    head = features // heads
    small = (-(-(heads + 3) // 8) * 8, features)
    used = 96 * count
    vmem = pl.BlockSpec(memory_space=pltpu.VMEM)
    held = pl.BlockSpec(memory_space=pl.ANY)
    inputs = dict(
        hidden=(hidden, vmem),
        encoder=(encoder, vmem),
        out_grad=(out_grad, vmem),
        bias=(bias, vmem),
        **{f"square{number}": (member, held) for number, member in enumerate(squares)},
        gate=(gate, vmem),
        linear=(linear, vmem),
        down=(down, held),
        gains=(gains, vmem),
    )
    outputs = dict(
        layer_out=((tokens, features), BF),
        input_grad=((tokens, features), F32),
        encoder_grad=((enc, features), F32),
        small_out=(small, F32),
        out_squares=((8, rows, features), BF),
        out_down=((4, tall, features), BF),
        whole_gate=((rows, hidden_units), BF),
        whole_linear=((rows, hidden_units), BF),
    )
    square = (features, features)
    near = (2, count - 1)
    scratch = dict(
        weights=((8,) + square, BF),
        gate_quarter=((features, quarter), BF),
        linear_quarter=((features, quarter), BF),
        down_quarter=((quarter, features), BF),
        all_gains=((2 * count,) + gains.shape, BF),
        gain_rows=((16, features), F32),
        strip=((mine, tokens, length), F32),
        strip_sum=((tokens, length), F32),
        h1=((tokens, features), BF),
        h2=((tokens, features), BF),
        qkv_t=((3, features, tokens), BF),
        qkv_h=((3, width, length), BF),
        attn_h=((width, length), BF),
        attn_t=((features, tokens), BF),
        attn=((tokens, features), BF),
        lse=((mine, 1, length), F32),
        cross_kv=((2, states, features), BF),
        cross_t=((2, features, states), BF),
        cq_t=((features, tokens), BF),
        cattn_t=((features, tokens), BF),
        clse=((heads, 1, tokens), F32),
        x1=((tokens, features), F32),
        x2=((tokens, features), F32),
        gx=((tokens, features), F32),
        up=((tokens, features), F32),
        rounded=((tokens, features), BF),
        h3=((4, tokens, features), BF),
        grads_in=((4, tokens, features), BF),
        middle=((4 * tokens, quarter), BF),
        grad_gate=((4 * tokens, quarter), BF),
        grad_linear=((4 * tokens, quarter), BF),
        gh3=((4, tokens, features), BF),
        gh3_in=((3, tokens, features), BF),
        lout=((4, tokens, features), BF),
        lout_in=((3, tokens, features), BF),
        down_terms=((quarter, features), BF),
        gate_terms=((features, quarter), BF),
        linear_terms=((features, quarter), BF),
        down_y=((count, tall, features), BF),
        gate_y=((count, rows, quarter), BF),
        linear_y=((count, rows, quarter), BF),
        down_z=(near + (tall, features), BF),
        gate_z=(near + (rows, quarter), BF),
        linear_z=(near + (rows, quarter), BF),
        out_gate=((4, rows, quarter), BF),
        out_linear=((4, rows, quarter), BF),
        grad_t=((features, tokens), BF),
        gq_t=((features, tokens), BF),
        gq=((tokens, features), BF),
        cross_terms_t=((2, features, states), F32),
        cross_terms=((2, states, features), BF),
        cross_in=((count, 2, enc, features), BF),
        cross_sum=((2, enc, features), BF),
        terms=((2,) + square, BF),
        left=((2, 4, tokens, features), BF),
        right=((2, 4, tokens, features), BF),
        rounded_one=((tokens, features), BF),
        cattn=((tokens, features), BF),
        terms_y=((2, count, rows, features), BF),
        terms_z=((2,) + near + (rows, features), BF),
        grad_h=((width, length), BF),
        dkv=((2, head, length), F32),
        dqkv_h=((3, width, length), BF),
        dqkv_t=((3, features, tokens), BF),
        dqkv=((3, tokens, features), BF),
        small=((3,) + small, F32),
        small_in=((3,) + small, F32),
        small_depth=((count,) + small, F32),
    )
    names = list(inputs) + list(outputs) + list(scratch) + ["local", "sends", "recvs"]
    return pl.pallas_call(
        partial(layer_kernel, (count, tokens, features, enc, heads, quarter, rows, tall), names),
        out_shape=tuple(jax.ShapeDtypeStruct(shape, kind) for shape, kind in outputs.values()),
        in_specs=[spec for _, spec in inputs.values()],
        out_specs=[vmem] * len(outputs),
        scratch_shapes=[
            *(pltpu.VMEM(shape, kind) for shape, kind in scratch.values()),
            pltpu.SemaphoreType.DMA((9,)),
            pltpu.SemaphoreType.DMA((used,)),
            pltpu.SemaphoreType.DMA((used,)),
        ],
        compiler_params=pltpu.CompilerParams(
            collective_id=0, has_side_effects=True, vmem_limit_bytes=60 << 20
        ),
        cost_estimate=pl.CostEstimate(flops=8 * 10**9, bytes_accessed=10**7, transcendentals=10**6),
        name="layer",
    )(*(member for member, _ in inputs.values()))


def per_device_whole(
    hidden_in,
    encoder_states,
    out_grad,
    bucket_index,
    bias_table,
    self_gain,
    self_query,
    self_key,
    self_value,
    self_output,
    cross_gain,
    cross_query,
    cross_key,
    cross_value,
    cross_output,
    feed_gain,
    gate_weight,
    linear_weight,
    down_weight,
):
    count = lax.axis_size("ctx")
    rows, features = self_query.shape
    buckets, heads = bias_table.shape
    length = bucket_index.shape[0]
    mine = heads // count
    onehot = (bucket_index[:, None] == jnp.arange(buckets, dtype=jnp.int32)[None, :]).astype(jnp.float32)
    own_table = lax.dynamic_slice_in_dim(bias_table, lax.axis_index("ctx") * mine, mine, 1)
    own_table = jnp.pad(own_table, ((0, 0), (0, -mine % 8)))
    bias = jnp.dot(onehot, own_table, precision=HIGHEST).T
    gains = jnp.pad(jnp.stack([self_gain, cross_gain, feed_gain]), ((0, 13), (0, LANES - rows)))
    layer_out, input_grad, encoder_grad, small, squares, down, gate, linear = run_layer(
        hidden_in[0],
        encoder_states[0],
        out_grad[0],
        bias,
        (self_query, self_key, self_value, cross_key, cross_value, self_output, cross_query, cross_output),
        gate_weight,
        linear_weight,
        down_weight,
        gains,
    )
    grad_table = jnp.dot(onehot.T, small[:heads, :length].T, precision=HIGHEST)
    shard = lax.axis_index(("ctx", "fsdp"))
    gain_sums = lax.dynamic_slice_in_dim(small[heads : heads + 3], shard * rows, rows, 1)
    squares = squares.astype(jnp.float32)
    return (
        layer_out[None],
        input_grad[None],
        encoder_grad[None],
        grad_table,
        gain_sums[0],
        squares[0],
        squares[1],
        squares[2],
        squares[5],
        gain_sums[1],
        squares[6],
        squares[3],
        squares[4],
        squares[7],
        gain_sums[2],
        gate.astype(jnp.float32),
        linear.astype(jnp.float32),
        down.reshape(-1, features).astype(jnp.float32),
    )


def fits(mesh):
    return mesh.shape["seq"] == 4 and mesh.shape["fsdp"] == 2 and mesh.shape["ctx"] <= 4


def solution(mesh):
    return jax.shard_map(
        per_device_whole if fits(mesh) else per_device,
        mesh=mesh,
        in_specs=(
            P(("seq", "fsdp"), "ctx", None),
            P(("seq", "fsdp"), "ctx", None),
            P(("seq", "fsdp"), "ctx", None),
            P(),
            P(),
            P(("ctx", "fsdp")),
            P(("ctx", "fsdp"), None),
            P(("ctx", "fsdp"), None),
            P(("ctx", "fsdp"), None),
            P(("ctx", "fsdp"), None),
            P(("ctx", "fsdp")),
            P(("ctx", "fsdp"), None),
            P(("ctx", "fsdp"), None),
            P(("ctx", "fsdp"), None),
            P(("ctx", "fsdp"), None),
            P(("ctx", "fsdp")),
            P(("ctx", "fsdp"), None),
            P(("ctx", "fsdp"), None),
            P(("ctx", "fsdp"), None),
        ),
        out_specs=(
            P(("seq", "fsdp"), "ctx", None),
            P(("seq", "fsdp"), "ctx", None),
            P(("seq", "fsdp"), "ctx", None),
            P(),
            P(("ctx", "fsdp")),
            P(("ctx", "fsdp"), None),
            P(("ctx", "fsdp"), None),
            P(("ctx", "fsdp"), None),
            P(("ctx", "fsdp"), None),
            P(("ctx", "fsdp")),
            P(("ctx", "fsdp"), None),
            P(("ctx", "fsdp"), None),
            P(("ctx", "fsdp"), None),
            P(("ctx", "fsdp"), None),
            P(("ctx", "fsdp")),
            P(("ctx", "fsdp"), None),
            P(("ctx", "fsdp"), None),
            P(("ctx", "fsdp"), None),
        ),
        check_vma=False,
    )
```

```python
from functools import partial
import math

import jax
import jax.numpy as jnp
from jax import lax
from jax.experimental import pallas as pl
from jax.experimental.pallas import tpu as pltpu
from jax.sharding import PartitionSpec as P

EPSILON = 1e-06
NEGATIVE = -1e30
HIGHEST = lax.Precision.HIGHEST


LANES = 128


def fold_rows(rows, height):
    count = -(-rows.shape[-2] // height)
    short = count * height - rows.shape[-2]
    padding = [(0, 0)] * (rows.ndim - 2) + [(0, short), (0, 0)]
    padded = jnp.pad(rows, padding)
    return jnp.concatenate(
        [padded[..., number * height : (number + 1) * height, :] for number in range(count)],
        axis=-1,
    )


def unfold_rows(columns, row_count, features):
    count = columns.shape[-1] // features
    stacked = jnp.concatenate(
        [columns[..., number * features : (number + 1) * features] for number in range(count)],
        axis=-2,
    )
    return stacked[..., :row_count, :]


def gain_columns(gains, dtype):
    columns = jnp.stack([member.astype(dtype) for member in gains], axis=1)
    return jnp.pad(columns, ((0, 0), (0, LANES - columns.shape[1])))


def product(left, right):
    return jnp.dot(left, right, preferred_element_type=jnp.float32)


def row_contract(left, right):
    return lax.dot_general(
        left, right, (((0,), (0,)), ((), ())), preferred_element_type=jnp.float32
    )


def col_contract(left, right):
    return lax.dot_general(
        left, right, (((1,), (1,)), ((), ())), preferred_element_type=jnp.float32
    )


def norm_forward(values, gain):
    inverse = lax.rsqrt(jnp.mean(values * values, axis=-1, keepdims=True) + EPSILON)
    normed = values * inverse
    return ((normed * gain.astype(jnp.float32)).astype(jnp.bfloat16), normed, inverse)


def norm_backward(upstream, normed, inverse, gain):
    grad_gain = jnp.sum(upstream * normed, axis=0)
    grad_normed = upstream * gain.astype(jnp.float32)
    grad_values = inverse * (
        grad_normed - normed * jnp.mean(grad_normed * normed, axis=-1, keepdims=True)
    )
    return (grad_values, grad_gain)


def geglu(gate_pre, linear_pre):
    return jax.nn.gelu(gate_pre, approximate=True) * linear_pre


def by_heads(values, head_count):
    return values.reshape(values.shape[0], head_count, values.shape[1] // head_count)


def band_onehot(bucket_rev, buckets, query_rows, key_rows, query_first, key_first):
    length = bucket_rev.shape[0] // 2
    offset_first = query_first - key_first
    upper_band = lax.dynamic_slice_in_dim(bucket_rev, length - 1 - offset_first, key_rows, 0)
    lower_band = lax.dynamic_slice_in_dim(
        bucket_rev, length - offset_first - query_rows, query_rows - 1, 0
    )
    slots = jnp.concatenate([upper_band, jnp.full((1,), -1, jnp.int32), lower_band])
    return (slots[:, None] == jnp.arange(buckets, dtype=jnp.int32)[None, :]).astype(jnp.float32)


def spread_band(band, query_rows, key_rows):
    head_count, width = band.shape
    tiled = jnp.broadcast_to(band[:, None, :], (head_count, query_rows, width)).reshape(
        head_count, query_rows * width
    )
    return tiled[:, : query_rows * (width - 1)].reshape(head_count, query_rows, width - 1)[
        :, :, :key_rows
    ]


def fold_band(grad_scores, width):
    head_count, query_rows, key_rows = grad_scores.shape
    padded = jnp.pad(grad_scores, ((0, 0), (0, 0), (0, width - 1 - key_rows))).reshape(
        head_count, query_rows * (width - 1)
    )
    padded = jnp.pad(padded, ((0, 0), (0, query_rows)))
    return jnp.sum(padded.reshape(head_count, query_rows, width), axis=1)


def self_scores(query, key_block, query_first, key_first, bucket_rev, bias_table):
    head_count = bias_table.shape[1]
    query_rows = query.shape[0]
    key_rows = key_block.shape[0]
    scores = jnp.einsum(
        "qhe,khe->hqk",
        by_heads(query, head_count),
        by_heads(key_block, head_count),
        preferred_element_type=jnp.float32,
    )
    offset = (query_first + jnp.arange(query_rows, dtype=jnp.int32))[:, None] - (
        key_first + jnp.arange(key_rows, dtype=jnp.int32)
    )[None, :]
    allowed = offset >= 0
    onehot = band_onehot(
        bucket_rev, bias_table.shape[0], query_rows, key_rows, query_first, key_first
    )
    band = jnp.dot(onehot, bias_table, precision=HIGHEST).T
    scores = jnp.where(allowed[None], scores + spread_band(band, query_rows, key_rows), NEGATIVE)
    return (scores, allowed, onehot)


def table_terms(grad_scores, onehot):
    band_grad = fold_band(grad_scores, onehot.shape[0])
    return jnp.dot(onehot.T, band_grad.T, precision=HIGHEST)


def fold_blocks(block_step, running, arrays, first_row):
    piece_rows = arrays[0].shape[0]
    block_size = math.gcd(piece_rows, 512) if piece_rows > 512 else piece_rows
    if block_size == piece_rows:
        return block_step(running, arrays, first_row)
    block_count = piece_rows // block_size
    stacked = tuple(
        (member.reshape((block_count, block_size) + member.shape[1:]) for member in arrays)
    )

    def scan_block(state_now, scanned):
        number, blocks = scanned
        return (block_step(state_now, blocks, first_row + number * block_size), None)

    result, _ = lax.scan(scan_block, running, (jnp.arange(block_count, dtype=jnp.int32), stacked))
    return result


def forward_step(running, blocks, key_first, query, query_first, bucket_rev, bias_table):
    top, total, mixed = running
    key_block, value_block = blocks
    head_count = bias_table.shape[1]
    scores, allowed, _ = self_scores(
        query, key_block, query_first, key_first, bucket_rev, bias_table
    )
    new_top = jnp.maximum(top, jnp.max(scores, axis=-1))
    weights = jnp.where(allowed[None], jnp.exp(scores - new_top[:, :, None]), 0.0)
    rescale = jnp.exp(top - new_top)
    total = total * rescale + jnp.sum(weights, axis=-1)
    update = jnp.einsum(
        "hqk,khe->qhe",
        weights.astype(jnp.bfloat16),
        by_heads(value_block, head_count),
        preferred_element_type=jnp.float32,
    )
    mixed = mixed * rescale.T[:, :, None] + update
    return (new_top, total, mixed)


def backward_core(
    query,
    grad_attn,
    lse_rows,
    delta_rows,
    key_block,
    value_block,
    query_first,
    key_first,
    bucket_rev,
    bias_table,
):
    head_count = bias_table.shape[1]
    scores, allowed, onehot = self_scores(
        query, key_block, query_first, key_first, bucket_rev, bias_table
    )
    probs = jnp.where(allowed[None], jnp.exp(scores - lse_rows.T[:, :, None]), 0.0)
    grad_probs = jnp.einsum(
        "qhe,khe->hqk",
        by_heads(grad_attn, head_count),
        by_heads(value_block, head_count),
        preferred_element_type=jnp.float32,
    )
    grad_scores = probs * (grad_probs - delta_rows.T[:, :, None])
    return (probs, grad_scores, onehot)


def partial_step(
    running,
    blocks,
    key_first,
    query,
    grad_attn,
    lse_rows,
    delta_rows,
    query_first,
    bucket_rev,
    bias_table,
):
    grad_query, grad_keys, grad_values, table_part = running
    key_block, value_block = blocks
    head_count = bias_table.shape[1]
    probs, grad_scores, onehot = backward_core(
        query,
        grad_attn,
        lse_rows,
        delta_rows,
        key_block,
        value_block,
        query_first,
        key_first,
        bucket_rev,
        bias_table,
    )
    rounded = grad_scores.astype(jnp.bfloat16)
    grad_query = grad_query + jnp.einsum(
        "hqk,khe->qhe", rounded, by_heads(key_block, head_count), preferred_element_type=jnp.float32
    )
    key_part = jnp.einsum(
        "hqk,qhe->khe", rounded, by_heads(query, head_count), preferred_element_type=jnp.float32
    ).reshape(key_block.shape[0], -1)
    value_part = jnp.einsum(
        "hqk,qhe->khe",
        probs.astype(jnp.bfloat16),
        by_heads(grad_attn, head_count),
        preferred_element_type=jnp.float32,
    ).reshape(key_block.shape[0], -1)
    grad_keys = lax.dynamic_update_slice_in_dim(grad_keys, key_part, key_first, 0)
    grad_values = lax.dynamic_update_slice_in_dim(grad_values, value_part, key_first, 0)
    table_part = table_part + table_terms(grad_scores, onehot)
    return (grad_query, grad_keys, grad_values, table_part)


def plain_forward(query, keys, values, head_count):
    scores = jnp.einsum(
        "qhe,khe->hqk",
        by_heads(query, head_count),
        by_heads(keys, head_count),
        preferred_element_type=jnp.float32,
    )
    top = jnp.max(scores, axis=-1, keepdims=True)
    weights = jnp.exp(scores - top)
    total = jnp.sum(weights, axis=-1, keepdims=True)
    mixed = jnp.einsum(
        "hqk,khe->qhe",
        weights.astype(jnp.bfloat16),
        by_heads(values, head_count),
        preferred_element_type=jnp.float32,
    )
    result = (
        (mixed / jnp.transpose(total, (1, 0, 2))).reshape(query.shape[0], -1).astype(jnp.bfloat16)
    )
    return (result, (top + jnp.log(total))[:, :, 0])


def plain_backward(query, keys, values, lse, output, grad_output, head_count):
    split_grad = by_heads(grad_output, head_count)
    delta = jnp.sum(
        split_grad.astype(jnp.float32) * by_heads(output, head_count).astype(jnp.float32), axis=-1
    ).T
    scores = jnp.einsum(
        "qhe,khe->hqk",
        by_heads(query, head_count),
        by_heads(keys, head_count),
        preferred_element_type=jnp.float32,
    )
    probs = jnp.exp(scores - lse[:, :, None])
    grad_probs = jnp.einsum(
        "qhe,khe->hqk", split_grad, by_heads(values, head_count), preferred_element_type=jnp.float32
    )
    rounded = (probs * (grad_probs - delta[:, :, None])).astype(jnp.bfloat16)
    grad_query = jnp.einsum(
        "hqk,khe->qhe", rounded, by_heads(keys, head_count), preferred_element_type=jnp.float32
    ).reshape(query.shape[0], -1)
    grad_keys = jnp.einsum(
        "hqk,qhe->khe", rounded, by_heads(query, head_count), preferred_element_type=jnp.float32
    ).reshape(keys.shape[0], -1)
    grad_values = jnp.einsum(
        "hqk,qhe->khe", probs.astype(jnp.bfloat16), split_grad, preferred_element_type=jnp.float32
    ).reshape(keys.shape[0], -1)
    return (grad_query, grad_keys, grad_values)


def reduce_terms(terms, table_terms):
    groups = lax.axis_size("seq")
    share = terms.shape[1] // groups
    stacked = jnp.stack(
        [terms[:, number * share : (number + 1) * share] for number in range(groups)]
    )
    part = lax.psum_scatter(stacked, "seq", scatter_dimension=0, tiled=False)
    table = lax.psum(table_terms, ("seq", "ctx", "fsdp"))
    part, table = lax.optimization_barrier((part, table))
    part = lax.psum_scatter(part, ("ctx", "fsdp"), scatter_dimension=0, tiled=True)
    return join_columns(lax.all_gather(part, "seq", axis=0, tiled=False)), table


def join_columns(stacked):
    return jnp.concatenate([stacked[number] for number in range(stacked.shape[0])], axis=1)


def gather_pack(pack):
    share = pack.shape[1] // lax.axis_size("seq")
    own = lax.dynamic_slice_in_dim(pack, lax.axis_index("seq") * share, share, 1)
    rows = lax.all_gather(own, ("ctx", "fsdp"), axis=0, tiled=True)
    return join_columns(lax.all_gather(rows, "seq", axis=0, tiled=False))


def even_columns(members):
    joined = jnp.concatenate(members, axis=1)
    return jnp.pad(joined, ((0, 0), (0, -joined.shape[1] % (LANES * lax.axis_size("seq")))))


def per_device(
    hidden_in,
    encoder_states,
    out_grad,
    bucket_index,
    bias_table,
    self_gain,
    self_query,
    self_key,
    self_value,
    self_output,
    cross_gain,
    cross_query,
    cross_key,
    cross_value,
    cross_output,
    feed_gain,
    gate_weight,
    linear_weight,
    down_weight,
):
    shards = lax.axis_size(("ctx", "fsdp"))
    features = self_query.shape[1]
    hidden = gate_weight.shape[1]
    pack = even_columns(
        [
            self_query,
            self_key,
            self_value,
            self_output,
            cross_query,
            cross_key,
            cross_value,
            cross_output,
            gate_weight,
            linear_weight,
            fold_rows(down_weight, self_query.shape[0]),
            gain_columns((self_gain, cross_gain, feed_gain), jnp.bfloat16),
        ]
    )
    pack = gather_pack(pack)
    (
        self_query,
        self_key,
        self_value,
        self_output,
        cross_query,
        cross_key,
        cross_value,
        cross_output,
    ) = (pack[:, number * features : (number + 1) * features] for number in range(8))
    first = 8 * features
    gate_weight = pack[:, first : first + hidden]
    linear_weight = pack[:, first + hidden : first + 2 * hidden]
    first = first + 2 * hidden
    width = -(-(hidden // shards) // (features // shards)) * features
    down_weight = unfold_rows(
        pack[:, first : first + width].reshape(shards, -1, width), hidden // shards, features
    ).reshape(hidden, features)
    gains = pack[:, first + width : first + width + LANES].T
    self_gain, cross_gain, feed_gain = gains[0], gains[1], gains[2]
    tokens = hidden_in.shape[1]
    length = bucket_index.shape[0]
    head_count = bias_table.shape[1]
    buckets = bias_table.shape[0]
    query_first = lax.axis_index("ctx") * tokens
    bucket_rev = jnp.flip(jnp.concatenate([jnp.full((length,), -1, jnp.int32), bucket_index]))
    start_x = hidden_in[0].astype(jnp.float32)
    norm_one, normed_one, inverse_one = norm_forward(start_x, self_gain)
    projected = product(norm_one, pack[:, : 3 * features]).astype(jnp.bfloat16)
    query = projected[:, :features]
    encoder_local = encoder_states[0]
    cross_local = product(encoder_local, pack[:, 5 * features : 7 * features]).astype(jnp.bfloat16)
    encoder_rows = encoder_local.shape[0]
    blocks = lax.all_gather(
        jnp.concatenate([projected[:, features:], cross_local], axis=0), "ctx", axis=0, tiled=False
    )
    both = blocks[:, :tokens].reshape(length, 2 * features)
    keys, values = both[:, :features], both[:, features:]
    both = blocks[:, tokens:].reshape(-1, 2 * features)
    cross_keys, cross_values = both[:, :features], both[:, features:]
    empty_top = jnp.full((head_count, tokens), NEGATIVE, jnp.float32)
    empty_total = jnp.zeros((head_count, tokens), jnp.float32)
    empty_mixed = jnp.zeros((tokens, head_count, query.shape[1] // head_count), jnp.float32)
    forward_bound = partial(
        forward_step,
        query=query,
        query_first=query_first,
        bucket_rev=bucket_rev,
        bias_table=bias_table,
    )
    top, total, mixed = fold_blocks(
        forward_bound,
        (empty_top, empty_total, empty_mixed),
        (keys, values),
        jnp.int32(0),
    )
    attn = (mixed / total.T[:, :, None]).reshape(tokens, -1).astype(jnp.bfloat16)
    self_lse = (top + jnp.log(total)).T
    after_self = start_x + product(attn, self_output)
    norm_two, normed_two, inverse_two = norm_forward(after_self, cross_gain)
    cross_q = product(norm_two, cross_query).astype(jnp.bfloat16)
    cattn, cross_lse = plain_forward(cross_q, cross_keys, cross_values, head_count)
    after_cross = after_self + product(cattn, cross_output)
    norm_three, normed_three, inverse_three = norm_forward(after_cross, feed_gain)
    gate_pre = product(norm_three, gate_weight)
    linear_pre = product(norm_three, linear_weight)
    middle = geglu(gate_pre, linear_pre).astype(jnp.bfloat16)
    layer_out = (after_cross + product(middle, down_weight)).astype(jnp.bfloat16)
    grad_top = out_grad[0]
    grad_down = row_contract(middle, grad_top)
    grad_middle = col_contract(grad_top, down_weight)
    _, pull_back = jax.vjp(geglu, gate_pre, linear_pre)
    grad_gate_pre, grad_linear_pre = pull_back(grad_middle)
    gate_round = grad_gate_pre.astype(jnp.bfloat16)
    linear_round = grad_linear_pre.astype(jnp.bfloat16)
    grad_gate = row_contract(norm_three, gate_round)
    grad_linear = row_contract(norm_three, linear_round)
    back_three, grad_feed_gain = norm_backward(
        col_contract(gate_round, gate_weight) + col_contract(linear_round, linear_weight),
        normed_three,
        inverse_three,
        feed_gain,
    )
    grad_after_cross = grad_top.astype(jnp.float32) + back_three
    cross_round = grad_after_cross.astype(jnp.bfloat16)
    grad_cross_output = row_contract(cattn, cross_round)
    grad_cattn = col_contract(cross_round, cross_output).astype(jnp.bfloat16)
    grad_cq, cross_key_terms, cross_value_terms = plain_backward(
        cross_q, cross_keys, cross_values, cross_lse, cattn, grad_cattn, head_count
    )
    grad_cq = grad_cq.astype(jnp.bfloat16)
    grad_cross_query = row_contract(norm_two, grad_cq)
    back_two, grad_cross_gain = norm_backward(
        col_contract(grad_cq, cross_query), normed_two, inverse_two, cross_gain
    )
    grad_after_self = grad_after_cross + back_two
    self_round = grad_after_self.astype(jnp.bfloat16)
    grad_self_output = row_contract(attn, self_round)
    grad_attn = col_contract(self_round, self_output).astype(jnp.bfloat16)
    delta_rows = jnp.sum(
        by_heads(grad_attn, head_count).astype(jnp.float32)
        * by_heads(attn, head_count).astype(jnp.float32),
        axis=-1,
    )
    empty_rows = jnp.zeros((tokens, query.shape[1]), jnp.float32)
    empty_table = jnp.zeros((buckets, head_count), jnp.float32)
    partial_bound = partial(
        partial_step,
        query=query,
        grad_attn=grad_attn,
        lse_rows=self_lse,
        delta_rows=delta_rows,
        query_first=query_first,
        bucket_rev=bucket_rev,
        bias_table=bias_table,
    )
    empty_whole = jnp.zeros((length, query.shape[1]), jnp.float32)
    grad_query, key_terms, value_terms, table_part = fold_blocks(
        partial_bound,
        (empty_rows.reshape(tokens, head_count, -1), empty_whole, empty_whole, empty_table),
        (keys, values),
        jnp.int32(0),
    )
    terms = jnp.concatenate(
        [
            jnp.concatenate([key_terms, value_terms], axis=1).reshape(-1, tokens, 2 * features),
            jnp.concatenate([cross_key_terms, cross_value_terms], axis=1).reshape(
                -1, encoder_rows, 2 * features
            ),
        ],
        axis=1,
    ).astype(jnp.bfloat16)
    sums = lax.psum_scatter(terms, "ctx", scatter_dimension=0, tiled=False)
    cross_both = sums[tokens:]
    grad_cross_both = row_contract(encoder_local, cross_both)
    grad_cross_key, grad_cross_value = (
        grad_cross_both[:, :features],
        grad_cross_both[:, features:],
    )
    encoder_grad = col_contract(cross_both, pack[:, 5 * features : 7 * features])
    grad_q = grad_query.reshape(tokens, -1).astype(jnp.bfloat16)
    grad_projected = jnp.concatenate([grad_q, sums[:tokens]], axis=1)
    grad_self_projections = row_contract(norm_one, grad_projected)
    upstream_one = col_contract(grad_projected, pack[:, : 3 * features])
    back_one, grad_self_gain = norm_backward(upstream_one, normed_one, inverse_one, self_gain)
    input_grad = grad_after_self + back_one
    folded = fold_rows(grad_down.reshape(shards, -1, features), features // shards)
    parts = [
        grad_self_projections,
        grad_self_output,
        grad_cross_query,
        grad_cross_both,
        grad_cross_output,
        grad_gate,
        grad_linear,
        folded.reshape(features, width),
        gain_columns((grad_self_gain, grad_cross_gain, grad_feed_gain), jnp.bfloat16),
    ]
    terms = even_columns([member.astype(jnp.bfloat16) for member in parts])
    summed, grad_table = reduce_terms(terms, table_part)
    summed = summed.astype(jnp.float32)
    squares = [summed[:, number * features : (number + 1) * features] for number in range(8)]
    first = 8 * features
    down_first = first + 2 * hidden
    gain_first = down_first + width
    return (
        layer_out[None],
        input_grad[None],
        encoder_grad[None],
        grad_table,
        summed[:, gain_first],
        squares[0],
        squares[1],
        squares[2],
        squares[3],
        summed[:, gain_first + 1],
        squares[4],
        squares[5],
        squares[6],
        squares[7],
        summed[:, gain_first + 2],
        summed[:, first : first + hidden],
        summed[:, first + hidden : down_first],
        unfold_rows(summed[:, down_first:gain_first], hidden // shards, features),
    )


MESH = pl.DeviceIdType.MESH
FAR_BELOW = -1e30


def remote(source, target, send_sem, recv_sem, device):
    return pltpu.make_async_remote_copy(
        src_ref=source,
        dst_ref=target,
        send_sem=send_sem,
        recv_sem=recv_sem,
        device_id=device,
        device_id_type=MESH,
    )


class Place:
    def __init__(self, count, sends, recvs):
        self.count, self.sends, self.recvs = count, sends, recvs
        self.seq = lax.axis_index("seq")
        self.side, self.core = self.seq // 2, self.seq % 2
        self.depth, self.row = lax.axis_index("ctx"), lax.axis_index("fsdp")
        self.quarter = self.seq
        self.to_x = self.at(1 - self.side, self.core, self.depth, self.row)
        self.to_y = self.at(self.side, self.core, self.depth, 1 - self.row)
        self.to_core = self.at(self.side, 1 - self.core, self.depth, self.row)
        self.to_far = self.at(1 - self.side, 1 - self.core, self.depth, self.row)
        self.x_quarter = 2 * (1 - self.side) + self.core
        self.core_quarter = 2 * self.side + 1 - self.core
        self.far_quarter = 2 * (1 - self.side) + 1 - self.core
        self.used = 0

    def at(self, side, core, depth, row):
        return (side * 2 + core, depth, row)

    def at_depth(self, depth):
        return (self.seq, depth, self.row)

    def take(self, number):
        first = self.used
        self.used += number
        return first

    def link(self, source, target, index, device):
        return remote(source, target, self.sends.at[index], self.recvs.at[index], device)

    def others(self, step):
        middle = self.count // 2
        for at in sorted(range(self.count), key=lambda at: abs(2 * at - self.count + 1) + (at < middle) * 0.5):
            @pl.when(self.depth != at)
            def _():
                step(at)


class Gather:
    def __init__(self, here, piece, spread):
        self.here, self.piece, self.spread = here, piece, spread
        count = here.count
        self.z_base = here.take(count)
        self.y_base = here.take(count)
        if spread:
            self.x_base = here.take(2 * count)
            self.c_base = here.take(4 * count)

    def row(self, other):
        return 1 - self.here.row if other else self.here.row

    def z_copy(self, at):
        here = self.here
        held = self.piece(here.depth, here.row, here.quarter)
        return remote(
            held, held, here.sends.at[self.z_base + at], here.recvs.at[self.z_base + here.depth], here.at_depth(at)
        )

    def z_arrival(self, at):
        held = self.piece(at, self.here.row, self.here.quarter)
        return self.here.link(held, held, self.z_base + at, self.here.to_y)

    def y_copy(self, at, other):
        held = self.piece(at, self.row(other), self.here.quarter)
        return self.here.link(held, held, self.y_base + at, self.here.to_y)

    def x_copy(self, at, other, quarter):
        held = self.piece(at, self.row(other), quarter)
        return self.here.link(held, held, self.x_base + other * self.here.count + at, self.here.to_x)

    def c_copy(self, at, other, level, quarter):
        held = self.piece(at, self.row(other), quarter)
        return self.here.link(
            held, held, self.c_base + (2 * level + other) * self.here.count + at, self.here.to_core
        )

    def onward(self, at, other):
        if self.spread:
            self.x_copy(at, other, self.here.quarter).start()
            self.c_copy(at, other, 0, self.here.quarter).start()

    def begin(self):
        self.here.others(lambda at: self.z_copy(at).start())
        self.y_copy(self.here.depth, 0).start()

    def z_phase(self):
        def step(at):
            self.z_arrival(at).wait_recv()
            self.y_copy(at, 0).start()
            self.onward(at, 0)

        self.here.others(step)

    def y_phase(self):
        def step(at):
            self.y_copy(at, 1).wait_recv()
            self.onward(at, 1)

        step(self.here.depth)
        self.here.others(step)

    def members(self, step):
        step(self.here.depth, 1)
        for other in (0, 1):
            self.here.others(lambda at: step(at, other))

    def x_phase(self):
        def step(at, other):
            self.x_copy(at, other, self.here.x_quarter).wait_recv()
            self.c_copy(at, other, 1, self.here.x_quarter).start()

        self.members(step)

    def finish(self):
        def step(at, other):
            self.c_copy(at, other, 0, self.here.core_quarter).wait_recv()
            self.c_copy(at, other, 1, self.here.far_quarter).wait_recv()

        self.members(step)

    def drain(self):
        here = self.here
        here.others(lambda at: self.z_copy(at).wait_send())
        self.y_copy(here.depth, 0).wait_send()
        here.others(lambda at: self.y_copy(at, 0).wait_send())

        def step(at, other):
            self.x_copy(at, other, here.quarter).wait_send()
            self.c_copy(at, other, 0, here.quarter).wait_send()
            self.c_copy(at, other, 1, here.x_quarter).wait_send()

        if self.spread:
            self.members(step)


class Scatter:
    def __init__(self, here, total, height, from_y, from_z, out):
        self.here, self.total, self.height, self.out = here, total, height, out
        self.from_y, self.from_z = from_y, from_z
        self.y_base = here.take(here.count)
        self.z_base = here.take(here.count)
        self.out_base = here.take(3)

    def block(self, depth, row):
        first = pl.multiple_of((depth * 2 + row) * self.height, self.height)
        return self.total.at[pl.ds(first, self.height), :]

    def y_copy(self, depth):
        here = self.here
        return here.link(self.block(depth, 1 - here.row), self.from_y.at[depth], self.y_base + depth, here.to_y)

    def y_begin(self):
        self.here.others(lambda at: self.y_copy(at).start())
        self.y_copy(self.here.depth).start()

    def z_copy(self, at):
        here = self.here
        return remote(
            self.block(at, here.row), self.from_z.at[here.depth], here.sends.at[self.z_base + at],
            here.recvs.at[self.z_base + here.depth], here.at_depth(at),
        )

    def y_phase(self):
        def step(at):
            self.y_copy(at).wait_recv()
            block = self.block(at, self.here.row)
            block[...] = block[...] + self.from_y[at]
            self.z_copy(at).start()

        self.here.others(step)

    def z_phase(self):
        here = self.here
        self.y_copy(here.depth).wait_recv()
        self.from_z[here.depth] = self.block(here.depth, here.row)[...] + self.from_y[here.depth]

        def wait(at):
            held = self.from_z.at[at]
            here.link(held, held, self.z_base + at, here.to_y).wait_recv()

        here.others(wait)
        summed = self.from_z[0].astype(jnp.float32)
        for at in range(1, here.count):
            summed = summed + self.from_z[at].astype(jnp.float32)
        self.out(here.quarter)[...] = summed.astype(jnp.bfloat16)
        self.out_copy(0).start()
        self.out_copy(1).start()

    def out_copy(self, level, quarter=None):
        here = self.here
        quarter = (here.quarter, here.quarter, here.x_quarter)[level] if quarter is None else quarter
        held = self.out(quarter)
        return here.link(held, held, self.out_base + level, here.to_x if level == 0 else here.to_core)

    def out_phase(self):
        self.out_copy(0, self.here.x_quarter).wait_recv()
        self.out_copy(2).start()

    def finish(self):
        here = self.here
        self.out_copy(1, here.core_quarter).wait_recv()
        self.out_copy(2, here.far_quarter).wait_recv()
        for level in range(3):
            self.out_copy(level).wait_send()
        self.y_copy(here.depth).wait_send()
        here.others(lambda at: self.y_copy(at).wait_send())
        here.others(lambda at: self.z_copy(at).wait_send())


class SmallSum:
    def __init__(self, here, held, landing, depth_held):
        self.here, self.held, self.landing, self.depth_held = here, held, landing, depth_held
        self.base = here.take(3 + here.count)
        self.partners = [here.to_core, here.to_x, here.to_y]

    def copy(self, level):
        return self.here.link(self.held.at[level], self.landing.at[level], self.base + level, self.partners[level])

    def z_copy(self, at):
        here = self.here
        held = self.depth_held.at[here.depth]
        return remote(
            held, held, here.sends.at[self.base + 3 + at], here.recvs.at[self.base + 3 + here.depth], here.at_depth(at)
        )

    def begin(self):
        self.copy(0).start()

    def level(self, level):
        here = self.here
        self.copy(level).wait_recv()
        summed = self.held[level] + self.landing[level]
        if level < 2:
            self.held[level + 1] = summed
            self.copy(level + 1).start()
        else:
            self.depth_held[here.depth] = summed
            for at in range(here.count):
                @pl.when(here.depth != at)
                def _():
                    self.z_copy(at).start()

    def finish(self):
        here = self.here
        for at in range(here.count):
            @pl.when(here.depth != at)
            def _():
                held = self.depth_held.at[at]
                here.link(held, held, self.base + 3 + at, here.to_y).wait_recv()
        summed = self.depth_held[0]
        for at in range(1, here.count):
            summed = summed + self.depth_held[at]
        for level in range(3):
            self.copy(level).wait_send()
        for at in range(here.count):
            @pl.when(here.depth != at)
            def _():
                self.z_copy(at).wait_send()
        return summed


class Swap:
    def __init__(self, here, source, target):
        self.here, self.source, self.target = here, source, target
        self.base = here.take(here.count)

    def copy(self, at):
        here = self.here
        return remote(
            self.source(at), self.target(here.depth), here.sends.at[self.base + at],
            here.recvs.at[self.base + here.depth], here.at_depth(at),
        )

    def begin(self):
        self.here.others(lambda at: self.copy(at).start())

    def arrive(self):
        def wait(at):
            held = self.target(at)
            self.here.link(held, held, self.base + at, self.here.to_y).wait_recv()

        self.here.others(wait)

    def drain(self):
        self.here.others(lambda at: self.copy(at).wait_send())


class SeqGather:
    def __init__(self, here, held):
        self.here, self.held = here, held
        self.base = here.take(3)

    def copy(self, level, index=None):
        here = self.here
        index = (here.quarter, here.quarter, here.x_quarter)[level] if index is None else index
        held = self.held.at[index]
        return here.link(held, held, self.base + level, here.to_x if level == 0 else here.to_core)

    def begin(self):
        self.copy(0).start()
        self.copy(1).start()

    def relay(self):
        self.copy(0, self.here.x_quarter).wait_recv()
        self.copy(2).start()

    def arrive(self):
        self.copy(1, self.here.core_quarter).wait_recv()
        self.copy(2, self.here.far_quarter).wait_recv()

    def drain(self):
        for level in range(3):
            self.copy(level).wait_send()


class SeqSum:
    def __init__(self, here, held, landing):
        self.here, self.held, self.landing = here, held, landing
        self.base = here.take(3)

    def copy(self, level):
        here = self.here
        index = (here.far_quarter, here.core_quarter, here.x_quarter)[level]
        return here.link(
            self.held.at[index], self.landing.at[level], self.base + level, here.to_x if level == 2 else here.to_core
        )

    def begin(self):
        self.copy(0).start()
        self.copy(1).start()

    def relay(self):
        here = self.here
        self.copy(0).wait_recv()
        self.held[here.x_quarter] = self.held[here.x_quarter] + self.landing[0]
        self.copy(2).start()

    def arrive(self):
        here = self.here
        self.copy(1).wait_recv()
        self.copy(2).wait_recv()
        own = self.held[here.quarter].astype(jnp.float32)
        return own + self.landing[1].astype(jnp.float32) + self.landing[2].astype(jnp.float32)

    def drain(self):
        for level in range(3):
            self.copy(level).wait_send()


class SeqSwap:
    def __init__(self, here, heights, landing):
        self.here, self.heights, self.landing = here, heights, landing
        self.base = here.take(4)

    def held(self, member, source):
        return self.landing.at[source, pl.ds(0, self.heights[member]), :]

    def copy(self, member, block):
        here = self.here
        return remote(
            block, self.held(member, here.seq), here.sends.at[self.base + member], here.recvs.at[self.base + here.seq],
            (member, here.depth, here.row),
        )

    def begin(self, member, block):
        here = self.here

        @pl.when(here.seq != member)
        def _():
            self.copy(member, block).start()

        @pl.when(here.seq == member)
        def _():
            self.held(member, here.seq)[...] = block[...]

    def arrive(self):
        here = self.here
        for member in range(4):
            @pl.when(here.seq == member)
            def _():
                for source in range(4):
                    if source != member:
                        held = self.held(member, source)
                        here.link(held, held, self.base + source, here.to_core).wait_recv()

    def drain(self):
        here = self.here
        for member in range(4):
            @pl.when(here.seq != member)
            def _():
                held = self.held(member, member)
                here.link(held, held, self.base + member, here.to_core).wait_send()


def tiles(total, width, body):
    def step(number, carry):
        body(pl.ds(pl.multiple_of(number * width, width), width))
        return carry

    lax.fori_loop(0, total // width, step, 0)


def times(left, right, left_dim, right_dim):
    return lax.dot_general(
        left, right, (((left_dim,), (right_dim,)), ((), ())), preferred_element_type=jnp.float32
    )


def normed_of(values):
    inverse = lax.rsqrt(jnp.mean(values * values, axis=-1, keepdims=True) + EPSILON)
    return values * inverse, inverse


def norm_back(upstream, values, gain):
    normed, inverse = normed_of(values)
    grad_gain = jnp.sum(upstream * normed, axis=0, keepdims=True)
    grad_normed = upstream * gain
    mean = jnp.mean(grad_normed * normed, axis=-1, keepdims=True)
    return inverse * (grad_normed - normed * mean), grad_gain


BF = jnp.bfloat16
F32 = jnp.float32


class Names:
    pass


def layer_kernel(sizes, names, *refs):
    r = Names()
    for name, ref in zip(names, refs):
        setattr(r, name, ref)
    count, tokens, features, enc, heads, quarter, rows, tall = sizes
    head = features // heads
    mine = heads // count
    width = mine * head
    length = count * tokens
    states = count * enc
    here = Place(count, r.sends, r.recvs)
    seq, depth, row = here.seq, here.depth, here.row

    own = pl.multiple_of((depth * 2 + row) * rows, rows)
    own_tall = pl.multiple_of((depth * 2 + row) * tall, tall)
    squares = [getattr(r, f"square{number}") for number in range(8)]
    local = [
        pltpu.make_async_copy(squares[number], r.weights.at[number, pl.ds(own, rows), :], r.local.at[number])
        for number in range(8)
    ]
    local.append(
        pltpu.make_async_copy(
            r.down.at[pl.ds(pl.multiple_of(seq * tall, tall), tall), :], r.down_quarter.at[pl.ds(own_tall, tall), :],
            r.local.at[8],
        )
    )
    for copy in local:
        copy.start()

    def weight_piece(chunk):
        return lambda at, at_row, quarter_at: r.weights.at[
            4 * chunk + quarter_at, pl.ds(pl.multiple_of((at * 2 + at_row) * rows, rows), rows), :
        ]

    def quarter_piece(whole, height):
        return lambda at, at_row, quarter_at: whole.at[
            pl.ds(pl.multiple_of((at * 2 + at_row) * height, height), height), :
        ]

    gathers = [
        Gather(here, weight_piece(0), True),
        Gather(here, weight_piece(1), True),
        Gather(here, quarter_piece(r.gate_quarter, rows), False),
        Gather(here, quarter_piece(r.linear_quarter, rows), False),
        Gather(here, quarter_piece(r.down_quarter, tall), False),
    ]
    mates = []
    for far in range(count):
        for flip in (0, 1):
            if far or flip:
                mates.append((lax.rem(depth + far, count), row if flip == 0 else 1 - row))
    partners = [(seq,) + mate for mate in mates] + [here.to_x, here.to_core, here.to_far]
    barrier = pltpu.get_barrier_semaphore()
    for partner in partners:
        pl.semaphore_signal(barrier, inc=1, device_id=partner, device_id_type=MESH)
    pl.semaphore_wait(barrier, len(partners))

    gain_base = here.take(2 * count - 1)
    r.all_gains[depth * 2 + row] = r.gains[...]
    gain_sends = [
        here.link(r.all_gains.at[depth * 2 + row], r.all_gains.at[depth * 2 + row], gain_base + number, (seq,) + mate)
        for number, mate in enumerate(mates)
    ]
    for copy in gain_sends:
        copy.start()
    for number in range(4):
        local[number].wait()
    gathers[0].begin()
    for number in range(4, 9):
        local[number].wait()
    gathers[1].begin()

    r.grads_in[seq] = r.out_grad[...]
    grads_in = SeqGather(here, r.grads_in)
    long = (tokens,) * 3 + (enc,)
    lefts = [SeqSwap(here, long, r.left.at[0]), SeqSwap(here, long[::-1], r.left.at[1])]
    rights = [SeqSwap(here, long, r.right.at[0]), SeqSwap(here, long[::-1], r.right.at[1])]

    for at in range(4):
        @pl.when(seq == at)
        def _():
            for source, whole in ((r.gate, r.gate_quarter), (r.linear, r.linear_quarter)):
                span = 4 * tall
                whole[pl.ds(own, rows), :] = jnp.concatenate(
                    [source[:, number * span + at * tall : number * span + (at + 1) * tall] for number in range(2 * count)],
                    axis=1,
                )

    key_at = lax.broadcasted_iota(jnp.int32, (tokens, length), 0)
    query_at = lax.broadcasted_iota(jnp.int32, (tokens, length), 1)
    for number in range(mine):
        strip = jnp.broadcast_to(r.bias[number : number + 1, :], (tokens, length))
        step = 1
        while step < tokens:
            strip = jnp.where((key_at // step) % 2 == 1, pltpu.roll(strip, step, 1), strip)
            step *= 2
        r.strip[number] = jnp.where(query_at >= key_at, strip, FAR_BELOW)

    for chunk in (2, 3, 4):
        gathers[chunk].begin()
    gathers[0].z_phase()
    gathers[0].y_phase()

    for far in range(count):
        for flip in (0, 1):
            if far or flip:
                source = lax.rem(depth + count - far, count) * 2 + (row if flip == 0 else 1 - row)
                held = r.all_gains.at[source]
                here.link(held, held, gain_base + far * 2 + flip - 1, here.to_core).wait_recv()
    lane = lax.broadcasted_iota(jnp.int32, (LANES, features), 0)
    column = lax.broadcasted_iota(jnp.int32, (LANES, features), 1)
    gain_rows = jnp.zeros((16, features), F32)
    for number in range(2 * count):
        select = jnp.logical_and(column - number * rows == lane, lane < rows)
        gain_rows = gain_rows + times(r.all_gains[number], select.astype(F32).astype(BF), 1, 0)
    r.gain_rows[...] = gain_rows

    def gain(number):
        return r.gain_rows[number : number + 1, :]

    x0 = r.hidden[...].astype(F32)
    h1 = (normed_of(x0)[0] * gain(0)).astype(BF)
    r.h1[...] = h1

    gathers[1].z_phase()
    gathers[0].x_phase()
    gathers[0].finish()

    for number in range(3):
        def project(at, number=number):
            r.qkv_t[number, at, :] = times(r.h1[...], r.weights[number, :, at], 1, 0).astype(BF).T

        tiles(features, 256, project)

    def head_rows(at):
        return pl.ds(pl.multiple_of(at * width, width), width)

    def token_lanes(at):
        return pl.ds(pl.multiple_of(at * tokens, tokens), tokens)

    def own_block(target, source):
        target[...] = source[...]

    qkv = Swap(
        here, lambda at: r.qkv_t.at[:, head_rows(at), :], lambda at: r.qkv_h.at[:, :, token_lanes(at)]
    )
    qkv.begin()
    own_block(r.qkv_h.at[:, :, token_lanes(depth)], r.qkv_t.at[:, head_rows(depth), :])

    gathers[1].y_phase()
    grads_in.begin()
    gathers[1].x_phase()
    gathers[1].finish()
    for member in range(3):
        lefts[0].begin(member, r.h1)
    lefts[0].begin(3, r.encoder)
    lefts[1].begin(0, r.encoder)

    for number in range(2):
        def project(at, number=number):
            r.cross_kv[number, pl.ds(pl.multiple_of(depth * enc, enc), enc), at] = times(
                r.encoder[...], r.weights[3 + number, :, at], 1, 0
            ).astype(BF)

        tiles(features, 256, project)

    def enc_rows(at):
        return pl.ds(pl.multiple_of(at * enc, enc), enc)

    own_kv = r.cross_kv.at[:, enc_rows(depth), :]
    cross = Swap(here, lambda at: own_kv, lambda at: r.cross_kv.at[:, enc_rows(at), :])
    cross.begin()

    qkv.arrive()

    def block_scores(number, block):
        keys = (block + 1) * tokens
        at = pl.ds(pl.multiple_of(number * head, head), head)
        query = r.qkv_h[0, at, block * tokens : keys]
        scores = times(r.qkv_h[1, at, :keys], query, 0, 0)
        bias = jnp.concatenate(
            [r.strip[number, :, (block - key) * tokens : (block - key + 1) * tokens] for key in range(block + 1)], axis=0
        )
        return scores + bias, at, keys, query

    def self_forward(number, carry):
        for block in range(count):
            scores, at, keys, _ = block_scores(number, block)
            top = jnp.max(scores, axis=0, keepdims=True)
            weights = jnp.exp(scores - top)
            total = jnp.sum(weights, axis=0, keepdims=True)
            mixed = times(r.qkv_h[2, at, :keys], weights.astype(BF), 1, 0)
            span = slice(block * tokens, keys)
            r.attn_h[at, span] = (mixed / total).astype(BF)
            r.lse[number, :, span] = top + jnp.log(total)
        return carry

    lax.fori_loop(0, mine, self_forward, 0)
    attn = Swap(here, lambda at: r.attn_h.at[:, token_lanes(at)], lambda at: r.attn_t.at[head_rows(at), :])
    attn.begin()
    own_block(r.attn_t.at[head_rows(depth), :], r.attn_h.at[:, token_lanes(depth)])

    for chunk in (2, 3, 4):
        gathers[chunk].z_phase()
    grads_in.relay()
    cross.arrive()
    for number in range(2):
        r.cross_t[number] = r.cross_kv[number].T
    attn.arrive()
    r.attn[...] = r.attn_t[...].T
    lefts[1].begin(1, r.attn)

    def after(at):
        r.x1[:, at] = r.hidden[:, at].astype(F32) + times(r.attn[...], r.weights[5, :, at], 1, 0)

    tiles(features, 256, after)
    h2 = (normed_of(r.x1[...])[0] * gain(1)).astype(BF)
    r.h2[...] = h2
    lefts[1].begin(2, r.h2)

    def project(at):
        r.cq_t[at, :] = times(r.h2[...], r.weights[6, :, at], 1, 0).astype(BF).T

    tiles(features, 256, project)

    def head_at(number):
        return pl.ds(pl.multiple_of(number * head, head), head)

    def cross_forward(number, carry):
        at = head_at(number)
        scores = times(r.cross_t[0, at, :], r.cq_t[at, :], 0, 0)
        top = jnp.max(scores, axis=0, keepdims=True)
        weights = jnp.exp(scores - top)
        total = jnp.sum(weights, axis=0, keepdims=True)
        mixed = times(r.cross_t[1, at, :], weights.astype(BF), 1, 0)
        r.cattn_t[at, :] = (mixed / total).astype(BF)
        r.clse[number] = top + jnp.log(total)
        return carry

    lax.fori_loop(0, heads, cross_forward, 0)
    r.cattn[...] = r.cattn_t[...].T
    lefts[1].begin(3, r.cattn)

    def after(at):
        r.x2[:, at] = r.x1[:, at] + times(r.cattn[...], r.weights[7, :, at], 1, 0)

    tiles(features, 256, after)
    r.h3[seq] = (normed_of(r.x2[...])[0] * gain(2)).astype(BF)
    h3 = SeqGather(here, r.h3)
    h3.begin()
    gathers[2].y_phase()
    gathers[3].y_phase()
    h3.relay()
    gathers[4].y_phase()
    grads_in.arrive()
    h3.arrive()

    group = 4 * tokens
    hidden_rows = r.h3[...].reshape(group, features)
    grad_rows = r.grads_in[...].reshape(group, features)
    root = math.sqrt(2.0 / math.pi)

    def feed(at):
        gate = times(hidden_rows, r.gate_quarter[:, at], 1, 0)
        linear = times(hidden_rows, r.linear_quarter[:, at], 1, 0)
        grad = times(grad_rows, r.down_quarter[at, :], 1, 1)
        square = gate * gate
        bent = jnp.tanh(root * gate * (1.0 + 0.044715 * square))
        half = 0.5 * (1.0 + bent)
        curve = gate * half
        slope = half + 0.5 * gate * (1.0 - bent * bent) * (root * (1.0 + 3 * 0.044715 * square))
        r.middle[:, at] = (curve * linear).astype(BF)
        r.grad_gate[:, at] = (grad * linear * slope).astype(BF)
        r.grad_linear[:, at] = (grad * curve).astype(BF)

    tiles(quarter, 256, feed)

    def back(at):
        upstream = times(r.grad_gate[...], r.gate_quarter[at, :], 1, 1) + times(
            r.grad_linear[...], r.linear_quarter[at, :], 1, 1
        )
        r.gh3[:, :, at] = upstream.reshape(4, tokens, -1).astype(BF)

    tiles(features, 256, back)
    gh3 = SeqSum(here, r.gh3, r.gh3_in)
    gh3.begin()

    def forth(at):
        r.lout[:, :, at] = times(r.middle[...], r.down_quarter[:, at], 1, 0).reshape(4, tokens, -1).astype(BF)

    tiles(features, 256, forth)
    lout = SeqSum(here, r.lout, r.lout_in)
    gh3.relay()
    lout.begin()

    def down_terms(at):
        r.down_terms[at, :] = times(r.middle[:, at], grad_rows, 0, 0).astype(BF)

    tiles(quarter, 256, down_terms)
    feeds = [
        Scatter(here, r.down_terms, tall, r.down_y, r.down_z, lambda q: r.out_down.at[q]),
        Scatter(here, r.gate_terms, rows, r.gate_y, r.gate_z, lambda q: r.out_gate.at[q]),
        Scatter(here, r.linear_terms, rows, r.linear_y, r.linear_z, lambda q: r.out_linear.at[q]),
    ]
    feeds[0].y_begin()

    def gate_terms(at):
        r.gate_terms[at, :] = times(hidden_of(at), r.grad_gate[...], 0, 0).astype(BF)

    def linear_terms(at):
        r.linear_terms[at, :] = times(hidden_of(at), r.grad_linear[...], 0, 0).astype(BF)

    def hidden_of(at):
        return r.h3[:, :, at].reshape(group, -1)

    tiles(features, 256, gate_terms)
    feeds[1].y_begin()
    lout.relay()
    tiles(features, 256, linear_terms)
    feeds[2].y_begin()

    grad_x2, gain_three = norm_back(gh3.arrive(), r.x2[...], gain(2))
    grad_x2 = r.out_grad[...].astype(F32) + grad_x2
    r.gx[...] = grad_x2
    rounded = grad_x2.astype(BF)
    r.rounded[...] = rounded
    rights[1].begin(3, r.rounded)

    def pull(at):
        r.grad_t[at, :] = times(r.rounded[...], r.weights[7, at, :], 1, 1).astype(BF).T

    tiles(features, 256, pull)

    def cross_backward(number, carry):
        at = head_at(number)
        grad = r.grad_t[at, :]
        delta = jnp.sum(grad.astype(F32) * r.cattn_t[at, :].astype(F32), axis=0, keepdims=True)
        query, keys = r.cq_t[at, :], r.cross_t[0, at, :]
        probs = jnp.exp(times(keys, query, 0, 0) - r.clse[number])
        terms = (probs * (times(r.cross_t[1, at, :], grad, 0, 0) - delta)).astype(BF)
        r.gq_t[at, :] = times(keys, terms, 1, 0).astype(BF)
        r.cross_terms_t[0, at, :] = times(query, terms, 1, 1)
        r.cross_terms_t[1, at, :] = times(grad, probs.astype(BF), 1, 1)
        return carry

    lax.fori_loop(0, heads, cross_backward, 0)
    for number in range(2):
        r.cross_terms[number] = r.cross_terms_t[number].T.astype(BF)
    cross_terms = Swap(here, lambda at: r.cross_terms.at[:, enc_rows(at), :], lambda at: r.cross_in.at[at])
    cross_terms.begin()
    r.cross_in[depth] = r.cross_terms[:, enc_rows(depth), :]
    r.gq[...] = r.gq_t[...].T
    rights[1].begin(2, r.gq)

    spread = [
        Scatter(
            here, r.terms.at[chunk], rows, r.terms_y.at[chunk], r.terms_z.at[chunk],
            lambda q, chunk=chunk: r.out_squares.at[4 * chunk + q],
        )
        for chunk in range(2)
    ]

    def square_terms(chunk):
        lefts[chunk].arrive()
        rights[chunk].arrive()
        heights = lefts[chunk].heights
        short = heights.index(enc)
        for which, height in ((seq != short, tokens), (seq == short, enc)):
            @pl.when(which)
            def _():
                def body(at):
                    left = r.left[chunk, :, :height, at].reshape(4 * height, -1)
                    right = r.right[chunk, :, :height, :].reshape(4 * height, features)
                    r.terms[chunk, at, :] = times(left, right, 0, 0).astype(BF)

                tiles(features, 256, body)

        spread[chunk].y_begin()

    feeds[0].y_phase()

    def pull(at):
        r.up[:, at] = times(r.gq[...], r.weights[6, at, :], 1, 1)

    tiles(features, 256, pull)
    grad_x1, gain_two = norm_back(r.up[...], r.x1[...], gain(1))
    grad_x1 = r.gx[...] + grad_x1
    r.gx[...] = grad_x1
    r.rounded_one[...] = grad_x1.astype(BF)
    rights[1].begin(1, r.rounded_one)

    def pull(at):
        r.grad_t[at, :] = times(r.rounded_one[...], r.weights[5, at, :], 1, 1).astype(BF).T

    tiles(features, 256, pull)
    grad_attn = Swap(here, lambda at: r.grad_t.at[head_rows(at), :], lambda at: r.grad_h.at[:, token_lanes(at)])
    grad_attn.begin()
    own_block(r.grad_h.at[:, token_lanes(depth)], r.grad_t.at[head_rows(depth), :])

    feeds[1].y_phase()
    feeds[0].z_phase()
    cross_terms.arrive()
    summed = r.cross_in[0].astype(F32)
    for at in range(1, count):
        summed = summed + r.cross_in[at].astype(F32)
    r.cross_sum[...] = summed.astype(BF)
    rights[0].begin(3, r.cross_sum.at[0])
    rights[1].begin(0, r.cross_sum.at[1])
    square_terms(1)
    feeds[2].y_phase()
    r.layer_out[...] = (r.x2[...] + lout.arrive()).astype(BF)

    def encoder_back(at):
        r.encoder_grad[:, at] = times(r.cross_sum[0], r.weights[3, at, :], 1, 1) + times(
            r.cross_sum[1], r.weights[4, at, :], 1, 1
        )

    tiles(features, 256, encoder_back)
    feeds[1].z_phase()
    feeds[0].out_phase()
    spread[1].y_phase()

    grad_attn.arrive()

    def self_backward(number, carry):
        at = head_at(number)
        r.dkv[...] = jnp.zeros_like(r.dkv)
        r.strip_sum[...] = jnp.zeros_like(r.strip_sum)
        for block in range(count):
            scores, _, keys, query = block_scores(number, block)
            span = slice(block * tokens, keys)
            grad = r.grad_h[at, span]
            delta = jnp.sum(grad.astype(F32) * r.attn_h[at, span].astype(F32), axis=0, keepdims=True)
            probs = jnp.exp(scores - r.lse[number, :, span])
            grad_scores = probs * (times(r.qkv_h[2, at, :keys], grad, 0, 0) - delta)
            terms = grad_scores.astype(BF)
            r.dqkv_h[0, at, span] = times(r.qkv_h[1, at, :keys], terms, 1, 0).astype(BF)
            r.dkv[0, :, :keys] += times(query, terms, 1, 1)
            r.dkv[1, :, :keys] += times(grad, probs.astype(BF), 1, 1)
            for key in range(block + 1):
                lanes = slice((block - key) * tokens, (block - key + 1) * tokens)
                r.strip_sum[:, lanes] += grad_scores[key * tokens : (key + 1) * tokens, :]
        r.dqkv_h[1, at, :] = r.dkv[0].astype(BF)
        r.dqkv_h[2, at, :] = r.dkv[1].astype(BF)
        strip = r.strip_sum[...]
        step = 1
        while step < tokens:
            strip = jnp.where((key_at // step) % 2 == 1, pltpu.roll(strip, length - step, 1), strip)
            step *= 2
        r.small[0, pl.ds(mine * depth + number, 1), :length] = jnp.sum(strip, axis=0, keepdims=True)
        return carry

    r.small[0] = jnp.zeros(r.small.shape[1:], F32)
    lax.fori_loop(0, mine, self_backward, 0)
    dqkv = Swap(
        here, lambda at: r.dqkv_h.at[:, :, token_lanes(at)], lambda at: r.dqkv_t.at[:, head_rows(at), :]
    )
    dqkv.begin()
    own_block(r.dqkv_t.at[:, head_rows(depth), :], r.dqkv_h.at[:, :, token_lanes(depth)])
    feeds[2].z_phase()
    feeds[1].out_phase()
    spread[1].z_phase()
    dqkv.arrive()
    for number in range(3):
        r.dqkv[number] = r.dqkv_t[number].T
        rights[0].begin(number, r.dqkv.at[number])

    def pull(at):
        r.up[:, at] = (
            times(r.dqkv[0], r.weights[0, at, :], 1, 1)
            + times(r.dqkv[1], r.weights[1, at, :], 1, 1)
            + times(r.dqkv[2], r.weights[2, at, :], 1, 1)
        )

    tiles(features, 256, pull)
    grad_x0, gain_one = norm_back(r.up[...], r.hidden[...].astype(F32), gain(0))
    r.input_grad[...] = r.gx[...] + grad_x0
    for number, value in enumerate((gain_one, gain_two, gain_three)):
        r.small[0, heads + number : heads + number + 1, :] = value
    small = SmallSum(here, r.small, r.small_in, r.small_depth)
    small.begin()
    square_terms(0)
    feeds[2].out_phase()
    spread[1].out_phase()
    small.level(0)
    small.level(1)
    small.level(2)
    spread[0].y_phase()
    spread[0].z_phase()
    r.small_out[...] = small.finish()
    for work in gathers:
        work.drain()
    for copy in gain_sends:
        copy.wait_send()
    for work in (*lefts, *rights, qkv, attn, cross, cross_terms, grad_attn, dqkv, h3, grads_in, gh3, lout):
        work.drain()
    for work in feeds:
        work.finish()
    spread[1].finish()
    spread[0].out_phase()
    spread[0].finish()
    for source, whole in ((r.out_gate, r.whole_gate), (r.out_linear, r.whole_linear)):
        held = [source[at] for at in range(4)]
        whole[...] = jnp.concatenate(
            [held[at][:, number * tall : (number + 1) * tall] for number in range(2 * count) for at in range(4)], axis=1
        )


def run_layer(hidden, encoder, out_grad, bias, squares, gate, linear, down, gains):
    count = lax.axis_size("ctx")
    tokens, features = hidden.shape
    enc = encoder.shape[0]
    rows, hidden_units = gate.shape
    heads = features // 64
    quarter = hidden_units // 4
    tall = down.shape[0] // 4
    length, states = count * tokens, count * enc
    mine = heads // count
    width = features // count
    head = features // heads
    small = (-(-(heads + 3) // 8) * 8, features)
    used = 96 * count
    vmem = pl.BlockSpec(memory_space=pltpu.VMEM)
    held = pl.BlockSpec(memory_space=pl.ANY)
    inputs = dict(
        hidden=(hidden, vmem),
        encoder=(encoder, vmem),
        out_grad=(out_grad, vmem),
        bias=(bias, vmem),
        **{f"square{number}": (member, held) for number, member in enumerate(squares)},
        gate=(gate, vmem),
        linear=(linear, vmem),
        down=(down, held),
        gains=(gains, vmem),
    )
    outputs = dict(
        layer_out=((tokens, features), BF),
        input_grad=((tokens, features), F32),
        encoder_grad=((enc, features), F32),
        small_out=(small, F32),
        out_squares=((8, rows, features), BF),
        out_down=((4, tall, features), BF),
        whole_gate=((rows, hidden_units), BF),
        whole_linear=((rows, hidden_units), BF),
    )
    square = (features, features)
    near = (count,)
    scratch = dict(
        weights=((8,) + square, BF),
        gate_quarter=((features, quarter), BF),
        linear_quarter=((features, quarter), BF),
        down_quarter=((quarter, features), BF),
        all_gains=((2 * count,) + gains.shape, BF),
        gain_rows=((16, features), F32),
        strip=((mine, tokens, length), F32),
        strip_sum=((tokens, length), F32),
        h1=((tokens, features), BF),
        h2=((tokens, features), BF),
        qkv_t=((3, features, tokens), BF),
        qkv_h=((3, width, length), BF),
        attn_h=((width, length), BF),
        attn_t=((features, tokens), BF),
        attn=((tokens, features), BF),
        lse=((mine, 1, length), F32),
        cross_kv=((2, states, features), BF),
        cross_t=((2, features, states), BF),
        cq_t=((features, tokens), BF),
        cattn_t=((features, tokens), BF),
        clse=((heads, 1, tokens), F32),
        x1=((tokens, features), F32),
        x2=((tokens, features), F32),
        gx=((tokens, features), F32),
        up=((tokens, features), F32),
        rounded=((tokens, features), BF),
        h3=((4, tokens, features), BF),
        grads_in=((4, tokens, features), BF),
        middle=((4 * tokens, quarter), BF),
        grad_gate=((4 * tokens, quarter), BF),
        grad_linear=((4 * tokens, quarter), BF),
        gh3=((4, tokens, features), BF),
        gh3_in=((3, tokens, features), BF),
        lout=((4, tokens, features), BF),
        lout_in=((3, tokens, features), BF),
        down_terms=((quarter, features), BF),
        gate_terms=((features, quarter), BF),
        linear_terms=((features, quarter), BF),
        down_y=((count, tall, features), BF),
        gate_y=((count, rows, quarter), BF),
        linear_y=((count, rows, quarter), BF),
        down_z=(near + (tall, features), BF),
        gate_z=(near + (rows, quarter), BF),
        linear_z=(near + (rows, quarter), BF),
        out_gate=((4, rows, quarter), BF),
        out_linear=((4, rows, quarter), BF),
        grad_t=((features, tokens), BF),
        gq_t=((features, tokens), BF),
        gq=((tokens, features), BF),
        cross_terms_t=((2, features, states), F32),
        cross_terms=((2, states, features), BF),
        cross_in=((count, 2, enc, features), BF),
        cross_sum=((2, enc, features), BF),
        terms=((2,) + square, BF),
        left=((2, 4, tokens, features), BF),
        right=((2, 4, tokens, features), BF),
        rounded_one=((tokens, features), BF),
        cattn=((tokens, features), BF),
        terms_y=((2, count, rows, features), BF),
        terms_z=((2,) + near + (rows, features), BF),
        grad_h=((width, length), BF),
        dkv=((2, head, length), F32),
        dqkv_h=((3, width, length), BF),
        dqkv_t=((3, features, tokens), BF),
        dqkv=((3, tokens, features), BF),
        small=((3,) + small, F32),
        small_in=((3,) + small, F32),
        small_depth=((count,) + small, F32),
    )
    names = list(inputs) + list(outputs) + list(scratch) + ["local", "sends", "recvs"]
    return pl.pallas_call(
        partial(layer_kernel, (count, tokens, features, enc, heads, quarter, rows, tall), names),
        out_shape=tuple(jax.ShapeDtypeStruct(shape, kind) for shape, kind in outputs.values()),
        in_specs=[spec for _, spec in inputs.values()],
        out_specs=[vmem] * len(outputs),
        scratch_shapes=[
            *(pltpu.VMEM(shape, kind) for shape, kind in scratch.values()),
            pltpu.SemaphoreType.DMA((9,)),
            pltpu.SemaphoreType.DMA((used,)),
            pltpu.SemaphoreType.DMA((used,)),
        ],
        compiler_params=pltpu.CompilerParams(
            collective_id=0, has_side_effects=True, vmem_limit_bytes=60 << 20
        ),
        cost_estimate=pl.CostEstimate(flops=8 * 10**9, bytes_accessed=10**7, transcendentals=10**6),
        name="layer",
    )(*(member for member, _ in inputs.values()))


def per_device_whole(
    hidden_in,
    encoder_states,
    out_grad,
    bucket_index,
    bias_table,
    self_gain,
    self_query,
    self_key,
    self_value,
    self_output,
    cross_gain,
    cross_query,
    cross_key,
    cross_value,
    cross_output,
    feed_gain,
    gate_weight,
    linear_weight,
    down_weight,
):
    count = lax.axis_size("ctx")
    rows, features = self_query.shape
    buckets, heads = bias_table.shape
    length = bucket_index.shape[0]
    mine = heads // count
    onehot = (bucket_index[:, None] == jnp.arange(buckets, dtype=jnp.int32)[None, :]).astype(jnp.float32)
    own_table = lax.dynamic_slice_in_dim(bias_table, lax.axis_index("ctx") * mine, mine, 1)
    own_table = jnp.pad(own_table, ((0, 0), (0, -mine % 8)))
    bias = jnp.dot(onehot, own_table, precision=HIGHEST).T
    gains = jnp.pad(jnp.stack([self_gain, cross_gain, feed_gain]), ((0, 13), (0, LANES - rows)))
    layer_out, input_grad, encoder_grad, small, squares, down, gate, linear = run_layer(
        hidden_in[0],
        encoder_states[0],
        out_grad[0],
        bias,
        (self_query, self_key, self_value, cross_key, cross_value, self_output, cross_query, cross_output),
        gate_weight,
        linear_weight,
        down_weight,
        gains,
    )
    grad_table = jnp.dot(onehot.T, small[:heads, :length].T, precision=HIGHEST)
    shard = lax.axis_index(("ctx", "fsdp"))
    gain_sums = lax.dynamic_slice_in_dim(small[heads : heads + 3], shard * rows, rows, 1)
    squares = squares.astype(jnp.float32)
    return (
        layer_out[None],
        input_grad[None],
        encoder_grad[None],
        grad_table,
        gain_sums[0],
        squares[0],
        squares[1],
        squares[2],
        squares[5],
        gain_sums[1],
        squares[6],
        squares[3],
        squares[4],
        squares[7],
        gain_sums[2],
        gate.astype(jnp.float32),
        linear.astype(jnp.float32),
        down.reshape(-1, features).astype(jnp.float32),
    )


def fits(mesh):
    return mesh.shape["seq"] == 4 and mesh.shape["fsdp"] == 2 and mesh.shape["ctx"] <= 4


def solution(mesh):
    return jax.shard_map(
        per_device_whole if fits(mesh) else per_device,
        mesh=mesh,
        in_specs=(
            P(("seq", "fsdp"), "ctx", None),
            P(("seq", "fsdp"), "ctx", None),
            P(("seq", "fsdp"), "ctx", None),
            P(),
            P(),
            P(("ctx", "fsdp")),
            P(("ctx", "fsdp"), None),
            P(("ctx", "fsdp"), None),
            P(("ctx", "fsdp"), None),
            P(("ctx", "fsdp"), None),
            P(("ctx", "fsdp")),
            P(("ctx", "fsdp"), None),
            P(("ctx", "fsdp"), None),
            P(("ctx", "fsdp"), None),
            P(("ctx", "fsdp"), None),
            P(("ctx", "fsdp")),
            P(("ctx", "fsdp"), None),
            P(("ctx", "fsdp"), None),
            P(("ctx", "fsdp"), None),
        ),
        out_specs=(
            P(("seq", "fsdp"), "ctx", None),
            P(("seq", "fsdp"), "ctx", None),
            P(("seq", "fsdp"), "ctx", None),
            P(),
            P(("ctx", "fsdp")),
            P(("ctx", "fsdp"), None),
            P(("ctx", "fsdp"), None),
            P(("ctx", "fsdp"), None),
            P(("ctx", "fsdp"), None),
            P(("ctx", "fsdp")),
            P(("ctx", "fsdp"), None),
            P(("ctx", "fsdp"), None),
            P(("ctx", "fsdp"), None),
            P(("ctx", "fsdp"), None),
            P(("ctx", "fsdp")),
            P(("ctx", "fsdp"), None),
            P(("ctx", "fsdp"), None),
            P(("ctx", "fsdp"), None),
        ),
        check_vma=False,
    )
```

```python
from functools import partial
import math

import jax
import jax.numpy as jnp
from jax import lax
from jax.experimental import pallas as pl
from jax.experimental.pallas import tpu as pltpu
from jax.sharding import PartitionSpec as P

EPSILON = 1e-06
NEGATIVE = -1e30
HIGHEST = lax.Precision.HIGHEST


LANES = 128


def fold_rows(rows, height):
    count = -(-rows.shape[-2] // height)
    short = count * height - rows.shape[-2]
    padding = [(0, 0)] * (rows.ndim - 2) + [(0, short), (0, 0)]
    padded = jnp.pad(rows, padding)
    return jnp.concatenate(
        [padded[..., number * height : (number + 1) * height, :] for number in range(count)],
        axis=-1,
    )


def unfold_rows(columns, row_count, features):
    count = columns.shape[-1] // features
    stacked = jnp.concatenate(
        [columns[..., number * features : (number + 1) * features] for number in range(count)],
        axis=-2,
    )
    return stacked[..., :row_count, :]


def gain_columns(gains, dtype):
    columns = jnp.stack([member.astype(dtype) for member in gains], axis=1)
    return jnp.pad(columns, ((0, 0), (0, LANES - columns.shape[1])))


def product(left, right):
    return jnp.dot(left, right, preferred_element_type=jnp.float32)


def row_contract(left, right):
    return lax.dot_general(
        left, right, (((0,), (0,)), ((), ())), preferred_element_type=jnp.float32
    )


def col_contract(left, right):
    return lax.dot_general(
        left, right, (((1,), (1,)), ((), ())), preferred_element_type=jnp.float32
    )


def norm_forward(values, gain):
    inverse = lax.rsqrt(jnp.mean(values * values, axis=-1, keepdims=True) + EPSILON)
    normed = values * inverse
    return ((normed * gain.astype(jnp.float32)).astype(jnp.bfloat16), normed, inverse)


def norm_backward(upstream, normed, inverse, gain):
    grad_gain = jnp.sum(upstream * normed, axis=0)
    grad_normed = upstream * gain.astype(jnp.float32)
    grad_values = inverse * (
        grad_normed - normed * jnp.mean(grad_normed * normed, axis=-1, keepdims=True)
    )
    return (grad_values, grad_gain)


def geglu(gate_pre, linear_pre):
    return jax.nn.gelu(gate_pre, approximate=True) * linear_pre


def by_heads(values, head_count):
    return values.reshape(values.shape[0], head_count, values.shape[1] // head_count)


def band_onehot(bucket_rev, buckets, query_rows, key_rows, query_first, key_first):
    length = bucket_rev.shape[0] // 2
    offset_first = query_first - key_first
    upper_band = lax.dynamic_slice_in_dim(bucket_rev, length - 1 - offset_first, key_rows, 0)
    lower_band = lax.dynamic_slice_in_dim(
        bucket_rev, length - offset_first - query_rows, query_rows - 1, 0
    )
    slots = jnp.concatenate([upper_band, jnp.full((1,), -1, jnp.int32), lower_band])
    return (slots[:, None] == jnp.arange(buckets, dtype=jnp.int32)[None, :]).astype(jnp.float32)


def spread_band(band, query_rows, key_rows):
    head_count, width = band.shape
    tiled = jnp.broadcast_to(band[:, None, :], (head_count, query_rows, width)).reshape(
        head_count, query_rows * width
    )
    return tiled[:, : query_rows * (width - 1)].reshape(head_count, query_rows, width - 1)[
        :, :, :key_rows
    ]


def fold_band(grad_scores, width):
    head_count, query_rows, key_rows = grad_scores.shape
    padded = jnp.pad(grad_scores, ((0, 0), (0, 0), (0, width - 1 - key_rows))).reshape(
        head_count, query_rows * (width - 1)
    )
    padded = jnp.pad(padded, ((0, 0), (0, query_rows)))
    return jnp.sum(padded.reshape(head_count, query_rows, width), axis=1)


def self_scores(query, key_block, query_first, key_first, bucket_rev, bias_table):
    head_count = bias_table.shape[1]
    query_rows = query.shape[0]
    key_rows = key_block.shape[0]
    scores = jnp.einsum(
        "qhe,khe->hqk",
        by_heads(query, head_count),
        by_heads(key_block, head_count),
        preferred_element_type=jnp.float32,
    )
    offset = (query_first + jnp.arange(query_rows, dtype=jnp.int32))[:, None] - (
        key_first + jnp.arange(key_rows, dtype=jnp.int32)
    )[None, :]
    allowed = offset >= 0
    onehot = band_onehot(
        bucket_rev, bias_table.shape[0], query_rows, key_rows, query_first, key_first
    )
    band = jnp.dot(onehot, bias_table, precision=HIGHEST).T
    scores = jnp.where(allowed[None], scores + spread_band(band, query_rows, key_rows), NEGATIVE)
    return (scores, allowed, onehot)


def table_terms(grad_scores, onehot):
    band_grad = fold_band(grad_scores, onehot.shape[0])
    return jnp.dot(onehot.T, band_grad.T, precision=HIGHEST)


def fold_blocks(block_step, running, arrays, first_row):
    piece_rows = arrays[0].shape[0]
    block_size = math.gcd(piece_rows, 512) if piece_rows > 512 else piece_rows
    if block_size == piece_rows:
        return block_step(running, arrays, first_row)
    block_count = piece_rows // block_size
    stacked = tuple(
        (member.reshape((block_count, block_size) + member.shape[1:]) for member in arrays)
    )

    def scan_block(state_now, scanned):
        number, blocks = scanned
        return (block_step(state_now, blocks, first_row + number * block_size), None)

    result, _ = lax.scan(scan_block, running, (jnp.arange(block_count, dtype=jnp.int32), stacked))
    return result


def forward_step(running, blocks, key_first, query, query_first, bucket_rev, bias_table):
    top, total, mixed = running
    key_block, value_block = blocks
    head_count = bias_table.shape[1]
    scores, allowed, _ = self_scores(
        query, key_block, query_first, key_first, bucket_rev, bias_table
    )
    new_top = jnp.maximum(top, jnp.max(scores, axis=-1))
    weights = jnp.where(allowed[None], jnp.exp(scores - new_top[:, :, None]), 0.0)
    rescale = jnp.exp(top - new_top)
    total = total * rescale + jnp.sum(weights, axis=-1)
    update = jnp.einsum(
        "hqk,khe->qhe",
        weights.astype(jnp.bfloat16),
        by_heads(value_block, head_count),
        preferred_element_type=jnp.float32,
    )
    mixed = mixed * rescale.T[:, :, None] + update
    return (new_top, total, mixed)


def backward_core(
    query,
    grad_attn,
    lse_rows,
    delta_rows,
    key_block,
    value_block,
    query_first,
    key_first,
    bucket_rev,
    bias_table,
):
    head_count = bias_table.shape[1]
    scores, allowed, onehot = self_scores(
        query, key_block, query_first, key_first, bucket_rev, bias_table
    )
    probs = jnp.where(allowed[None], jnp.exp(scores - lse_rows.T[:, :, None]), 0.0)
    grad_probs = jnp.einsum(
        "qhe,khe->hqk",
        by_heads(grad_attn, head_count),
        by_heads(value_block, head_count),
        preferred_element_type=jnp.float32,
    )
    grad_scores = probs * (grad_probs - delta_rows.T[:, :, None])
    return (probs, grad_scores, onehot)


def partial_step(
    running,
    blocks,
    key_first,
    query,
    grad_attn,
    lse_rows,
    delta_rows,
    query_first,
    bucket_rev,
    bias_table,
):
    grad_query, grad_keys, grad_values, table_part = running
    key_block, value_block = blocks
    head_count = bias_table.shape[1]
    probs, grad_scores, onehot = backward_core(
        query,
        grad_attn,
        lse_rows,
        delta_rows,
        key_block,
        value_block,
        query_first,
        key_first,
        bucket_rev,
        bias_table,
    )
    rounded = grad_scores.astype(jnp.bfloat16)
    grad_query = grad_query + jnp.einsum(
        "hqk,khe->qhe", rounded, by_heads(key_block, head_count), preferred_element_type=jnp.float32
    )
    key_part = jnp.einsum(
        "hqk,qhe->khe", rounded, by_heads(query, head_count), preferred_element_type=jnp.float32
    ).reshape(key_block.shape[0], -1)
    value_part = jnp.einsum(
        "hqk,qhe->khe",
        probs.astype(jnp.bfloat16),
        by_heads(grad_attn, head_count),
        preferred_element_type=jnp.float32,
    ).reshape(key_block.shape[0], -1)
    grad_keys = lax.dynamic_update_slice_in_dim(grad_keys, key_part, key_first, 0)
    grad_values = lax.dynamic_update_slice_in_dim(grad_values, value_part, key_first, 0)
    table_part = table_part + table_terms(grad_scores, onehot)
    return (grad_query, grad_keys, grad_values, table_part)


def plain_forward(query, keys, values, head_count):
    scores = jnp.einsum(
        "qhe,khe->hqk",
        by_heads(query, head_count),
        by_heads(keys, head_count),
        preferred_element_type=jnp.float32,
    )
    top = jnp.max(scores, axis=-1, keepdims=True)
    weights = jnp.exp(scores - top)
    total = jnp.sum(weights, axis=-1, keepdims=True)
    mixed = jnp.einsum(
        "hqk,khe->qhe",
        weights.astype(jnp.bfloat16),
        by_heads(values, head_count),
        preferred_element_type=jnp.float32,
    )
    result = (
        (mixed / jnp.transpose(total, (1, 0, 2))).reshape(query.shape[0], -1).astype(jnp.bfloat16)
    )
    return (result, (top + jnp.log(total))[:, :, 0])


def plain_backward(query, keys, values, lse, output, grad_output, head_count):
    split_grad = by_heads(grad_output, head_count)
    delta = jnp.sum(
        split_grad.astype(jnp.float32) * by_heads(output, head_count).astype(jnp.float32), axis=-1
    ).T
    scores = jnp.einsum(
        "qhe,khe->hqk",
        by_heads(query, head_count),
        by_heads(keys, head_count),
        preferred_element_type=jnp.float32,
    )
    probs = jnp.exp(scores - lse[:, :, None])
    grad_probs = jnp.einsum(
        "qhe,khe->hqk", split_grad, by_heads(values, head_count), preferred_element_type=jnp.float32
    )
    rounded = (probs * (grad_probs - delta[:, :, None])).astype(jnp.bfloat16)
    grad_query = jnp.einsum(
        "hqk,khe->qhe", rounded, by_heads(keys, head_count), preferred_element_type=jnp.float32
    ).reshape(query.shape[0], -1)
    grad_keys = jnp.einsum(
        "hqk,qhe->khe", rounded, by_heads(query, head_count), preferred_element_type=jnp.float32
    ).reshape(keys.shape[0], -1)
    grad_values = jnp.einsum(
        "hqk,qhe->khe", probs.astype(jnp.bfloat16), split_grad, preferred_element_type=jnp.float32
    ).reshape(keys.shape[0], -1)
    return (grad_query, grad_keys, grad_values)


def reduce_terms(terms, table_terms):
    groups = lax.axis_size("seq")
    share = terms.shape[1] // groups
    stacked = jnp.stack(
        [terms[:, number * share : (number + 1) * share] for number in range(groups)]
    )
    part = lax.psum_scatter(stacked, "seq", scatter_dimension=0, tiled=False)
    table = lax.psum(table_terms, ("seq", "ctx", "fsdp"))
    part, table = lax.optimization_barrier((part, table))
    part = lax.psum_scatter(part, ("ctx", "fsdp"), scatter_dimension=0, tiled=True)
    return join_columns(lax.all_gather(part, "seq", axis=0, tiled=False)), table


def join_columns(stacked):
    return jnp.concatenate([stacked[number] for number in range(stacked.shape[0])], axis=1)


def gather_pack(pack):
    share = pack.shape[1] // lax.axis_size("seq")
    own = lax.dynamic_slice_in_dim(pack, lax.axis_index("seq") * share, share, 1)
    rows = lax.all_gather(own, ("ctx", "fsdp"), axis=0, tiled=True)
    return join_columns(lax.all_gather(rows, "seq", axis=0, tiled=False))


def even_columns(members):
    joined = jnp.concatenate(members, axis=1)
    return jnp.pad(joined, ((0, 0), (0, -joined.shape[1] % (LANES * lax.axis_size("seq")))))


def per_device(
    hidden_in,
    encoder_states,
    out_grad,
    bucket_index,
    bias_table,
    self_gain,
    self_query,
    self_key,
    self_value,
    self_output,
    cross_gain,
    cross_query,
    cross_key,
    cross_value,
    cross_output,
    feed_gain,
    gate_weight,
    linear_weight,
    down_weight,
):
    shards = lax.axis_size(("ctx", "fsdp"))
    features = self_query.shape[1]
    hidden = gate_weight.shape[1]
    pack = even_columns(
        [
            self_query,
            self_key,
            self_value,
            self_output,
            cross_query,
            cross_key,
            cross_value,
            cross_output,
            gate_weight,
            linear_weight,
            fold_rows(down_weight, self_query.shape[0]),
            gain_columns((self_gain, cross_gain, feed_gain), jnp.bfloat16),
        ]
    )
    pack = gather_pack(pack)
    (
        self_query,
        self_key,
        self_value,
        self_output,
        cross_query,
        cross_key,
        cross_value,
        cross_output,
    ) = (pack[:, number * features : (number + 1) * features] for number in range(8))
    first = 8 * features
    gate_weight = pack[:, first : first + hidden]
    linear_weight = pack[:, first + hidden : first + 2 * hidden]
    first = first + 2 * hidden
    width = -(-(hidden // shards) // (features // shards)) * features
    down_weight = unfold_rows(
        pack[:, first : first + width].reshape(shards, -1, width), hidden // shards, features
    ).reshape(hidden, features)
    gains = pack[:, first + width : first + width + LANES].T
    self_gain, cross_gain, feed_gain = gains[0], gains[1], gains[2]
    tokens = hidden_in.shape[1]
    length = bucket_index.shape[0]
    head_count = bias_table.shape[1]
    buckets = bias_table.shape[0]
    query_first = lax.axis_index("ctx") * tokens
    bucket_rev = jnp.flip(jnp.concatenate([jnp.full((length,), -1, jnp.int32), bucket_index]))
    start_x = hidden_in[0].astype(jnp.float32)
    norm_one, normed_one, inverse_one = norm_forward(start_x, self_gain)
    projected = product(norm_one, pack[:, : 3 * features]).astype(jnp.bfloat16)
    query = projected[:, :features]
    encoder_local = encoder_states[0]
    cross_local = product(encoder_local, pack[:, 5 * features : 7 * features]).astype(jnp.bfloat16)
    encoder_rows = encoder_local.shape[0]
    blocks = lax.all_gather(
        jnp.concatenate([projected[:, features:], cross_local], axis=0), "ctx", axis=0, tiled=False
    )
    both = blocks[:, :tokens].reshape(length, 2 * features)
    keys, values = both[:, :features], both[:, features:]
    both = blocks[:, tokens:].reshape(-1, 2 * features)
    cross_keys, cross_values = both[:, :features], both[:, features:]
    empty_top = jnp.full((head_count, tokens), NEGATIVE, jnp.float32)
    empty_total = jnp.zeros((head_count, tokens), jnp.float32)
    empty_mixed = jnp.zeros((tokens, head_count, query.shape[1] // head_count), jnp.float32)
    forward_bound = partial(
        forward_step,
        query=query,
        query_first=query_first,
        bucket_rev=bucket_rev,
        bias_table=bias_table,
    )
    top, total, mixed = fold_blocks(
        forward_bound,
        (empty_top, empty_total, empty_mixed),
        (keys, values),
        jnp.int32(0),
    )
    attn = (mixed / total.T[:, :, None]).reshape(tokens, -1).astype(jnp.bfloat16)
    self_lse = (top + jnp.log(total)).T
    after_self = start_x + product(attn, self_output)
    norm_two, normed_two, inverse_two = norm_forward(after_self, cross_gain)
    cross_q = product(norm_two, cross_query).astype(jnp.bfloat16)
    cattn, cross_lse = plain_forward(cross_q, cross_keys, cross_values, head_count)
    after_cross = after_self + product(cattn, cross_output)
    norm_three, normed_three, inverse_three = norm_forward(after_cross, feed_gain)
    gate_pre = product(norm_three, gate_weight)
    linear_pre = product(norm_three, linear_weight)
    middle = geglu(gate_pre, linear_pre).astype(jnp.bfloat16)
    layer_out = (after_cross + product(middle, down_weight)).astype(jnp.bfloat16)
    grad_top = out_grad[0]
    grad_down = row_contract(middle, grad_top)
    grad_middle = col_contract(grad_top, down_weight)
    _, pull_back = jax.vjp(geglu, gate_pre, linear_pre)
    grad_gate_pre, grad_linear_pre = pull_back(grad_middle)
    gate_round = grad_gate_pre.astype(jnp.bfloat16)
    linear_round = grad_linear_pre.astype(jnp.bfloat16)
    grad_gate = row_contract(norm_three, gate_round)
    grad_linear = row_contract(norm_three, linear_round)
    back_three, grad_feed_gain = norm_backward(
        col_contract(gate_round, gate_weight) + col_contract(linear_round, linear_weight),
        normed_three,
        inverse_three,
        feed_gain,
    )
    grad_after_cross = grad_top.astype(jnp.float32) + back_three
    cross_round = grad_after_cross.astype(jnp.bfloat16)
    grad_cross_output = row_contract(cattn, cross_round)
    grad_cattn = col_contract(cross_round, cross_output).astype(jnp.bfloat16)
    grad_cq, cross_key_terms, cross_value_terms = plain_backward(
        cross_q, cross_keys, cross_values, cross_lse, cattn, grad_cattn, head_count
    )
    grad_cq = grad_cq.astype(jnp.bfloat16)
    grad_cross_query = row_contract(norm_two, grad_cq)
    back_two, grad_cross_gain = norm_backward(
        col_contract(grad_cq, cross_query), normed_two, inverse_two, cross_gain
    )
    grad_after_self = grad_after_cross + back_two
    self_round = grad_after_self.astype(jnp.bfloat16)
    grad_self_output = row_contract(attn, self_round)
    grad_attn = col_contract(self_round, self_output).astype(jnp.bfloat16)
    delta_rows = jnp.sum(
        by_heads(grad_attn, head_count).astype(jnp.float32)
        * by_heads(attn, head_count).astype(jnp.float32),
        axis=-1,
    )
    empty_rows = jnp.zeros((tokens, query.shape[1]), jnp.float32)
    empty_table = jnp.zeros((buckets, head_count), jnp.float32)
    partial_bound = partial(
        partial_step,
        query=query,
        grad_attn=grad_attn,
        lse_rows=self_lse,
        delta_rows=delta_rows,
        query_first=query_first,
        bucket_rev=bucket_rev,
        bias_table=bias_table,
    )
    empty_whole = jnp.zeros((length, query.shape[1]), jnp.float32)
    grad_query, key_terms, value_terms, table_part = fold_blocks(
        partial_bound,
        (empty_rows.reshape(tokens, head_count, -1), empty_whole, empty_whole, empty_table),
        (keys, values),
        jnp.int32(0),
    )
    terms = jnp.concatenate(
        [
            jnp.concatenate([key_terms, value_terms], axis=1).reshape(-1, tokens, 2 * features),
            jnp.concatenate([cross_key_terms, cross_value_terms], axis=1).reshape(
                -1, encoder_rows, 2 * features
            ),
        ],
        axis=1,
    ).astype(jnp.bfloat16)
    sums = lax.psum_scatter(terms, "ctx", scatter_dimension=0, tiled=False)
    cross_both = sums[tokens:]
    grad_cross_both = row_contract(encoder_local, cross_both)
    grad_cross_key, grad_cross_value = (
        grad_cross_both[:, :features],
        grad_cross_both[:, features:],
    )
    encoder_grad = col_contract(cross_both, pack[:, 5 * features : 7 * features])
    grad_q = grad_query.reshape(tokens, -1).astype(jnp.bfloat16)
    grad_projected = jnp.concatenate([grad_q, sums[:tokens]], axis=1)
    grad_self_projections = row_contract(norm_one, grad_projected)
    upstream_one = col_contract(grad_projected, pack[:, : 3 * features])
    back_one, grad_self_gain = norm_backward(upstream_one, normed_one, inverse_one, self_gain)
    input_grad = grad_after_self + back_one
    folded = fold_rows(grad_down.reshape(shards, -1, features), features // shards)
    parts = [
        grad_self_projections,
        grad_self_output,
        grad_cross_query,
        grad_cross_both,
        grad_cross_output,
        grad_gate,
        grad_linear,
        folded.reshape(features, width),
        gain_columns((grad_self_gain, grad_cross_gain, grad_feed_gain), jnp.bfloat16),
    ]
    terms = even_columns([member.astype(jnp.bfloat16) for member in parts])
    summed, grad_table = reduce_terms(terms, table_part)
    summed = summed.astype(jnp.float32)
    squares = [summed[:, number * features : (number + 1) * features] for number in range(8)]
    first = 8 * features
    down_first = first + 2 * hidden
    gain_first = down_first + width
    return (
        layer_out[None],
        input_grad[None],
        encoder_grad[None],
        grad_table,
        summed[:, gain_first],
        squares[0],
        squares[1],
        squares[2],
        squares[3],
        summed[:, gain_first + 1],
        squares[4],
        squares[5],
        squares[6],
        squares[7],
        summed[:, gain_first + 2],
        summed[:, first : first + hidden],
        summed[:, first + hidden : down_first],
        unfold_rows(summed[:, down_first:gain_first], hidden // shards, features),
    )


MESH = pl.DeviceIdType.MESH
FAR_BELOW = -1e30


def remote(source, target, send_sem, recv_sem, device):
    return pltpu.make_async_remote_copy(
        src_ref=source,
        dst_ref=target,
        send_sem=send_sem,
        recv_sem=recv_sem,
        device_id=device,
        device_id_type=MESH,
    )


class Place:
    def __init__(self, count, sends, recvs):
        self.count, self.sends, self.recvs = count, sends, recvs
        self.seq = lax.axis_index("seq")
        self.side, self.core = self.seq // 2, self.seq % 2
        self.depth, self.row = lax.axis_index("ctx"), lax.axis_index("fsdp")
        self.quarter = self.seq
        self.to_x = self.at(1 - self.side, self.core, self.depth, self.row)
        self.to_y = self.at(self.side, self.core, self.depth, 1 - self.row)
        self.to_core = self.at(self.side, 1 - self.core, self.depth, self.row)
        self.to_far = self.at(1 - self.side, 1 - self.core, self.depth, self.row)
        self.x_quarter = 2 * (1 - self.side) + self.core
        self.core_quarter = 2 * self.side + 1 - self.core
        self.far_quarter = 2 * (1 - self.side) + 1 - self.core
        self.used = 0

    def at(self, side, core, depth, row):
        return (side * 2 + core, depth, row)

    def at_depth(self, depth):
        return (self.seq, depth, self.row)

    def take(self, number):
        first = self.used
        self.used += number
        return first

    def link(self, source, target, index, device):
        return remote(source, target, self.sends.at[index], self.recvs.at[index], device)

    def others(self, step):
        middle = self.count // 2
        for at in sorted(range(self.count), key=lambda at: abs(2 * at - self.count + 1) + (at < middle) * 0.5):
            @pl.when(self.depth != at)
            def _():
                step(at)


class Gather:
    def __init__(self, here, piece, spread):
        self.here, self.piece, self.spread = here, piece, spread
        count = here.count
        self.z_base = here.take(count)
        self.y_base = here.take(count)
        if spread:
            self.x_base = here.take(2 * count)
            self.c_base = here.take(4 * count)

    def row(self, other):
        return 1 - self.here.row if other else self.here.row

    def z_copy(self, at):
        here = self.here
        held = self.piece(here.depth, here.row, here.quarter)
        return remote(
            held, held, here.sends.at[self.z_base + at], here.recvs.at[self.z_base + here.depth], here.at_depth(at)
        )

    def z_arrival(self, at):
        held = self.piece(at, self.here.row, self.here.quarter)
        return self.here.link(held, held, self.z_base + at, self.here.to_y)

    def y_copy(self, at, other):
        held = self.piece(at, self.row(other), self.here.quarter)
        return self.here.link(held, held, self.y_base + at, self.here.to_y)

    def x_copy(self, at, other, quarter):
        held = self.piece(at, self.row(other), quarter)
        return self.here.link(held, held, self.x_base + other * self.here.count + at, self.here.to_x)

    def c_copy(self, at, other, level, quarter):
        held = self.piece(at, self.row(other), quarter)
        return self.here.link(
            held, held, self.c_base + (2 * level + other) * self.here.count + at, self.here.to_core
        )

    def onward(self, at, other):
        if self.spread:
            self.x_copy(at, other, self.here.quarter).start()
            self.c_copy(at, other, 0, self.here.quarter).start()

    def begin(self):
        self.here.others(lambda at: self.z_copy(at).start())
        self.y_copy(self.here.depth, 0).start()

    def z_phase(self):
        def step(at):
            self.z_arrival(at).wait_recv()
            self.y_copy(at, 0).start()
            self.onward(at, 0)

        self.here.others(step)

    def y_phase(self):
        def step(at):
            self.y_copy(at, 1).wait_recv()
            self.onward(at, 1)

        step(self.here.depth)
        self.here.others(step)

    def members(self, step):
        step(self.here.depth, 1)
        for other in (0, 1):
            self.here.others(lambda at: step(at, other))

    def x_phase(self):
        def step(at, other):
            self.x_copy(at, other, self.here.x_quarter).wait_recv()
            self.c_copy(at, other, 1, self.here.x_quarter).start()

        self.members(step)

    def finish(self):
        def step(at, other):
            self.c_copy(at, other, 0, self.here.core_quarter).wait_recv()
            self.c_copy(at, other, 1, self.here.far_quarter).wait_recv()

        self.members(step)

    def drain(self):
        here = self.here
        here.others(lambda at: self.z_copy(at).wait_send())
        self.y_copy(here.depth, 0).wait_send()
        here.others(lambda at: self.y_copy(at, 0).wait_send())

        def step(at, other):
            self.x_copy(at, other, here.quarter).wait_send()
            self.c_copy(at, other, 0, here.quarter).wait_send()
            self.c_copy(at, other, 1, here.x_quarter).wait_send()

        if self.spread:
            self.members(step)


class Scatter:
    def __init__(self, here, total, height, from_y, from_z, out):
        self.here, self.total, self.height, self.out = here, total, height, out
        self.from_y, self.from_z = from_y, from_z
        self.y_base = here.take(here.count)
        self.z_base = here.take(here.count)
        self.out_base = here.take(3)

    def block(self, depth, row):
        first = pl.multiple_of((depth * 2 + row) * self.height, self.height)
        return self.total.at[pl.ds(first, self.height), :]

    def y_copy(self, depth):
        here = self.here
        return here.link(self.block(depth, 1 - here.row), self.from_y.at[depth], self.y_base + depth, here.to_y)

    def y_begin(self):
        self.here.others(lambda at: self.y_copy(at).start())
        self.y_copy(self.here.depth).start()

    def z_copy(self, at):
        here = self.here
        return remote(
            self.block(at, here.row), self.from_z.at[here.depth], here.sends.at[self.z_base + at],
            here.recvs.at[self.z_base + here.depth], here.at_depth(at),
        )

    def y_phase(self):
        def step(at):
            self.y_copy(at).wait_recv()
            block = self.block(at, self.here.row)
            block[...] = block[...] + self.from_y[at]
            self.z_copy(at).start()

        self.here.others(step)

    def z_phase(self):
        here = self.here
        self.y_copy(here.depth).wait_recv()
        self.from_z[here.depth] = self.block(here.depth, here.row)[...] + self.from_y[here.depth]

        def wait(at):
            held = self.from_z.at[at]
            here.link(held, held, self.z_base + at, here.to_y).wait_recv()

        here.others(wait)
        summed = self.from_z[0].astype(jnp.float32)
        for at in range(1, here.count):
            summed = summed + self.from_z[at].astype(jnp.float32)
        self.out(here.quarter)[...] = summed.astype(jnp.bfloat16)
        self.out_copy(0).start()
        self.out_copy(1).start()

    def out_copy(self, level, quarter=None):
        here = self.here
        quarter = (here.quarter, here.quarter, here.x_quarter)[level] if quarter is None else quarter
        held = self.out(quarter)
        return here.link(held, held, self.out_base + level, here.to_x if level == 0 else here.to_core)

    def out_phase(self):
        self.out_copy(0, self.here.x_quarter).wait_recv()
        self.out_copy(2).start()

    def finish(self):
        here = self.here
        self.out_copy(1, here.core_quarter).wait_recv()
        self.out_copy(2, here.far_quarter).wait_recv()
        for level in range(3):
            self.out_copy(level).wait_send()
        self.y_copy(here.depth).wait_send()
        here.others(lambda at: self.y_copy(at).wait_send())
        here.others(lambda at: self.z_copy(at).wait_send())


class SmallSum:
    def __init__(self, here, held, landing, depth_held):
        self.here, self.held, self.landing, self.depth_held = here, held, landing, depth_held
        self.base = here.take(3 + here.count)
        self.partners = [here.to_core, here.to_x, here.to_y]

    def copy(self, level):
        return self.here.link(self.held.at[level], self.landing.at[level], self.base + level, self.partners[level])

    def z_copy(self, at):
        here = self.here
        held = self.depth_held.at[here.depth]
        return remote(
            held, held, here.sends.at[self.base + 3 + at], here.recvs.at[self.base + 3 + here.depth], here.at_depth(at)
        )

    def begin(self):
        self.copy(0).start()

    def level(self, level):
        here = self.here
        self.copy(level).wait_recv()
        summed = self.held[level] + self.landing[level]
        if level < 2:
            self.held[level + 1] = summed
            self.copy(level + 1).start()
        else:
            self.depth_held[here.depth] = summed
            for at in range(here.count):
                @pl.when(here.depth != at)
                def _():
                    self.z_copy(at).start()

    def finish(self):
        here = self.here
        for at in range(here.count):
            @pl.when(here.depth != at)
            def _():
                held = self.depth_held.at[at]
                here.link(held, held, self.base + 3 + at, here.to_y).wait_recv()
        summed = self.depth_held[0]
        for at in range(1, here.count):
            summed = summed + self.depth_held[at]
        for level in range(3):
            self.copy(level).wait_send()
        for at in range(here.count):
            @pl.when(here.depth != at)
            def _():
                self.z_copy(at).wait_send()
        return summed


class Swap:
    def __init__(self, here, source, target):
        self.here, self.source, self.target = here, source, target
        self.base = here.take(here.count)

    def copy(self, at):
        here = self.here
        return remote(
            self.source(at), self.target(here.depth), here.sends.at[self.base + at],
            here.recvs.at[self.base + here.depth], here.at_depth(at),
        )

    def begin(self):
        self.here.others(lambda at: self.copy(at).start())

    def arrive(self):
        def wait(at):
            held = self.target(at)
            self.here.link(held, held, self.base + at, self.here.to_y).wait_recv()

        self.here.others(wait)

    def drain(self):
        self.here.others(lambda at: self.copy(at).wait_send())


class SeqGather:
    def __init__(self, here, held):
        self.here, self.held = here, held
        self.base = here.take(3)

    def copy(self, level, index=None):
        here = self.here
        index = (here.quarter, here.quarter, here.x_quarter)[level] if index is None else index
        held = self.held.at[index]
        return here.link(held, held, self.base + level, here.to_x if level == 0 else here.to_core)

    def begin(self):
        self.copy(0).start()
        self.copy(1).start()

    def relay(self):
        self.copy(0, self.here.x_quarter).wait_recv()
        self.copy(2).start()

    def arrive(self):
        self.copy(1, self.here.core_quarter).wait_recv()
        self.copy(2, self.here.far_quarter).wait_recv()

    def drain(self):
        for level in range(3):
            self.copy(level).wait_send()


class SeqSum:
    def __init__(self, here, held, landing):
        self.here, self.held, self.landing = here, held, landing
        self.base = here.take(3)

    def copy(self, level):
        here = self.here
        index = (here.far_quarter, here.core_quarter, here.x_quarter)[level]
        return here.link(
            self.held.at[index], self.landing.at[level], self.base + level, here.to_x if level == 2 else here.to_core
        )

    def begin(self):
        self.copy(0).start()
        self.copy(1).start()

    def relay(self):
        here = self.here
        self.copy(0).wait_recv()
        self.held[here.x_quarter] = self.held[here.x_quarter] + self.landing[0]
        self.copy(2).start()

    def arrive(self):
        here = self.here
        self.copy(1).wait_recv()
        self.copy(2).wait_recv()
        own = self.held[here.quarter].astype(jnp.float32)
        return own + self.landing[1].astype(jnp.float32) + self.landing[2].astype(jnp.float32)

    def drain(self):
        for level in range(3):
            self.copy(level).wait_send()


class SeqSwap:
    def __init__(self, here, heights, landing):
        self.here, self.heights, self.landing = here, heights, landing
        self.base = here.take(4)

    def held(self, member, source):
        return self.landing.at[source, pl.ds(0, self.heights[member]), :]

    def copy(self, member, block):
        here = self.here
        return remote(
            block, self.held(member, here.seq), here.sends.at[self.base + member], here.recvs.at[self.base + here.seq],
            (member, here.depth, here.row),
        )

    def begin(self, member, block):
        here = self.here

        @pl.when(here.seq != member)
        def _():
            self.copy(member, block).start()

        @pl.when(here.seq == member)
        def _():
            self.held(member, here.seq)[...] = block[...]

    def arrive(self):
        here = self.here
        for member in range(4):
            @pl.when(here.seq == member)
            def _():
                for source in range(4):
                    if source != member:
                        held = self.held(member, source)
                        here.link(held, held, self.base + source, here.to_core).wait_recv()

    def drain(self):
        here = self.here
        for member in range(4):
            @pl.when(here.seq != member)
            def _():
                held = self.held(member, member)
                here.link(held, held, self.base + member, here.to_core).wait_send()


def tiles(total, width, body):
    def step(number, carry):
        body(pl.ds(pl.multiple_of(number * width, width), width))
        return carry

    lax.fori_loop(0, total // width, step, 0)


def times(left, right, left_dim, right_dim):
    return lax.dot_general(
        left, right, (((left_dim,), (right_dim,)), ((), ())), preferred_element_type=jnp.float32
    )


def normed_of(values):
    inverse = lax.rsqrt(jnp.mean(values * values, axis=-1, keepdims=True) + EPSILON)
    return values * inverse, inverse


def norm_back(upstream, values, gain):
    normed, inverse = normed_of(values)
    grad_gain = jnp.sum(upstream * normed, axis=0, keepdims=True)
    grad_normed = upstream * gain
    mean = jnp.mean(grad_normed * normed, axis=-1, keepdims=True)
    return inverse * (grad_normed - normed * mean), grad_gain


BF = jnp.bfloat16
F32 = jnp.float32


class Names:
    pass


def layer_kernel(sizes, names, *refs):
    r = Names()
    for name, ref in zip(names, refs):
        setattr(r, name, ref)
    count, tokens, features, enc, heads, quarter, rows, tall = sizes
    head = features // heads
    mine = heads // count
    width = mine * head
    length = count * tokens
    states = count * enc
    here = Place(count, r.sends, r.recvs)
    seq, depth, row = here.seq, here.depth, here.row

    own = pl.multiple_of((depth * 2 + row) * rows, rows)
    own_tall = pl.multiple_of((depth * 2 + row) * tall, tall)
    squares = [getattr(r, f"square{number}") for number in range(8)]
    local = [
        pltpu.make_async_copy(squares[number], r.weights.at[number, pl.ds(own, rows), :], r.local.at[number])
        for number in range(8)
    ]
    local.append(
        pltpu.make_async_copy(
            r.down.at[pl.ds(pl.multiple_of(seq * tall, tall), tall), :], r.down_quarter.at[pl.ds(own_tall, tall), :],
            r.local.at[8],
        )
    )
    for copy in local:
        copy.start()

    def weight_piece(chunk):
        return lambda at, at_row, quarter_at: r.weights.at[
            4 * chunk + quarter_at, pl.ds(pl.multiple_of((at * 2 + at_row) * rows, rows), rows), :
        ]

    def quarter_piece(whole, height):
        return lambda at, at_row, quarter_at: whole.at[
            pl.ds(pl.multiple_of((at * 2 + at_row) * height, height), height), :
        ]

    gathers = [
        Gather(here, weight_piece(0), True),
        Gather(here, weight_piece(1), True),
        Gather(here, quarter_piece(r.gate_quarter, rows), False),
        Gather(here, quarter_piece(r.linear_quarter, rows), False),
        Gather(here, quarter_piece(r.down_quarter, tall), False),
    ]
    mates = []
    for far in range(count):
        for flip in (0, 1):
            if far or flip:
                mates.append((lax.rem(depth + far, count), row if flip == 0 else 1 - row))
    partners = [(seq,) + mate for mate in mates] + [here.to_x, here.to_core, here.to_far]
    barrier = pltpu.get_barrier_semaphore()
    for partner in partners:
        pl.semaphore_signal(barrier, inc=1, device_id=partner, device_id_type=MESH)
    pl.semaphore_wait(barrier, len(partners))

    gain_base = here.take(2 * count - 1)
    r.all_gains[depth * 2 + row] = r.gains[...]
    gain_sends = [
        here.link(r.all_gains.at[depth * 2 + row], r.all_gains.at[depth * 2 + row], gain_base + number, (seq,) + mate)
        for number, mate in enumerate(mates)
    ]
    for copy in gain_sends:
        copy.start()
    for number in range(4):
        local[number].wait()
    gathers[0].begin()
    for number in range(4, 9):
        local[number].wait()
    gathers[1].begin()

    r.grads_in[seq] = r.out_grad[...]
    grads_in = SeqGather(here, r.grads_in)
    long = (tokens,) * 3 + (enc,)
    lefts = [SeqSwap(here, long, r.left.at[0]), SeqSwap(here, long[::-1], r.left.at[1])]
    rights = [SeqSwap(here, long, r.right.at[0]), SeqSwap(here, long[::-1], r.right.at[1])]

    for at in range(4):
        @pl.when(seq == at)
        def _():
            for source, whole in ((r.gate, r.gate_quarter), (r.linear, r.linear_quarter)):
                span = 4 * tall
                whole[pl.ds(own, rows), :] = jnp.concatenate(
                    [source[:, number * span + at * tall : number * span + (at + 1) * tall] for number in range(2 * count)],
                    axis=1,
                )

    key_at = lax.broadcasted_iota(jnp.int32, (tokens, length), 0)
    query_at = lax.broadcasted_iota(jnp.int32, (tokens, length), 1)
    for number in range(mine):
        strip = jnp.broadcast_to(r.bias[number : number + 1, :], (tokens, length))
        step = 1
        while step < tokens:
            strip = jnp.where((key_at // step) % 2 == 1, pltpu.roll(strip, step, 1), strip)
            step *= 2
        r.strip[number] = jnp.where(query_at >= key_at, strip, FAR_BELOW)

    for chunk in (2, 3, 4):
        gathers[chunk].begin()
    gathers[0].z_phase()
    gathers[0].y_phase()

    for far in range(count):
        for flip in (0, 1):
            if far or flip:
                source = lax.rem(depth + count - far, count) * 2 + (row if flip == 0 else 1 - row)
                held = r.all_gains.at[source]
                here.link(held, held, gain_base + far * 2 + flip - 1, here.to_core).wait_recv()
    lane = lax.broadcasted_iota(jnp.int32, (LANES, features), 0)
    column = lax.broadcasted_iota(jnp.int32, (LANES, features), 1)
    gain_rows = jnp.zeros((16, features), F32)
    for number in range(2 * count):
        select = jnp.logical_and(column - number * rows == lane, lane < rows)
        gain_rows = gain_rows + times(r.all_gains[number], select.astype(F32).astype(BF), 1, 0)
    r.gain_rows[...] = gain_rows

    def gain(number):
        return r.gain_rows[number : number + 1, :]

    x0 = r.hidden[...].astype(F32)
    h1 = (normed_of(x0)[0] * gain(0)).astype(BF)
    r.h1[...] = h1

    gathers[1].z_phase()
    gathers[0].x_phase()
    gathers[0].finish()

    def head_rows(at):
        return pl.ds(pl.multiple_of(at * width, width), width)

    def token_lanes(at):
        return pl.ds(pl.multiple_of(at * tokens, tokens), tokens)

    def own_block(target, source):
        target[...] = source[...]

    qkv = [
        Swap(
            here, lambda at, number=number: r.qkv_t.at[number, head_rows(at), :],
            lambda at, number=number: r.qkv_h.at[number, :, token_lanes(at)],
        )
        for number in range(3)
    ]
    for number in range(3):
        def project(at, number=number):
            r.qkv_t[number, at, :] = times(r.h1[...], r.weights[number, :, at], 1, 0).astype(BF).T

        tiles(features, 256, project)
        qkv[number].begin()
    own_block(r.qkv_h.at[:, :, token_lanes(depth)], r.qkv_t.at[:, head_rows(depth), :])

    gathers[1].y_phase()
    grads_in.begin()
    gathers[1].x_phase()
    gathers[1].finish()
    for member in range(3):
        lefts[0].begin(member, r.h1)
    lefts[0].begin(3, r.encoder)
    lefts[1].begin(0, r.encoder)

    for number in range(2):
        def project(at, number=number):
            r.cross_kv[number, pl.ds(pl.multiple_of(depth * enc, enc), enc), at] = times(
                r.encoder[...], r.weights[3 + number, :, at], 1, 0
            ).astype(BF)

        tiles(features, 256, project)

    def enc_rows(at):
        return pl.ds(pl.multiple_of(at * enc, enc), enc)

    own_kv = r.cross_kv.at[:, enc_rows(depth), :]
    cross = Swap(here, lambda at: own_kv, lambda at: r.cross_kv.at[:, enc_rows(at), :])
    cross.begin()

    for work in qkv:
        work.arrive()

    def block_scores(number, block):
        keys = (block + 1) * tokens
        at = pl.ds(pl.multiple_of(number * head, head), head)
        query = r.qkv_h[0, at, block * tokens : keys]
        scores = times(r.qkv_h[1, at, :keys], query, 0, 0)
        bias = jnp.concatenate(
            [r.strip[number, :, (block - key) * tokens : (block - key + 1) * tokens] for key in range(block + 1)], axis=0
        )
        return scores + bias, at, keys, query

    def self_forward(number, carry):
        for block in range(count):
            scores, at, keys, _ = block_scores(number, block)
            top = jnp.max(scores, axis=0, keepdims=True)
            weights = jnp.exp(scores - top)
            total = jnp.sum(weights, axis=0, keepdims=True)
            mixed = times(r.qkv_h[2, at, :keys], weights.astype(BF), 1, 0)
            span = slice(block * tokens, keys)
            r.attn_h[at, span] = (mixed / total).astype(BF)
            r.lse[number, :, span] = top + jnp.log(total)
        return carry

    lax.fori_loop(0, mine, self_forward, 0)
    attn = Swap(here, lambda at: r.attn_h.at[:, token_lanes(at)], lambda at: r.attn_t.at[head_rows(at), :])
    attn.begin()
    own_block(r.attn_t.at[head_rows(depth), :], r.attn_h.at[:, token_lanes(depth)])

    for chunk in (2, 3, 4):
        gathers[chunk].z_phase()
    grads_in.relay()
    cross.arrive()
    for number in range(2):
        r.cross_t[number] = r.cross_kv[number].T
    attn.arrive()
    r.attn[...] = r.attn_t[...].T
    lefts[1].begin(1, r.attn)

    def after(at):
        r.x1[:, at] = r.hidden[:, at].astype(F32) + times(r.attn[...], r.weights[5, :, at], 1, 0)

    tiles(features, 256, after)
    h2 = (normed_of(r.x1[...])[0] * gain(1)).astype(BF)
    r.h2[...] = h2
    lefts[1].begin(2, r.h2)

    def project(at):
        r.cq_t[at, :] = times(r.h2[...], r.weights[6, :, at], 1, 0).astype(BF).T

    tiles(features, 256, project)

    def head_at(number):
        return pl.ds(pl.multiple_of(number * head, head), head)

    def cross_forward(number, carry):
        at = head_at(number)
        scores = times(r.cross_t[0, at, :], r.cq_t[at, :], 0, 0)
        top = jnp.max(scores, axis=0, keepdims=True)
        weights = jnp.exp(scores - top)
        total = jnp.sum(weights, axis=0, keepdims=True)
        mixed = times(r.cross_t[1, at, :], weights.astype(BF), 1, 0)
        r.cattn_t[at, :] = (mixed / total).astype(BF)
        r.clse[number] = top + jnp.log(total)
        return carry

    lax.fori_loop(0, heads, cross_forward, 0)
    r.cattn[...] = r.cattn_t[...].T
    lefts[1].begin(3, r.cattn)

    def after(at):
        r.x2[:, at] = r.x1[:, at] + times(r.cattn[...], r.weights[7, :, at], 1, 0)

    tiles(features, 256, after)
    r.h3[seq] = (normed_of(r.x2[...])[0] * gain(2)).astype(BF)
    h3 = SeqGather(here, r.h3)
    h3.begin()
    gathers[2].y_phase()
    gathers[3].y_phase()
    h3.relay()
    gathers[4].y_phase()
    grads_in.arrive()
    h3.arrive()

    group = 4 * tokens
    hidden_rows = r.h3[...].reshape(group, features)
    grad_rows = r.grads_in[...].reshape(group, features)
    root = math.sqrt(2.0 / math.pi)

    def feed(at):
        gate = times(hidden_rows, r.gate_quarter[:, at], 1, 0)
        linear = times(hidden_rows, r.linear_quarter[:, at], 1, 0)
        grad = times(grad_rows, r.down_quarter[at, :], 1, 1)
        square = gate * gate
        bent = jnp.tanh(root * gate * (1.0 + 0.044715 * square))
        half = 0.5 * (1.0 + bent)
        curve = gate * half
        slope = half + 0.5 * gate * (1.0 - bent * bent) * (root * (1.0 + 3 * 0.044715 * square))
        r.middle[:, at] = (curve * linear).astype(BF)
        r.grad_gate[:, at] = (grad * linear * slope).astype(BF)
        r.grad_linear[:, at] = (grad * curve).astype(BF)

    tiles(quarter, 256, feed)

    def back(at):
        upstream = times(r.grad_gate[...], r.gate_quarter[at, :], 1, 1) + times(
            r.grad_linear[...], r.linear_quarter[at, :], 1, 1
        )
        r.gh3[:, :, at] = upstream.reshape(4, tokens, -1).astype(BF)

    tiles(features, 256, back)
    gh3 = SeqSum(here, r.gh3, r.gh3_in)
    gh3.begin()

    def forth(at):
        r.lout[:, :, at] = times(r.middle[...], r.down_quarter[:, at], 1, 0).reshape(4, tokens, -1).astype(BF)

    tiles(features, 256, forth)
    lout = SeqSum(here, r.lout, r.lout_in)
    gh3.relay()
    lout.begin()

    def down_terms(at):
        r.down_terms[at, :] = times(r.middle[:, at], grad_rows, 0, 0).astype(BF)

    tiles(quarter, 256, down_terms)
    feeds = [
        Scatter(here, r.down_terms, tall, r.down_y, r.down_z, lambda q: r.out_down.at[q]),
        Scatter(here, r.gate_terms, rows, r.gate_y, r.gate_z, lambda q: r.out_gate.at[q]),
        Scatter(here, r.linear_terms, rows, r.linear_y, r.linear_z, lambda q: r.out_linear.at[q]),
    ]
    feeds[0].y_begin()

    def gate_terms(at):
        r.gate_terms[at, :] = times(hidden_of(at), r.grad_gate[...], 0, 0).astype(BF)

    def linear_terms(at):
        r.linear_terms[at, :] = times(hidden_of(at), r.grad_linear[...], 0, 0).astype(BF)

    def hidden_of(at):
        return r.h3[:, :, at].reshape(group, -1)

    tiles(features, 256, gate_terms)
    feeds[1].y_begin()
    lout.relay()
    tiles(features, 256, linear_terms)
    feeds[2].y_begin()

    grad_x2, gain_three = norm_back(gh3.arrive(), r.x2[...], gain(2))
    grad_x2 = r.out_grad[...].astype(F32) + grad_x2
    r.gx[...] = grad_x2
    rounded = grad_x2.astype(BF)
    r.rounded[...] = rounded
    rights[1].begin(3, r.rounded)

    def pull(at):
        r.grad_t[at, :] = times(r.rounded[...], r.weights[7, at, :], 1, 1).astype(BF).T

    tiles(features, 256, pull)

    def cross_backward(number, carry):
        at = head_at(number)
        grad = r.grad_t[at, :]
        delta = jnp.sum(grad.astype(F32) * r.cattn_t[at, :].astype(F32), axis=0, keepdims=True)
        query, keys = r.cq_t[at, :], r.cross_t[0, at, :]
        probs = jnp.exp(times(keys, query, 0, 0) - r.clse[number])
        terms = (probs * (times(r.cross_t[1, at, :], grad, 0, 0) - delta)).astype(BF)
        r.gq_t[at, :] = times(keys, terms, 1, 0).astype(BF)
        r.cross_terms_t[0, at, :] = times(query, terms, 1, 1)
        r.cross_terms_t[1, at, :] = times(grad, probs.astype(BF), 1, 1)
        return carry

    lax.fori_loop(0, heads, cross_backward, 0)
    for number in range(2):
        r.cross_terms[number] = r.cross_terms_t[number].T.astype(BF)
    cross_terms = Swap(here, lambda at: r.cross_terms.at[:, enc_rows(at), :], lambda at: r.cross_in.at[at])
    cross_terms.begin()
    r.cross_in[depth] = r.cross_terms[:, enc_rows(depth), :]
    r.gq[...] = r.gq_t[...].T
    rights[1].begin(2, r.gq)

    spread = [
        Scatter(
            here, r.terms.at[chunk], rows, r.terms_y.at[chunk], r.terms_z.at[chunk],
            lambda q, chunk=chunk: r.out_squares.at[4 * chunk + q],
        )
        for chunk in range(2)
    ]

    def square_terms(chunk):
        lefts[chunk].arrive()
        rights[chunk].arrive()
        heights = lefts[chunk].heights
        short = heights.index(enc)
        for which, height in ((seq != short, tokens), (seq == short, enc)):
            @pl.when(which)
            def _():
                def body(at):
                    left = r.left[chunk, :, :height, at].reshape(4 * height, -1)
                    right = r.right[chunk, :, :height, :].reshape(4 * height, features)
                    r.terms[chunk, at, :] = times(left, right, 0, 0).astype(BF)

                tiles(features, 256, body)

        spread[chunk].y_begin()

    feeds[0].y_phase()

    def pull(at):
        r.up[:, at] = times(r.gq[...], r.weights[6, at, :], 1, 1)

    tiles(features, 256, pull)
    grad_x1, gain_two = norm_back(r.up[...], r.x1[...], gain(1))
    grad_x1 = r.gx[...] + grad_x1
    r.gx[...] = grad_x1
    r.rounded_one[...] = grad_x1.astype(BF)
    rights[1].begin(1, r.rounded_one)

    def pull(at):
        r.grad_t[at, :] = times(r.rounded_one[...], r.weights[5, at, :], 1, 1).astype(BF).T

    tiles(features, 256, pull)
    grad_attn = Swap(here, lambda at: r.grad_t.at[head_rows(at), :], lambda at: r.grad_h.at[:, token_lanes(at)])
    grad_attn.begin()
    own_block(r.grad_h.at[:, token_lanes(depth)], r.grad_t.at[head_rows(depth), :])

    feeds[1].y_phase()
    feeds[0].z_phase()
    cross_terms.arrive()
    summed = r.cross_in[0].astype(F32)
    for at in range(1, count):
        summed = summed + r.cross_in[at].astype(F32)
    r.cross_sum[...] = summed.astype(BF)
    rights[0].begin(3, r.cross_sum.at[0])
    rights[1].begin(0, r.cross_sum.at[1])
    square_terms(1)
    feeds[2].y_phase()
    r.layer_out[...] = (r.x2[...] + lout.arrive()).astype(BF)

    def encoder_back(at):
        r.encoder_grad[:, at] = times(r.cross_sum[0], r.weights[3, at, :], 1, 1) + times(
            r.cross_sum[1], r.weights[4, at, :], 1, 1
        )

    tiles(features, 256, encoder_back)
    feeds[1].z_phase()
    feeds[0].out_phase()
    spread[1].y_phase()

    grad_attn.arrive()

    def self_backward(number, carry):
        at = head_at(number)
        r.dkv[...] = jnp.zeros_like(r.dkv)
        r.strip_sum[...] = jnp.zeros_like(r.strip_sum)
        for block in range(count):
            scores, _, keys, query = block_scores(number, block)
            span = slice(block * tokens, keys)
            grad = r.grad_h[at, span]
            delta = jnp.sum(grad.astype(F32) * r.attn_h[at, span].astype(F32), axis=0, keepdims=True)
            probs = jnp.exp(scores - r.lse[number, :, span])
            grad_scores = probs * (times(r.qkv_h[2, at, :keys], grad, 0, 0) - delta)
            terms = grad_scores.astype(BF)
            r.dqkv_h[0, at, span] = times(r.qkv_h[1, at, :keys], terms, 1, 0).astype(BF)
            r.dkv[0, :, :keys] += times(query, terms, 1, 1)
            r.dkv[1, :, :keys] += times(grad, probs.astype(BF), 1, 1)
            for key in range(block + 1):
                lanes = slice((block - key) * tokens, (block - key + 1) * tokens)
                r.strip_sum[:, lanes] += grad_scores[key * tokens : (key + 1) * tokens, :]
        r.dqkv_h[1, at, :] = r.dkv[0].astype(BF)
        r.dqkv_h[2, at, :] = r.dkv[1].astype(BF)
        strip = r.strip_sum[...]
        step = 1
        while step < tokens:
            strip = jnp.where((key_at // step) % 2 == 1, pltpu.roll(strip, length - step, 1), strip)
            step *= 2
        r.small[0, pl.ds(mine * depth + number, 1), :length] = jnp.sum(strip, axis=0, keepdims=True)
        return carry

    r.small[0] = jnp.zeros(r.small.shape[1:], F32)
    lax.fori_loop(0, mine, self_backward, 0)
    dqkv = [
        Swap(
            here, lambda at, number=number: r.dqkv_h.at[number, :, token_lanes(at)],
            lambda at, number=number: r.dqkv_t.at[number, head_rows(at), :],
        )
        for number in range(3)
    ]
    for work in dqkv:
        work.begin()
    own_block(r.dqkv_t.at[:, head_rows(depth), :], r.dqkv_h.at[:, :, token_lanes(depth)])
    feeds[2].z_phase()
    feeds[1].out_phase()
    spread[1].z_phase()
    for work in gathers:
        work.drain()
    for copy in gain_sends:
        copy.wait_send()
    for work in (*lefts, *qkv, attn, cross, cross_terms, grad_attn, h3, grads_in, gh3, lout):
        work.drain()
    for number in range(3):
        dqkv[number].arrive()
        r.dqkv[number] = r.dqkv_t[number].T
        rights[0].begin(number, r.dqkv.at[number])

    def pull(at):
        r.up[:, at] = (
            times(r.dqkv[0], r.weights[0, at, :], 1, 1)
            + times(r.dqkv[1], r.weights[1, at, :], 1, 1)
            + times(r.dqkv[2], r.weights[2, at, :], 1, 1)
        )

    tiles(features, 256, pull)
    grad_x0, gain_one = norm_back(r.up[...], r.hidden[...].astype(F32), gain(0))
    r.input_grad[...] = r.gx[...] + grad_x0
    for number, value in enumerate((gain_one, gain_two, gain_three)):
        r.small[0, heads + number : heads + number + 1, :] = value
    small = SmallSum(here, r.small, r.small_in, r.small_depth)
    small.begin()
    feeds[2].out_phase()
    spread[1].out_phase()
    small.level(0)
    square_terms(0)
    small.level(1)
    spread[0].y_phase()
    for work in feeds:
        work.finish()
    for source, whole in ((r.out_gate, r.whole_gate), (r.out_linear, r.whole_linear)):
        held = [source[at] for at in range(4)]
        whole[...] = jnp.concatenate(
            [held[at][:, number * tall : (number + 1) * tall] for number in range(2 * count) for at in range(4)], axis=1
        )
    small.level(2)
    spread[0].z_phase()
    for work in (*rights, *dqkv):
        work.drain()
    spread[1].finish()
    r.small_out[...] = small.finish()
    spread[0].out_phase()
    spread[0].finish()


def run_layer(hidden, encoder, out_grad, bias, squares, gate, linear, down, gains):
    count = lax.axis_size("ctx")
    tokens, features = hidden.shape
    enc = encoder.shape[0]
    rows, hidden_units = gate.shape
    heads = features // 64
    quarter = hidden_units // 4
    tall = down.shape[0] // 4
    length, states = count * tokens, count * enc
    mine = heads // count
    width = features // count
    head = features // heads
    small = (-(-(heads + 3) // 8) * 8, features)
    used = 96 * count
    vmem = pl.BlockSpec(memory_space=pltpu.VMEM)
    held = pl.BlockSpec(memory_space=pl.ANY)
    inputs = dict(
        hidden=(hidden, vmem),
        encoder=(encoder, vmem),
        out_grad=(out_grad, vmem),
        bias=(bias, vmem),
        **{f"square{number}": (member, held) for number, member in enumerate(squares)},
        gate=(gate, vmem),
        linear=(linear, vmem),
        down=(down, held),
        gains=(gains, vmem),
    )
    outputs = dict(
        layer_out=((tokens, features), BF),
        input_grad=((tokens, features), F32),
        encoder_grad=((enc, features), F32),
        small_out=(small, F32),
        out_squares=((8, rows, features), BF),
        out_down=((4, tall, features), BF),
        whole_gate=((rows, hidden_units), BF),
        whole_linear=((rows, hidden_units), BF),
    )
    square = (features, features)
    near = (count,)
    scratch = dict(
        weights=((8,) + square, BF),
        gate_quarter=((features, quarter), BF),
        linear_quarter=((features, quarter), BF),
        down_quarter=((quarter, features), BF),
        all_gains=((2 * count,) + gains.shape, BF),
        gain_rows=((16, features), F32),
        strip=((mine, tokens, length), F32),
        strip_sum=((tokens, length), F32),
        h1=((tokens, features), BF),
        h2=((tokens, features), BF),
        qkv_t=((3, features, tokens), BF),
        qkv_h=((3, width, length), BF),
        attn_h=((width, length), BF),
        attn_t=((features, tokens), BF),
        attn=((tokens, features), BF),
        lse=((mine, 1, length), F32),
        cross_kv=((2, states, features), BF),
        cross_t=((2, features, states), BF),
        cq_t=((features, tokens), BF),
        cattn_t=((features, tokens), BF),
        clse=((heads, 1, tokens), F32),
        x1=((tokens, features), F32),
        x2=((tokens, features), F32),
        gx=((tokens, features), F32),
        up=((tokens, features), F32),
        rounded=((tokens, features), BF),
        h3=((4, tokens, features), BF),
        grads_in=((4, tokens, features), BF),
        middle=((4 * tokens, quarter), BF),
        grad_gate=((4 * tokens, quarter), BF),
        grad_linear=((4 * tokens, quarter), BF),
        gh3=((4, tokens, features), BF),
        gh3_in=((3, tokens, features), BF),
        lout=((4, tokens, features), BF),
        lout_in=((3, tokens, features), BF),
        down_terms=((quarter, features), BF),
        gate_terms=((features, quarter), BF),
        linear_terms=((features, quarter), BF),
        down_y=((count, tall, features), BF),
        gate_y=((count, rows, quarter), BF),
        linear_y=((count, rows, quarter), BF),
        down_z=(near + (tall, features), BF),
        gate_z=(near + (rows, quarter), BF),
        linear_z=(near + (rows, quarter), BF),
        out_gate=((4, rows, quarter), BF),
        out_linear=((4, rows, quarter), BF),
        grad_t=((features, tokens), BF),
        gq_t=((features, tokens), BF),
        gq=((tokens, features), BF),
        cross_terms_t=((2, features, states), F32),
        cross_terms=((2, states, features), BF),
        cross_in=((count, 2, enc, features), BF),
        cross_sum=((2, enc, features), BF),
        terms=((2,) + square, BF),
        left=((2, 4, tokens, features), BF),
        right=((2, 4, tokens, features), BF),
        rounded_one=((tokens, features), BF),
        cattn=((tokens, features), BF),
        terms_y=((2, count, rows, features), BF),
        terms_z=((2,) + near + (rows, features), BF),
        grad_h=((width, length), BF),
        dkv=((2, head, length), F32),
        dqkv_h=((3, width, length), BF),
        dqkv_t=((3, features, tokens), BF),
        dqkv=((3, tokens, features), BF),
        small=((3,) + small, F32),
        small_in=((3,) + small, F32),
        small_depth=((count,) + small, F32),
    )
    names = list(inputs) + list(outputs) + list(scratch) + ["local", "sends", "recvs"]
    return pl.pallas_call(
        partial(layer_kernel, (count, tokens, features, enc, heads, quarter, rows, tall), names),
        out_shape=tuple(jax.ShapeDtypeStruct(shape, kind) for shape, kind in outputs.values()),
        in_specs=[spec for _, spec in inputs.values()],
        out_specs=[vmem] * len(outputs),
        scratch_shapes=[
            *(pltpu.VMEM(shape, kind) for shape, kind in scratch.values()),
            pltpu.SemaphoreType.DMA((9,)),
            pltpu.SemaphoreType.DMA((used,)),
            pltpu.SemaphoreType.DMA((used,)),
        ],
        compiler_params=pltpu.CompilerParams(
            collective_id=0, has_side_effects=True, vmem_limit_bytes=60 << 20
        ),
        cost_estimate=pl.CostEstimate(flops=8 * 10**9, bytes_accessed=10**7, transcendentals=10**6),
        name="layer",
    )(*(member for member, _ in inputs.values()))


def per_device_whole(
    hidden_in,
    encoder_states,
    out_grad,
    bucket_index,
    bias_table,
    self_gain,
    self_query,
    self_key,
    self_value,
    self_output,
    cross_gain,
    cross_query,
    cross_key,
    cross_value,
    cross_output,
    feed_gain,
    gate_weight,
    linear_weight,
    down_weight,
):
    count = lax.axis_size("ctx")
    rows, features = self_query.shape
    buckets, heads = bias_table.shape
    length = bucket_index.shape[0]
    mine = heads // count
    onehot = (bucket_index[:, None] == jnp.arange(buckets, dtype=jnp.int32)[None, :]).astype(jnp.float32)
    own_table = lax.dynamic_slice_in_dim(bias_table, lax.axis_index("ctx") * mine, mine, 1)
    own_table = jnp.pad(own_table, ((0, 0), (0, -mine % 8)))
    bias = jnp.dot(onehot, own_table, precision=HIGHEST).T
    gains = jnp.pad(jnp.stack([self_gain, cross_gain, feed_gain]), ((0, 13), (0, LANES - rows)))
    layer_out, input_grad, encoder_grad, small, squares, down, gate, linear = run_layer(
        hidden_in[0],
        encoder_states[0],
        out_grad[0],
        bias,
        (self_query, self_key, self_value, cross_key, cross_value, self_output, cross_query, cross_output),
        gate_weight,
        linear_weight,
        down_weight,
        gains,
    )
    grad_table = jnp.dot(onehot.T, small[:heads, :length].T, precision=HIGHEST)
    shard = lax.axis_index(("ctx", "fsdp"))
    gain_sums = lax.dynamic_slice_in_dim(small[heads : heads + 3], shard * rows, rows, 1)
    squares = squares.astype(jnp.float32)
    return (
        layer_out[None],
        input_grad[None],
        encoder_grad[None],
        grad_table,
        gain_sums[0],
        squares[0],
        squares[1],
        squares[2],
        squares[5],
        gain_sums[1],
        squares[6],
        squares[3],
        squares[4],
        squares[7],
        gain_sums[2],
        gate.astype(jnp.float32),
        linear.astype(jnp.float32),
        down.reshape(-1, features).astype(jnp.float32),
    )


def fits(mesh):
    return mesh.shape["seq"] == 4 and mesh.shape["fsdp"] == 2 and mesh.shape["ctx"] <= 4


def solution(mesh):
    return jax.shard_map(
        per_device_whole if fits(mesh) else per_device,
        mesh=mesh,
        in_specs=(
            P(("seq", "fsdp"), "ctx", None),
            P(("seq", "fsdp"), "ctx", None),
            P(("seq", "fsdp"), "ctx", None),
            P(),
            P(),
            P(("ctx", "fsdp")),
            P(("ctx", "fsdp"), None),
            P(("ctx", "fsdp"), None),
            P(("ctx", "fsdp"), None),
            P(("ctx", "fsdp"), None),
            P(("ctx", "fsdp")),
            P(("ctx", "fsdp"), None),
            P(("ctx", "fsdp"), None),
            P(("ctx", "fsdp"), None),
            P(("ctx", "fsdp"), None),
            P(("ctx", "fsdp")),
            P(("ctx", "fsdp"), None),
            P(("ctx", "fsdp"), None),
            P(("ctx", "fsdp"), None),
        ),
        out_specs=(
            P(("seq", "fsdp"), "ctx", None),
            P(("seq", "fsdp"), "ctx", None),
            P(("seq", "fsdp"), "ctx", None),
            P(),
            P(("ctx", "fsdp")),
            P(("ctx", "fsdp"), None),
            P(("ctx", "fsdp"), None),
            P(("ctx", "fsdp"), None),
            P(("ctx", "fsdp"), None),
            P(("ctx", "fsdp")),
            P(("ctx", "fsdp"), None),
            P(("ctx", "fsdp"), None),
            P(("ctx", "fsdp"), None),
            P(("ctx", "fsdp"), None),
            P(("ctx", "fsdp")),
            P(("ctx", "fsdp"), None),
            P(("ctx", "fsdp"), None),
            P(("ctx", "fsdp"), None),
        ),
        check_vma=False,
    )
```

```python
from functools import partial
import math

import jax
import jax.numpy as jnp
from jax import lax
from jax.experimental import pallas as pl
from jax.experimental.pallas import tpu as pltpu
from jax.sharding import PartitionSpec as P

EPSILON = 1e-06
NEGATIVE = -1e30
HIGHEST = lax.Precision.HIGHEST


LANES = 128


def fold_rows(rows, height):
    count = -(-rows.shape[-2] // height)
    short = count * height - rows.shape[-2]
    padding = [(0, 0)] * (rows.ndim - 2) + [(0, short), (0, 0)]
    padded = jnp.pad(rows, padding)
    return jnp.concatenate(
        [padded[..., number * height : (number + 1) * height, :] for number in range(count)],
        axis=-1,
    )


def unfold_rows(columns, row_count, features):
    count = columns.shape[-1] // features
    stacked = jnp.concatenate(
        [columns[..., number * features : (number + 1) * features] for number in range(count)],
        axis=-2,
    )
    return stacked[..., :row_count, :]


def gain_columns(gains, dtype):
    columns = jnp.stack([member.astype(dtype) for member in gains], axis=1)
    return jnp.pad(columns, ((0, 0), (0, LANES - columns.shape[1])))


def product(left, right):
    return jnp.dot(left, right, preferred_element_type=jnp.float32)


def row_contract(left, right):
    return lax.dot_general(
        left, right, (((0,), (0,)), ((), ())), preferred_element_type=jnp.float32
    )


def col_contract(left, right):
    return lax.dot_general(
        left, right, (((1,), (1,)), ((), ())), preferred_element_type=jnp.float32
    )


def norm_forward(values, gain):
    inverse = lax.rsqrt(jnp.mean(values * values, axis=-1, keepdims=True) + EPSILON)
    normed = values * inverse
    return ((normed * gain.astype(jnp.float32)).astype(jnp.bfloat16), normed, inverse)


def norm_backward(upstream, normed, inverse, gain):
    grad_gain = jnp.sum(upstream * normed, axis=0)
    grad_normed = upstream * gain.astype(jnp.float32)
    grad_values = inverse * (
        grad_normed - normed * jnp.mean(grad_normed * normed, axis=-1, keepdims=True)
    )
    return (grad_values, grad_gain)


def geglu(gate_pre, linear_pre):
    return jax.nn.gelu(gate_pre, approximate=True) * linear_pre


def by_heads(values, head_count):
    return values.reshape(values.shape[0], head_count, values.shape[1] // head_count)


def band_onehot(bucket_rev, buckets, query_rows, key_rows, query_first, key_first):
    length = bucket_rev.shape[0] // 2
    offset_first = query_first - key_first
    upper_band = lax.dynamic_slice_in_dim(bucket_rev, length - 1 - offset_first, key_rows, 0)
    lower_band = lax.dynamic_slice_in_dim(
        bucket_rev, length - offset_first - query_rows, query_rows - 1, 0
    )
    slots = jnp.concatenate([upper_band, jnp.full((1,), -1, jnp.int32), lower_band])
    return (slots[:, None] == jnp.arange(buckets, dtype=jnp.int32)[None, :]).astype(jnp.float32)


def spread_band(band, query_rows, key_rows):
    head_count, width = band.shape
    tiled = jnp.broadcast_to(band[:, None, :], (head_count, query_rows, width)).reshape(
        head_count, query_rows * width
    )
    return tiled[:, : query_rows * (width - 1)].reshape(head_count, query_rows, width - 1)[
        :, :, :key_rows
    ]


def fold_band(grad_scores, width):
    head_count, query_rows, key_rows = grad_scores.shape
    padded = jnp.pad(grad_scores, ((0, 0), (0, 0), (0, width - 1 - key_rows))).reshape(
        head_count, query_rows * (width - 1)
    )
    padded = jnp.pad(padded, ((0, 0), (0, query_rows)))
    return jnp.sum(padded.reshape(head_count, query_rows, width), axis=1)


def self_scores(query, key_block, query_first, key_first, bucket_rev, bias_table):
    head_count = bias_table.shape[1]
    query_rows = query.shape[0]
    key_rows = key_block.shape[0]
    scores = jnp.einsum(
        "qhe,khe->hqk",
        by_heads(query, head_count),
        by_heads(key_block, head_count),
        preferred_element_type=jnp.float32,
    )
    offset = (query_first + jnp.arange(query_rows, dtype=jnp.int32))[:, None] - (
        key_first + jnp.arange(key_rows, dtype=jnp.int32)
    )[None, :]
    allowed = offset >= 0
    onehot = band_onehot(
        bucket_rev, bias_table.shape[0], query_rows, key_rows, query_first, key_first
    )
    band = jnp.dot(onehot, bias_table, precision=HIGHEST).T
    scores = jnp.where(allowed[None], scores + spread_band(band, query_rows, key_rows), NEGATIVE)
    return (scores, allowed, onehot)


def table_terms(grad_scores, onehot):
    band_grad = fold_band(grad_scores, onehot.shape[0])
    return jnp.dot(onehot.T, band_grad.T, precision=HIGHEST)


def fold_blocks(block_step, running, arrays, first_row):
    piece_rows = arrays[0].shape[0]
    block_size = math.gcd(piece_rows, 512) if piece_rows > 512 else piece_rows
    if block_size == piece_rows:
        return block_step(running, arrays, first_row)
    block_count = piece_rows // block_size
    stacked = tuple(
        (member.reshape((block_count, block_size) + member.shape[1:]) for member in arrays)
    )

    def scan_block(state_now, scanned):
        number, blocks = scanned
        return (block_step(state_now, blocks, first_row + number * block_size), None)

    result, _ = lax.scan(scan_block, running, (jnp.arange(block_count, dtype=jnp.int32), stacked))
    return result


def forward_step(running, blocks, key_first, query, query_first, bucket_rev, bias_table):
    top, total, mixed = running
    key_block, value_block = blocks
    head_count = bias_table.shape[1]
    scores, allowed, _ = self_scores(
        query, key_block, query_first, key_first, bucket_rev, bias_table
    )
    new_top = jnp.maximum(top, jnp.max(scores, axis=-1))
    weights = jnp.where(allowed[None], jnp.exp(scores - new_top[:, :, None]), 0.0)
    rescale = jnp.exp(top - new_top)
    total = total * rescale + jnp.sum(weights, axis=-1)
    update = jnp.einsum(
        "hqk,khe->qhe",
        weights.astype(jnp.bfloat16),
        by_heads(value_block, head_count),
        preferred_element_type=jnp.float32,
    )
    mixed = mixed * rescale.T[:, :, None] + update
    return (new_top, total, mixed)


def backward_core(
    query,
    grad_attn,
    lse_rows,
    delta_rows,
    key_block,
    value_block,
    query_first,
    key_first,
    bucket_rev,
    bias_table,
):
    head_count = bias_table.shape[1]
    scores, allowed, onehot = self_scores(
        query, key_block, query_first, key_first, bucket_rev, bias_table
    )
    probs = jnp.where(allowed[None], jnp.exp(scores - lse_rows.T[:, :, None]), 0.0)
    grad_probs = jnp.einsum(
        "qhe,khe->hqk",
        by_heads(grad_attn, head_count),
        by_heads(value_block, head_count),
        preferred_element_type=jnp.float32,
    )
    grad_scores = probs * (grad_probs - delta_rows.T[:, :, None])
    return (probs, grad_scores, onehot)


def partial_step(
    running,
    blocks,
    key_first,
    query,
    grad_attn,
    lse_rows,
    delta_rows,
    query_first,
    bucket_rev,
    bias_table,
):
    grad_query, grad_keys, grad_values, table_part = running
    key_block, value_block = blocks
    head_count = bias_table.shape[1]
    probs, grad_scores, onehot = backward_core(
        query,
        grad_attn,
        lse_rows,
        delta_rows,
        key_block,
        value_block,
        query_first,
        key_first,
        bucket_rev,
        bias_table,
    )
    rounded = grad_scores.astype(jnp.bfloat16)
    grad_query = grad_query + jnp.einsum(
        "hqk,khe->qhe", rounded, by_heads(key_block, head_count), preferred_element_type=jnp.float32
    )
    key_part = jnp.einsum(
        "hqk,qhe->khe", rounded, by_heads(query, head_count), preferred_element_type=jnp.float32
    ).reshape(key_block.shape[0], -1)
    value_part = jnp.einsum(
        "hqk,qhe->khe",
        probs.astype(jnp.bfloat16),
        by_heads(grad_attn, head_count),
        preferred_element_type=jnp.float32,
    ).reshape(key_block.shape[0], -1)
    grad_keys = lax.dynamic_update_slice_in_dim(grad_keys, key_part, key_first, 0)
    grad_values = lax.dynamic_update_slice_in_dim(grad_values, value_part, key_first, 0)
    table_part = table_part + table_terms(grad_scores, onehot)
    return (grad_query, grad_keys, grad_values, table_part)


def plain_forward(query, keys, values, head_count):
    scores = jnp.einsum(
        "qhe,khe->hqk",
        by_heads(query, head_count),
        by_heads(keys, head_count),
        preferred_element_type=jnp.float32,
    )
    top = jnp.max(scores, axis=-1, keepdims=True)
    weights = jnp.exp(scores - top)
    total = jnp.sum(weights, axis=-1, keepdims=True)
    mixed = jnp.einsum(
        "hqk,khe->qhe",
        weights.astype(jnp.bfloat16),
        by_heads(values, head_count),
        preferred_element_type=jnp.float32,
    )
    result = (
        (mixed / jnp.transpose(total, (1, 0, 2))).reshape(query.shape[0], -1).astype(jnp.bfloat16)
    )
    return (result, (top + jnp.log(total))[:, :, 0])


def plain_backward(query, keys, values, lse, output, grad_output, head_count):
    split_grad = by_heads(grad_output, head_count)
    delta = jnp.sum(
        split_grad.astype(jnp.float32) * by_heads(output, head_count).astype(jnp.float32), axis=-1
    ).T
    scores = jnp.einsum(
        "qhe,khe->hqk",
        by_heads(query, head_count),
        by_heads(keys, head_count),
        preferred_element_type=jnp.float32,
    )
    probs = jnp.exp(scores - lse[:, :, None])
    grad_probs = jnp.einsum(
        "qhe,khe->hqk", split_grad, by_heads(values, head_count), preferred_element_type=jnp.float32
    )
    rounded = (probs * (grad_probs - delta[:, :, None])).astype(jnp.bfloat16)
    grad_query = jnp.einsum(
        "hqk,khe->qhe", rounded, by_heads(keys, head_count), preferred_element_type=jnp.float32
    ).reshape(query.shape[0], -1)
    grad_keys = jnp.einsum(
        "hqk,qhe->khe", rounded, by_heads(query, head_count), preferred_element_type=jnp.float32
    ).reshape(keys.shape[0], -1)
    grad_values = jnp.einsum(
        "hqk,qhe->khe", probs.astype(jnp.bfloat16), split_grad, preferred_element_type=jnp.float32
    ).reshape(keys.shape[0], -1)
    return (grad_query, grad_keys, grad_values)


def reduce_terms(terms, table_terms):
    groups = lax.axis_size("seq")
    share = terms.shape[1] // groups
    stacked = jnp.stack(
        [terms[:, number * share : (number + 1) * share] for number in range(groups)]
    )
    part = lax.psum_scatter(stacked, "seq", scatter_dimension=0, tiled=False)
    table = lax.psum(table_terms, ("seq", "ctx", "fsdp"))
    part, table = lax.optimization_barrier((part, table))
    part = lax.psum_scatter(part, ("ctx", "fsdp"), scatter_dimension=0, tiled=True)
    return join_columns(lax.all_gather(part, "seq", axis=0, tiled=False)), table


def join_columns(stacked):
    return jnp.concatenate([stacked[number] for number in range(stacked.shape[0])], axis=1)


def gather_pack(pack):
    share = pack.shape[1] // lax.axis_size("seq")
    own = lax.dynamic_slice_in_dim(pack, lax.axis_index("seq") * share, share, 1)
    rows = lax.all_gather(own, ("ctx", "fsdp"), axis=0, tiled=True)
    return join_columns(lax.all_gather(rows, "seq", axis=0, tiled=False))


def even_columns(members):
    joined = jnp.concatenate(members, axis=1)
    return jnp.pad(joined, ((0, 0), (0, -joined.shape[1] % (LANES * lax.axis_size("seq")))))


def per_device(
    hidden_in,
    encoder_states,
    out_grad,
    bucket_index,
    bias_table,
    self_gain,
    self_query,
    self_key,
    self_value,
    self_output,
    cross_gain,
    cross_query,
    cross_key,
    cross_value,
    cross_output,
    feed_gain,
    gate_weight,
    linear_weight,
    down_weight,
):
    shards = lax.axis_size(("ctx", "fsdp"))
    features = self_query.shape[1]
    hidden = gate_weight.shape[1]
    pack = even_columns(
        [
            self_query,
            self_key,
            self_value,
            self_output,
            cross_query,
            cross_key,
            cross_value,
            cross_output,
            gate_weight,
            linear_weight,
            fold_rows(down_weight, self_query.shape[0]),
            gain_columns((self_gain, cross_gain, feed_gain), jnp.bfloat16),
        ]
    )
    pack = gather_pack(pack)
    (
        self_query,
        self_key,
        self_value,
        self_output,
        cross_query,
        cross_key,
        cross_value,
        cross_output,
    ) = (pack[:, number * features : (number + 1) * features] for number in range(8))
    first = 8 * features
    gate_weight = pack[:, first : first + hidden]
    linear_weight = pack[:, first + hidden : first + 2 * hidden]
    first = first + 2 * hidden
    width = -(-(hidden // shards) // (features // shards)) * features
    down_weight = unfold_rows(
        pack[:, first : first + width].reshape(shards, -1, width), hidden // shards, features
    ).reshape(hidden, features)
    gains = pack[:, first + width : first + width + LANES].T
    self_gain, cross_gain, feed_gain = gains[0], gains[1], gains[2]
    tokens = hidden_in.shape[1]
    length = bucket_index.shape[0]
    head_count = bias_table.shape[1]
    buckets = bias_table.shape[0]
    query_first = lax.axis_index("ctx") * tokens
    bucket_rev = jnp.flip(jnp.concatenate([jnp.full((length,), -1, jnp.int32), bucket_index]))
    start_x = hidden_in[0].astype(jnp.float32)
    norm_one, normed_one, inverse_one = norm_forward(start_x, self_gain)
    projected = product(norm_one, pack[:, : 3 * features]).astype(jnp.bfloat16)
    query = projected[:, :features]
    encoder_local = encoder_states[0]
    cross_local = product(encoder_local, pack[:, 5 * features : 7 * features]).astype(jnp.bfloat16)
    encoder_rows = encoder_local.shape[0]
    blocks = lax.all_gather(
        jnp.concatenate([projected[:, features:], cross_local], axis=0), "ctx", axis=0, tiled=False
    )
    both = blocks[:, :tokens].reshape(length, 2 * features)
    keys, values = both[:, :features], both[:, features:]
    both = blocks[:, tokens:].reshape(-1, 2 * features)
    cross_keys, cross_values = both[:, :features], both[:, features:]
    empty_top = jnp.full((head_count, tokens), NEGATIVE, jnp.float32)
    empty_total = jnp.zeros((head_count, tokens), jnp.float32)
    empty_mixed = jnp.zeros((tokens, head_count, query.shape[1] // head_count), jnp.float32)
    forward_bound = partial(
        forward_step,
        query=query,
        query_first=query_first,
        bucket_rev=bucket_rev,
        bias_table=bias_table,
    )
    top, total, mixed = fold_blocks(
        forward_bound,
        (empty_top, empty_total, empty_mixed),
        (keys, values),
        jnp.int32(0),
    )
    attn = (mixed / total.T[:, :, None]).reshape(tokens, -1).astype(jnp.bfloat16)
    self_lse = (top + jnp.log(total)).T
    after_self = start_x + product(attn, self_output)
    norm_two, normed_two, inverse_two = norm_forward(after_self, cross_gain)
    cross_q = product(norm_two, cross_query).astype(jnp.bfloat16)
    cattn, cross_lse = plain_forward(cross_q, cross_keys, cross_values, head_count)
    after_cross = after_self + product(cattn, cross_output)
    norm_three, normed_three, inverse_three = norm_forward(after_cross, feed_gain)
    gate_pre = product(norm_three, gate_weight)
    linear_pre = product(norm_three, linear_weight)
    middle = geglu(gate_pre, linear_pre).astype(jnp.bfloat16)
    layer_out = (after_cross + product(middle, down_weight)).astype(jnp.bfloat16)
    grad_top = out_grad[0]
    grad_down = row_contract(middle, grad_top)
    grad_middle = col_contract(grad_top, down_weight)
    _, pull_back = jax.vjp(geglu, gate_pre, linear_pre)
    grad_gate_pre, grad_linear_pre = pull_back(grad_middle)
    gate_round = grad_gate_pre.astype(jnp.bfloat16)
    linear_round = grad_linear_pre.astype(jnp.bfloat16)
    grad_gate = row_contract(norm_three, gate_round)
    grad_linear = row_contract(norm_three, linear_round)
    back_three, grad_feed_gain = norm_backward(
        col_contract(gate_round, gate_weight) + col_contract(linear_round, linear_weight),
        normed_three,
        inverse_three,
        feed_gain,
    )
    grad_after_cross = grad_top.astype(jnp.float32) + back_three
    cross_round = grad_after_cross.astype(jnp.bfloat16)
    grad_cross_output = row_contract(cattn, cross_round)
    grad_cattn = col_contract(cross_round, cross_output).astype(jnp.bfloat16)
    grad_cq, cross_key_terms, cross_value_terms = plain_backward(
        cross_q, cross_keys, cross_values, cross_lse, cattn, grad_cattn, head_count
    )
    grad_cq = grad_cq.astype(jnp.bfloat16)
    grad_cross_query = row_contract(norm_two, grad_cq)
    back_two, grad_cross_gain = norm_backward(
        col_contract(grad_cq, cross_query), normed_two, inverse_two, cross_gain
    )
    grad_after_self = grad_after_cross + back_two
    self_round = grad_after_self.astype(jnp.bfloat16)
    grad_self_output = row_contract(attn, self_round)
    grad_attn = col_contract(self_round, self_output).astype(jnp.bfloat16)
    delta_rows = jnp.sum(
        by_heads(grad_attn, head_count).astype(jnp.float32)
        * by_heads(attn, head_count).astype(jnp.float32),
        axis=-1,
    )
    empty_rows = jnp.zeros((tokens, query.shape[1]), jnp.float32)
    empty_table = jnp.zeros((buckets, head_count), jnp.float32)
    partial_bound = partial(
        partial_step,
        query=query,
        grad_attn=grad_attn,
        lse_rows=self_lse,
        delta_rows=delta_rows,
        query_first=query_first,
        bucket_rev=bucket_rev,
        bias_table=bias_table,
    )
    empty_whole = jnp.zeros((length, query.shape[1]), jnp.float32)
    grad_query, key_terms, value_terms, table_part = fold_blocks(
        partial_bound,
        (empty_rows.reshape(tokens, head_count, -1), empty_whole, empty_whole, empty_table),
        (keys, values),
        jnp.int32(0),
    )
    terms = jnp.concatenate(
        [
            jnp.concatenate([key_terms, value_terms], axis=1).reshape(-1, tokens, 2 * features),
            jnp.concatenate([cross_key_terms, cross_value_terms], axis=1).reshape(
                -1, encoder_rows, 2 * features
            ),
        ],
        axis=1,
    ).astype(jnp.bfloat16)
    sums = lax.psum_scatter(terms, "ctx", scatter_dimension=0, tiled=False)
    cross_both = sums[tokens:]
    grad_cross_both = row_contract(encoder_local, cross_both)
    grad_cross_key, grad_cross_value = (
        grad_cross_both[:, :features],
        grad_cross_both[:, features:],
    )
    encoder_grad = col_contract(cross_both, pack[:, 5 * features : 7 * features])
    grad_q = grad_query.reshape(tokens, -1).astype(jnp.bfloat16)
    grad_projected = jnp.concatenate([grad_q, sums[:tokens]], axis=1)
    grad_self_projections = row_contract(norm_one, grad_projected)
    upstream_one = col_contract(grad_projected, pack[:, : 3 * features])
    back_one, grad_self_gain = norm_backward(upstream_one, normed_one, inverse_one, self_gain)
    input_grad = grad_after_self + back_one
    folded = fold_rows(grad_down.reshape(shards, -1, features), features // shards)
    parts = [
        grad_self_projections,
        grad_self_output,
        grad_cross_query,
        grad_cross_both,
        grad_cross_output,
        grad_gate,
        grad_linear,
        folded.reshape(features, width),
        gain_columns((grad_self_gain, grad_cross_gain, grad_feed_gain), jnp.bfloat16),
    ]
    terms = even_columns([member.astype(jnp.bfloat16) for member in parts])
    summed, grad_table = reduce_terms(terms, table_part)
    summed = summed.astype(jnp.float32)
    squares = [summed[:, number * features : (number + 1) * features] for number in range(8)]
    first = 8 * features
    down_first = first + 2 * hidden
    gain_first = down_first + width
    return (
        layer_out[None],
        input_grad[None],
        encoder_grad[None],
        grad_table,
        summed[:, gain_first],
        squares[0],
        squares[1],
        squares[2],
        squares[3],
        summed[:, gain_first + 1],
        squares[4],
        squares[5],
        squares[6],
        squares[7],
        summed[:, gain_first + 2],
        summed[:, first : first + hidden],
        summed[:, first + hidden : down_first],
        unfold_rows(summed[:, down_first:gain_first], hidden // shards, features),
    )


MESH = pl.DeviceIdType.MESH
FAR_BELOW = -1e30


def remote(source, target, send_sem, recv_sem, device):
    return pltpu.make_async_remote_copy(
        src_ref=source,
        dst_ref=target,
        send_sem=send_sem,
        recv_sem=recv_sem,
        device_id=device,
        device_id_type=MESH,
    )


class Place:
    def __init__(self, count, sends, recvs):
        self.count, self.sends, self.recvs = count, sends, recvs
        self.seq = lax.axis_index("seq")
        self.side, self.core = self.seq // 2, self.seq % 2
        self.depth, self.row = lax.axis_index("ctx"), lax.axis_index("fsdp")
        self.quarter = self.seq
        self.to_x = self.at(1 - self.side, self.core, self.depth, self.row)
        self.to_y = self.at(self.side, self.core, self.depth, 1 - self.row)
        self.to_core = self.at(self.side, 1 - self.core, self.depth, self.row)
        self.to_far = self.at(1 - self.side, 1 - self.core, self.depth, self.row)
        self.x_quarter = 2 * (1 - self.side) + self.core
        self.core_quarter = 2 * self.side + 1 - self.core
        self.far_quarter = 2 * (1 - self.side) + 1 - self.core
        self.used = 0

    def at(self, side, core, depth, row):
        return (side * 2 + core, depth, row)

    def at_depth(self, depth):
        return (self.seq, depth, self.row)

    def take(self, number):
        first = self.used
        self.used += number
        return first

    def link(self, source, target, index, device):
        return remote(source, target, self.sends.at[index], self.recvs.at[index], device)

    def others(self, step):
        middle = self.count // 2
        for at in sorted(range(self.count), key=lambda at: abs(2 * at - self.count + 1) + (at < middle) * 0.5):
            @pl.when(self.depth != at)
            def _():
                step(at)


class Gather:
    def __init__(self, here, piece, spread):
        self.here, self.piece, self.spread = here, piece, spread
        count = here.count
        self.z_base = here.take(count)
        self.y_base = here.take(count)
        if spread:
            self.x_base = here.take(2 * count)
            self.c_base = here.take(4 * count)

    def row(self, other):
        return 1 - self.here.row if other else self.here.row

    def z_copy(self, at):
        here = self.here
        held = self.piece(here.depth, here.row, here.quarter)
        return remote(
            held, held, here.sends.at[self.z_base + at], here.recvs.at[self.z_base + here.depth], here.at_depth(at)
        )

    def z_arrival(self, at):
        held = self.piece(at, self.here.row, self.here.quarter)
        return self.here.link(held, held, self.z_base + at, self.here.to_y)

    def y_copy(self, at, other):
        held = self.piece(at, self.row(other), self.here.quarter)
        return self.here.link(held, held, self.y_base + at, self.here.to_y)

    def x_copy(self, at, other, quarter):
        held = self.piece(at, self.row(other), quarter)
        return self.here.link(held, held, self.x_base + other * self.here.count + at, self.here.to_x)

    def c_copy(self, at, other, level, quarter):
        held = self.piece(at, self.row(other), quarter)
        return self.here.link(
            held, held, self.c_base + (2 * level + other) * self.here.count + at, self.here.to_core
        )

    def onward(self, at, other):
        if self.spread:
            self.x_copy(at, other, self.here.quarter).start()
            self.c_copy(at, other, 0, self.here.quarter).start()

    def begin(self):
        self.here.others(lambda at: self.z_copy(at).start())
        self.y_copy(self.here.depth, 0).start()

    def z_phase(self):
        def step(at):
            self.z_arrival(at).wait_recv()
            self.y_copy(at, 0).start()
            self.onward(at, 0)

        self.here.others(step)

    def y_phase(self):
        def step(at):
            self.y_copy(at, 1).wait_recv()
            self.onward(at, 1)

        step(self.here.depth)
        self.here.others(step)

    def members(self, step):
        step(self.here.depth, 1)
        for other in (0, 1):
            self.here.others(lambda at: step(at, other))

    def x_phase(self):
        def step(at, other):
            self.x_copy(at, other, self.here.x_quarter).wait_recv()
            self.c_copy(at, other, 1, self.here.x_quarter).start()

        self.members(step)

    def finish(self):
        def step(at, other):
            self.c_copy(at, other, 0, self.here.core_quarter).wait_recv()
            self.c_copy(at, other, 1, self.here.far_quarter).wait_recv()

        self.members(step)

    def drain(self):
        here = self.here
        here.others(lambda at: self.z_copy(at).wait_send())
        self.y_copy(here.depth, 0).wait_send()
        here.others(lambda at: self.y_copy(at, 0).wait_send())

        def step(at, other):
            self.x_copy(at, other, here.quarter).wait_send()
            self.c_copy(at, other, 0, here.quarter).wait_send()
            self.c_copy(at, other, 1, here.x_quarter).wait_send()

        if self.spread:
            self.members(step)


class Scatter:
    def __init__(self, here, total, height, from_y, from_z, out):
        self.here, self.total, self.height, self.out = here, total, height, out
        self.from_y, self.from_z = from_y, from_z
        self.y_base = here.take(here.count)
        self.z_base = here.take(here.count)
        self.out_base = here.take(3)

    def block(self, depth, row):
        first = pl.multiple_of((depth * 2 + row) * self.height, self.height)
        return self.total.at[pl.ds(first, self.height), :]

    def y_copy(self, depth):
        here = self.here
        return here.link(self.block(depth, 1 - here.row), self.from_y.at[depth], self.y_base + depth, here.to_y)

    def y_begin(self):
        self.here.others(lambda at: self.y_copy(at).start())
        self.y_copy(self.here.depth).start()

    def z_copy(self, at):
        here = self.here
        return remote(
            self.block(at, here.row), self.from_z.at[here.depth], here.sends.at[self.z_base + at],
            here.recvs.at[self.z_base + here.depth], here.at_depth(at),
        )

    def y_phase(self):
        def step(at):
            self.y_copy(at).wait_recv()
            block = self.block(at, self.here.row)
            block[...] = block[...] + self.from_y[at]
            self.z_copy(at).start()

        self.here.others(step)

    def z_phase(self):
        here = self.here
        self.y_copy(here.depth).wait_recv()
        self.from_z[here.depth] = self.block(here.depth, here.row)[...] + self.from_y[here.depth]

        def wait(at):
            held = self.from_z.at[at]
            here.link(held, held, self.z_base + at, here.to_y).wait_recv()

        here.others(wait)
        summed = self.from_z[0].astype(jnp.float32)
        for at in range(1, here.count):
            summed = summed + self.from_z[at].astype(jnp.float32)
        self.out(here.quarter)[...] = summed.astype(jnp.bfloat16)
        self.out_copy(0).start()
        self.out_copy(1).start()

    def out_copy(self, level, quarter=None):
        here = self.here
        quarter = (here.quarter, here.quarter, here.x_quarter)[level] if quarter is None else quarter
        held = self.out(quarter)
        return here.link(held, held, self.out_base + level, here.to_x if level == 0 else here.to_core)

    def out_phase(self):
        self.out_copy(0, self.here.x_quarter).wait_recv()
        self.out_copy(2).start()

    def finish(self):
        here = self.here
        self.out_copy(1, here.core_quarter).wait_recv()
        self.out_copy(2, here.far_quarter).wait_recv()
        for level in range(3):
            self.out_copy(level).wait_send()
        self.y_copy(here.depth).wait_send()
        here.others(lambda at: self.y_copy(at).wait_send())
        here.others(lambda at: self.z_copy(at).wait_send())


class SmallSum:
    def __init__(self, here, held, landing, depth_held):
        self.here, self.held, self.landing, self.depth_held = here, held, landing, depth_held
        self.base = here.take(3 + here.count)
        self.partners = [here.to_core, here.to_x, here.to_y]

    def copy(self, level):
        return self.here.link(self.held.at[level], self.landing.at[level], self.base + level, self.partners[level])

    def z_copy(self, at):
        here = self.here
        held = self.depth_held.at[here.depth]
        return remote(
            held, held, here.sends.at[self.base + 3 + at], here.recvs.at[self.base + 3 + here.depth], here.at_depth(at)
        )

    def begin(self):
        self.copy(0).start()

    def level(self, level):
        here = self.here
        self.copy(level).wait_recv()
        summed = self.held[level] + self.landing[level]
        if level < 2:
            self.held[level + 1] = summed
            self.copy(level + 1).start()
        else:
            self.depth_held[here.depth] = summed
            for at in range(here.count):
                @pl.when(here.depth != at)
                def _():
                    self.z_copy(at).start()

    def finish(self):
        here = self.here
        for at in range(here.count):
            @pl.when(here.depth != at)
            def _():
                held = self.depth_held.at[at]
                here.link(held, held, self.base + 3 + at, here.to_y).wait_recv()
        summed = self.depth_held[0]
        for at in range(1, here.count):
            summed = summed + self.depth_held[at]
        for level in range(3):
            self.copy(level).wait_send()
        for at in range(here.count):
            @pl.when(here.depth != at)
            def _():
                self.z_copy(at).wait_send()
        return summed


class Swap:
    def __init__(self, here, source, target):
        self.here, self.source, self.target = here, source, target
        self.base = here.take(here.count)

    def copy(self, at):
        here = self.here
        return remote(
            self.source(at), self.target(here.depth), here.sends.at[self.base + at],
            here.recvs.at[self.base + here.depth], here.at_depth(at),
        )

    def begin(self):
        self.here.others(lambda at: self.copy(at).start())

    def arrive(self):
        def wait(at):
            held = self.target(at)
            self.here.link(held, held, self.base + at, self.here.to_y).wait_recv()

        self.here.others(wait)

    def drain(self):
        self.here.others(lambda at: self.copy(at).wait_send())


class SeqGather:
    def __init__(self, here, held):
        self.here, self.held = here, held
        self.base = here.take(3)

    def copy(self, level, index=None):
        here = self.here
        index = (here.quarter, here.quarter, here.x_quarter)[level] if index is None else index
        held = self.held.at[index]
        return here.link(held, held, self.base + level, here.to_x if level == 0 else here.to_core)

    def begin(self):
        self.copy(0).start()
        self.copy(1).start()

    def relay(self):
        self.copy(0, self.here.x_quarter).wait_recv()
        self.copy(2).start()

    def arrive(self):
        self.copy(1, self.here.core_quarter).wait_recv()
        self.copy(2, self.here.far_quarter).wait_recv()

    def drain(self):
        for level in range(3):
            self.copy(level).wait_send()


class SeqSum:
    def __init__(self, here, held, landing):
        self.here, self.held, self.landing = here, held, landing
        self.base = here.take(3)

    def copy(self, level):
        here = self.here
        index = (here.far_quarter, here.core_quarter, here.x_quarter)[level]
        return here.link(
            self.held.at[index], self.landing.at[level], self.base + level, here.to_x if level == 2 else here.to_core
        )

    def begin(self):
        self.copy(0).start()
        self.copy(1).start()

    def relay(self):
        here = self.here
        self.copy(0).wait_recv()
        self.held[here.x_quarter] = self.held[here.x_quarter] + self.landing[0]
        self.copy(2).start()

    def arrive(self):
        here = self.here
        self.copy(1).wait_recv()
        self.copy(2).wait_recv()
        own = self.held[here.quarter].astype(jnp.float32)
        return own + self.landing[1].astype(jnp.float32) + self.landing[2].astype(jnp.float32)

    def drain(self):
        for level in range(3):
            self.copy(level).wait_send()


class SeqSwap:
    def __init__(self, here, heights, landing):
        self.here, self.heights, self.landing = here, heights, landing
        self.base = here.take(4)

    def held(self, member, source):
        return self.landing.at[source, pl.ds(0, self.heights[member]), :]

    def copy(self, member, block):
        here = self.here
        return remote(
            block, self.held(member, here.seq), here.sends.at[self.base + member], here.recvs.at[self.base + here.seq],
            (member, here.depth, here.row),
        )

    def begin(self, member, block):
        here = self.here

        @pl.when(here.seq != member)
        def _():
            self.copy(member, block).start()

        @pl.when(here.seq == member)
        def _():
            self.held(member, here.seq)[...] = block[...]

    def arrive(self):
        here = self.here
        for member in range(4):
            @pl.when(here.seq == member)
            def _():
                for source in range(4):
                    if source != member:
                        held = self.held(member, source)
                        here.link(held, held, self.base + source, here.to_core).wait_recv()

    def drain(self):
        here = self.here
        for member in range(4):
            @pl.when(here.seq != member)
            def _():
                held = self.held(member, member)
                here.link(held, held, self.base + member, here.to_core).wait_send()


def tiles(total, width, body):
    def step(number, carry):
        body(pl.ds(pl.multiple_of(number * width, width), width))
        return carry

    lax.fori_loop(0, total // width, step, 0)


def times(left, right, left_dim, right_dim):
    return lax.dot_general(
        left, right, (((left_dim,), (right_dim,)), ((), ())), preferred_element_type=jnp.float32
    )


def normed_of(values):
    inverse = lax.rsqrt(jnp.mean(values * values, axis=-1, keepdims=True) + EPSILON)
    return values * inverse, inverse


def norm_back(upstream, values, gain):
    normed, inverse = normed_of(values)
    grad_gain = jnp.sum(upstream * normed, axis=0, keepdims=True)
    grad_normed = upstream * gain
    mean = jnp.mean(grad_normed * normed, axis=-1, keepdims=True)
    return inverse * (grad_normed - normed * mean), grad_gain


BF = jnp.bfloat16
F32 = jnp.float32


class Names:
    pass


def layer_kernel(sizes, names, *refs):
    r = Names()
    for name, ref in zip(names, refs):
        setattr(r, name, ref)
    count, tokens, features, enc, heads, quarter, rows, tall = sizes
    head = features // heads
    mine = heads // count
    width = mine * head
    length = count * tokens
    states = count * enc
    here = Place(count, r.sends, r.recvs)
    seq, depth, row = here.seq, here.depth, here.row

    own = pl.multiple_of((depth * 2 + row) * rows, rows)
    own_tall = pl.multiple_of((depth * 2 + row) * tall, tall)
    squares = [getattr(r, f"square{number}") for number in range(8)]
    local = [
        pltpu.make_async_copy(squares[number], r.weights.at[number, pl.ds(own, rows), :], r.local.at[number])
        for number in range(8)
    ]
    local.append(
        pltpu.make_async_copy(
            r.down.at[pl.ds(pl.multiple_of(seq * tall, tall), tall), :], r.down_quarter.at[pl.ds(own_tall, tall), :],
            r.local.at[8],
        )
    )
    for copy in local:
        copy.start()

    def weight_piece(chunk):
        return lambda at, at_row, quarter_at: r.weights.at[
            4 * chunk + quarter_at, pl.ds(pl.multiple_of((at * 2 + at_row) * rows, rows), rows), :
        ]

    def quarter_piece(whole, height):
        return lambda at, at_row, quarter_at: whole.at[
            pl.ds(pl.multiple_of((at * 2 + at_row) * height, height), height), :
        ]

    gathers = [
        Gather(here, weight_piece(0), True),
        Gather(here, weight_piece(1), True),
        Gather(here, quarter_piece(r.gate_quarter, rows), False),
        Gather(here, quarter_piece(r.linear_quarter, rows), False),
        Gather(here, quarter_piece(r.down_quarter, tall), False),
    ]
    mates = []
    for far in range(count):
        for flip in (0, 1):
            if far or flip:
                mates.append((lax.rem(depth + far, count), row if flip == 0 else 1 - row))
    partners = [(seq,) + mate for mate in mates] + [here.to_x, here.to_core, here.to_far]
    barrier = pltpu.get_barrier_semaphore()
    for partner in partners:
        pl.semaphore_signal(barrier, inc=1, device_id=partner, device_id_type=MESH)
    pl.semaphore_wait(barrier, len(partners))

    gain_base = here.take(2 * count - 1)
    r.all_gains[depth * 2 + row] = r.gains[...]
    gain_sends = [
        here.link(r.all_gains.at[depth * 2 + row], r.all_gains.at[depth * 2 + row], gain_base + number, (seq,) + mate)
        for number, mate in enumerate(mates)
    ]
    for copy in gain_sends:
        copy.start()
    for number in range(4):
        local[number].wait()
    gathers[0].begin()
    for number in range(4, 9):
        local[number].wait()
    gathers[1].begin()

    r.grads_in[seq] = r.out_grad[...]
    grads_in = SeqGather(here, r.grads_in)
    long = (tokens,) * 3 + (enc,)
    lefts = [SeqSwap(here, long, r.left.at[0]), SeqSwap(here, long[::-1], r.left.at[1])]
    rights = [SeqSwap(here, long, r.right.at[0]), SeqSwap(here, long[::-1], r.right.at[1])]

    for at in range(4):
        @pl.when(seq == at)
        def _():
            for source, whole in ((r.gate, r.gate_quarter), (r.linear, r.linear_quarter)):
                span = 4 * tall
                whole[pl.ds(own, rows), :] = jnp.concatenate(
                    [source[:, number * span + at * tall : number * span + (at + 1) * tall] for number in range(2 * count)],
                    axis=1,
                )

    key_at = lax.broadcasted_iota(jnp.int32, (tokens, length), 0)
    query_at = lax.broadcasted_iota(jnp.int32, (tokens, length), 1)
    for number in range(mine):
        strip = jnp.broadcast_to(r.bias[number : number + 1, :], (tokens, length))
        step = 1
        while step < tokens:
            strip = jnp.where((key_at // step) % 2 == 1, pltpu.roll(strip, step, 1), strip)
            step *= 2
        r.strip[number] = jnp.where(query_at >= key_at, strip, FAR_BELOW)

    for chunk in (2, 3, 4):
        gathers[chunk].begin()
    gathers[0].z_phase()
    gathers[0].y_phase()

    for far in range(count):
        for flip in (0, 1):
            if far or flip:
                source = lax.rem(depth + count - far, count) * 2 + (row if flip == 0 else 1 - row)
                held = r.all_gains.at[source]
                here.link(held, held, gain_base + far * 2 + flip - 1, here.to_core).wait_recv()
    lane = lax.broadcasted_iota(jnp.int32, (LANES, features), 0)
    column = lax.broadcasted_iota(jnp.int32, (LANES, features), 1)
    gain_rows = jnp.zeros((16, features), F32)
    for number in range(2 * count):
        select = jnp.logical_and(column - number * rows == lane, lane < rows)
        gain_rows = gain_rows + times(r.all_gains[number], select.astype(F32).astype(BF), 1, 0)
    r.gain_rows[...] = gain_rows

    def gain(number):
        return r.gain_rows[number : number + 1, :]

    x0 = r.hidden[...].astype(F32)
    h1 = (normed_of(x0)[0] * gain(0)).astype(BF)
    r.h1[...] = h1

    gathers[1].z_phase()
    gathers[0].x_phase()
    gathers[0].finish()

    def head_rows(at):
        return pl.ds(pl.multiple_of(at * width, width), width)

    def token_lanes(at):
        return pl.ds(pl.multiple_of(at * tokens, tokens), tokens)

    def own_block(target, source):
        target[...] = source[...]

    qkv = [
        Swap(
            here, lambda at, number=number: r.qkv_t.at[number, head_rows(at), :],
            lambda at, number=number: r.qkv_h.at[number, :, token_lanes(at)],
        )
        for number in range(3)
    ]
    for number in range(3):
        def project(at, number=number):
            r.qkv_t[number, at, :] = times(r.h1[...], r.weights[number, :, at], 1, 0).astype(BF).T

        tiles(features, 256, project)
        qkv[number].begin()
    own_block(r.qkv_h.at[:, :, token_lanes(depth)], r.qkv_t.at[:, head_rows(depth), :])

    gathers[1].y_phase()
    grads_in.begin()
    gathers[1].x_phase()
    gathers[1].finish()
    for member in range(3):
        lefts[0].begin(member, r.h1)
    lefts[0].begin(3, r.encoder)
    lefts[1].begin(0, r.encoder)

    for number in range(2):
        def project(at, number=number):
            r.cross_kv[number, pl.ds(pl.multiple_of(depth * enc, enc), enc), at] = times(
                r.encoder[...], r.weights[3 + number, :, at], 1, 0
            ).astype(BF)

        tiles(features, 256, project)

    def enc_rows(at):
        return pl.ds(pl.multiple_of(at * enc, enc), enc)

    own_kv = r.cross_kv.at[:, enc_rows(depth), :]
    cross = Swap(here, lambda at: own_kv, lambda at: r.cross_kv.at[:, enc_rows(at), :])
    cross.begin()

    for work in qkv:
        work.arrive()

    def block_scores(number, block):
        keys = (block + 1) * tokens
        at = pl.ds(pl.multiple_of(number * head, head), head)
        query = r.qkv_h[0, at, block * tokens : keys]
        scores = times(r.qkv_h[1, at, :keys], query, 0, 0)
        bias = jnp.concatenate(
            [r.strip[number, :, (block - key) * tokens : (block - key + 1) * tokens] for key in range(block + 1)], axis=0
        )
        return scores + bias, at, keys, query

    def self_forward(number, carry):
        for block in range(count):
            scores, at, keys, _ = block_scores(number, block)
            top = jnp.max(scores, axis=0, keepdims=True)
            weights = jnp.exp(scores - top)
            total = jnp.sum(weights, axis=0, keepdims=True)
            mixed = times(r.qkv_h[2, at, :keys], weights.astype(BF), 1, 0)
            span = slice(block * tokens, keys)
            r.attn_h[at, span] = (mixed / total).astype(BF)
            r.lse[number, :, span] = top + jnp.log(total)
        return carry

    lax.fori_loop(0, mine, self_forward, 0)
    attn = Swap(here, lambda at: r.attn_h.at[:, token_lanes(at)], lambda at: r.attn_t.at[head_rows(at), :])
    attn.begin()
    own_block(r.attn_t.at[head_rows(depth), :], r.attn_h.at[:, token_lanes(depth)])

    for chunk in (2, 3, 4):
        gathers[chunk].z_phase()
    grads_in.relay()
    cross.arrive()
    for number in range(2):
        r.cross_t[number] = r.cross_kv[number].T
    attn.arrive()
    r.attn[...] = r.attn_t[...].T
    lefts[1].begin(1, r.attn)

    def after(at):
        r.x1[:, at] = r.hidden[:, at].astype(F32) + times(r.attn[...], r.weights[5, :, at], 1, 0)

    tiles(features, 256, after)
    h2 = (normed_of(r.x1[...])[0] * gain(1)).astype(BF)
    r.h2[...] = h2
    lefts[1].begin(2, r.h2)

    def project(at):
        r.cq_t[at, :] = times(r.h2[...], r.weights[6, :, at], 1, 0).astype(BF).T

    tiles(features, 256, project)

    def head_at(number):
        return pl.ds(pl.multiple_of(number * head, head), head)

    def cross_forward(number, carry):
        at = head_at(number)
        scores = times(r.cross_t[0, at, :], r.cq_t[at, :], 0, 0)
        top = jnp.max(scores, axis=0, keepdims=True)
        weights = jnp.exp(scores - top)
        total = jnp.sum(weights, axis=0, keepdims=True)
        mixed = times(r.cross_t[1, at, :], weights.astype(BF), 1, 0)
        r.cattn_t[at, :] = (mixed / total).astype(BF)
        r.clse[number] = top + jnp.log(total)
        return carry

    lax.fori_loop(0, heads, cross_forward, 0)
    r.cattn[...] = r.cattn_t[...].T
    lefts[1].begin(3, r.cattn)

    def after(at):
        r.x2[:, at] = r.x1[:, at] + times(r.cattn[...], r.weights[7, :, at], 1, 0)

    tiles(features, 256, after)
    r.h3[seq] = (normed_of(r.x2[...])[0] * gain(2)).astype(BF)
    h3 = SeqGather(here, r.h3)
    h3.begin()
    gathers[2].y_phase()
    gathers[3].y_phase()
    h3.relay()
    gathers[4].y_phase()
    grads_in.arrive()
    h3.arrive()

    group = 4 * tokens
    hidden_rows = r.h3[...].reshape(group, features)
    grad_rows = r.grads_in[...].reshape(group, features)
    root = math.sqrt(2.0 / math.pi)

    def feed(at):
        gate = times(hidden_rows, r.gate_quarter[:, at], 1, 0)
        linear = times(hidden_rows, r.linear_quarter[:, at], 1, 0)
        grad = times(grad_rows, r.down_quarter[at, :], 1, 1)
        square = gate * gate
        bent = jnp.tanh(root * gate * (1.0 + 0.044715 * square))
        half = 0.5 * (1.0 + bent)
        curve = gate * half
        slope = half + 0.5 * gate * (1.0 - bent * bent) * (root * (1.0 + 3 * 0.044715 * square))
        r.middle[:, at] = (curve * linear).astype(BF)
        r.grad_gate[:, at] = (grad * linear * slope).astype(BF)
        r.grad_linear[:, at] = (grad * curve).astype(BF)

    tiles(quarter, 256, feed)

    def back(at):
        upstream = times(r.grad_gate[...], r.gate_quarter[at, :], 1, 1) + times(
            r.grad_linear[...], r.linear_quarter[at, :], 1, 1
        )
        r.gh3[:, :, at] = upstream.reshape(4, tokens, -1).astype(BF)

    tiles(features, 256, back)
    gh3 = SeqSum(here, r.gh3, r.gh3_in)
    gh3.begin()

    def forth(at):
        r.lout[:, :, at] = times(r.middle[...], r.down_quarter[:, at], 1, 0).reshape(4, tokens, -1).astype(BF)

    tiles(features, 256, forth)
    lout = SeqSum(here, r.lout, r.lout_in)
    gh3.relay()
    lout.begin()

    def down_terms(at):
        r.down_terms[at, :] = times(r.middle[:, at], grad_rows, 0, 0).astype(BF)

    tiles(quarter, 256, down_terms)
    feeds = [
        Scatter(here, r.down_terms, tall, r.down_y, r.down_z, lambda q: r.out_down.at[q]),
        Scatter(here, r.gate_terms, rows, r.gate_y, r.gate_z, lambda q: r.out_gate.at[q]),
        Scatter(here, r.linear_terms, rows, r.linear_y, r.linear_z, lambda q: r.out_linear.at[q]),
    ]
    feeds[0].y_begin()

    def gate_terms(at):
        r.gate_terms[at, :] = times(hidden_of(at), r.grad_gate[...], 0, 0).astype(BF)

    def linear_terms(at):
        r.linear_terms[at, :] = times(hidden_of(at), r.grad_linear[...], 0, 0).astype(BF)

    def hidden_of(at):
        return r.h3[:, :, at].reshape(group, -1)

    tiles(features, 256, gate_terms)
    feeds[1].y_begin()
    lout.relay()
    tiles(features, 256, linear_terms)
    feeds[2].y_begin()

    grad_x2, gain_three = norm_back(gh3.arrive(), r.x2[...], gain(2))
    grad_x2 = r.out_grad[...].astype(F32) + grad_x2
    r.gx[...] = grad_x2
    rounded = grad_x2.astype(BF)
    r.rounded[...] = rounded
    rights[1].begin(3, r.rounded)

    def pull(at):
        r.grad_t[at, :] = times(r.rounded[...], r.weights[7, at, :], 1, 1).astype(BF).T

    tiles(features, 256, pull)

    def cross_backward(number, carry):
        at = head_at(number)
        grad = r.grad_t[at, :]
        delta = jnp.sum(grad.astype(F32) * r.cattn_t[at, :].astype(F32), axis=0, keepdims=True)
        query, keys = r.cq_t[at, :], r.cross_t[0, at, :]
        probs = jnp.exp(times(keys, query, 0, 0) - r.clse[number])
        terms = (probs * (times(r.cross_t[1, at, :], grad, 0, 0) - delta)).astype(BF)
        r.gq_t[at, :] = times(keys, terms, 1, 0).astype(BF)
        r.cross_terms_t[0, at, :] = times(query, terms, 1, 1)
        r.cross_terms_t[1, at, :] = times(grad, probs.astype(BF), 1, 1)
        return carry

    lax.fori_loop(0, heads, cross_backward, 0)
    for number in range(2):
        r.cross_terms[number] = r.cross_terms_t[number].T.astype(BF)
    cross_terms = Swap(here, lambda at: r.cross_terms.at[:, enc_rows(at), :], lambda at: r.cross_in.at[at])
    cross_terms.begin()
    r.cross_in[depth] = r.cross_terms[:, enc_rows(depth), :]
    r.gq[...] = r.gq_t[...].T
    rights[1].begin(2, r.gq)

    spread = [
        Scatter(
            here, r.terms.at[chunk], rows, r.terms_y.at[chunk], r.terms_z.at[chunk],
            lambda q, chunk=chunk: r.out_squares.at[4 * chunk + q],
        )
        for chunk in range(2)
    ]

    def square_terms(chunk):
        lefts[chunk].arrive()
        rights[chunk].arrive()
        heights = lefts[chunk].heights
        short = heights.index(enc)
        for which, height in ((seq != short, tokens), (seq == short, enc)):
            @pl.when(which)
            def _():
                def body(at):
                    left = r.left[chunk, :, :height, at].reshape(4 * height, -1)
                    right = r.right[chunk, :, :height, :].reshape(4 * height, features)
                    r.terms[chunk, at, :] = times(left, right, 0, 0).astype(BF)

                tiles(features, 256, body)

        spread[chunk].y_begin()


    def pull(at):
        r.up[:, at] = times(r.gq[...], r.weights[6, at, :], 1, 1)

    tiles(features, 256, pull)
    grad_x1, gain_two = norm_back(r.up[...], r.x1[...], gain(1))
    grad_x1 = r.gx[...] + grad_x1
    r.gx[...] = grad_x1
    r.rounded_one[...] = grad_x1.astype(BF)
    rights[1].begin(1, r.rounded_one)

    def pull(at):
        r.grad_t[at, :] = times(r.rounded_one[...], r.weights[5, at, :], 1, 1).astype(BF).T

    tiles(features, 256, pull)
    grad_attn = Swap(here, lambda at: r.grad_t.at[head_rows(at), :], lambda at: r.grad_h.at[:, token_lanes(at)])
    grad_attn.begin()
    own_block(r.grad_h.at[:, token_lanes(depth)], r.grad_t.at[head_rows(depth), :])

    feeds[0].y_phase()
    cross_terms.arrive()
    summed = r.cross_in[0].astype(F32)
    for at in range(1, count):
        summed = summed + r.cross_in[at].astype(F32)
    r.cross_sum[...] = summed.astype(BF)
    rights[0].begin(3, r.cross_sum.at[0])
    rights[1].begin(0, r.cross_sum.at[1])
    r.layer_out[...] = (r.x2[...] + lout.arrive()).astype(BF)

    def encoder_back(at):
        r.encoder_grad[:, at] = times(r.cross_sum[0], r.weights[3, at, :], 1, 1) + times(
            r.cross_sum[1], r.weights[4, at, :], 1, 1
        )

    tiles(features, 256, encoder_back)
    feeds[1].y_phase()

    grad_attn.arrive()

    def self_backward(number, carry):
        at = head_at(number)
        r.dkv[...] = jnp.zeros_like(r.dkv)
        r.strip_sum[...] = jnp.zeros_like(r.strip_sum)
        for block in range(count):
            scores, _, keys, query = block_scores(number, block)
            span = slice(block * tokens, keys)
            grad = r.grad_h[at, span]
            delta = jnp.sum(grad.astype(F32) * r.attn_h[at, span].astype(F32), axis=0, keepdims=True)
            probs = jnp.exp(scores - r.lse[number, :, span])
            grad_scores = probs * (times(r.qkv_h[2, at, :keys], grad, 0, 0) - delta)
            terms = grad_scores.astype(BF)
            r.dqkv_h[0, at, span] = times(r.qkv_h[1, at, :keys], terms, 1, 0).astype(BF)
            r.dkv[0, :, :keys] += times(query, terms, 1, 1)
            r.dkv[1, :, :keys] += times(grad, probs.astype(BF), 1, 1)
            for key in range(block + 1):
                lanes = slice((block - key) * tokens, (block - key + 1) * tokens)
                r.strip_sum[:, lanes] += grad_scores[key * tokens : (key + 1) * tokens, :]
        r.dqkv_h[1, at, :] = r.dkv[0].astype(BF)
        r.dqkv_h[2, at, :] = r.dkv[1].astype(BF)
        strip = r.strip_sum[...]
        step = 1
        while step < tokens:
            strip = jnp.where((key_at // step) % 2 == 1, pltpu.roll(strip, length - step, 1), strip)
            step *= 2
        r.small[0, pl.ds(mine * depth + number, 1), :length] = jnp.sum(strip, axis=0, keepdims=True)
        return carry

    r.small[0] = jnp.zeros(r.small.shape[1:], F32)
    lax.fori_loop(0, mine, self_backward, 0)
    dqkv = [
        Swap(
            here, lambda at, number=number: r.dqkv_h.at[number, :, token_lanes(at)],
            lambda at, number=number: r.dqkv_t.at[number, head_rows(at), :],
        )
        for number in range(3)
    ]
    for work in dqkv:
        work.begin()
    own_block(r.dqkv_t.at[:, head_rows(depth), :], r.dqkv_h.at[:, :, token_lanes(depth)])
    square_terms(1)
    feeds[2].y_phase()
    feeds[0].z_phase()
    feeds[1].z_phase()
    for work in gathers:
        work.drain()
    for copy in gain_sends:
        copy.wait_send()
    for work in (*lefts, *qkv, attn, cross, cross_terms, grad_attn, h3, grads_in, gh3, lout):
        work.drain()
    for number in range(3):
        dqkv[number].arrive()
        r.dqkv[number] = r.dqkv_t[number].T
        rights[0].begin(number, r.dqkv.at[number])
    feeds[2].z_phase()
    for work in feeds[:2]:
        work.out_phase()
    spread[1].y_phase()

    def pull(at):
        r.up[:, at] = (
            times(r.dqkv[0], r.weights[0, at, :], 1, 1)
            + times(r.dqkv[1], r.weights[1, at, :], 1, 1)
            + times(r.dqkv[2], r.weights[2, at, :], 1, 1)
        )

    tiles(features, 256, pull)
    grad_x0, gain_one = norm_back(r.up[...], r.hidden[...].astype(F32), gain(0))
    r.input_grad[...] = r.gx[...] + grad_x0
    for number, value in enumerate((gain_one, gain_two, gain_three)):
        r.small[0, heads + number : heads + number + 1, :] = value
    small = SmallSum(here, r.small, r.small_in, r.small_depth)
    small.begin()
    small.level(0)
    square_terms(0)
    feeds[2].out_phase()
    spread[1].z_phase()
    small.level(1)
    spread[0].y_phase()
    spread[1].out_phase()
    for work in feeds:
        work.finish()
    for source, whole in ((r.out_gate, r.whole_gate), (r.out_linear, r.whole_linear)):
        held = [source[at] for at in range(4)]
        whole[...] = jnp.concatenate(
            [held[at][:, number * tall : (number + 1) * tall] for number in range(2 * count) for at in range(4)], axis=1
        )
    small.level(2)
    spread[0].z_phase()
    for work in (*rights, *dqkv):
        work.drain()
    spread[1].finish()
    r.small_out[...] = small.finish()
    spread[0].out_phase()
    spread[0].finish()


def run_layer(hidden, encoder, out_grad, bias, squares, gate, linear, down, gains):
    count = lax.axis_size("ctx")
    tokens, features = hidden.shape
    enc = encoder.shape[0]
    rows, hidden_units = gate.shape
    heads = features // 64
    quarter = hidden_units // 4
    tall = down.shape[0] // 4
    length, states = count * tokens, count * enc
    mine = heads // count
    width = features // count
    head = features // heads
    small = (-(-(heads + 3) // 8) * 8, features)
    used = 96 * count
    vmem = pl.BlockSpec(memory_space=pltpu.VMEM)
    held = pl.BlockSpec(memory_space=pl.ANY)
    inputs = dict(
        hidden=(hidden, vmem),
        encoder=(encoder, vmem),
        out_grad=(out_grad, vmem),
        bias=(bias, vmem),
        **{f"square{number}": (member, held) for number, member in enumerate(squares)},
        gate=(gate, vmem),
        linear=(linear, vmem),
        down=(down, held),
        gains=(gains, vmem),
    )
    outputs = dict(
        layer_out=((tokens, features), BF),
        input_grad=((tokens, features), F32),
        encoder_grad=((enc, features), F32),
        small_out=(small, F32),
        out_squares=((8, rows, features), BF),
        out_down=((4, tall, features), BF),
        whole_gate=((rows, hidden_units), BF),
        whole_linear=((rows, hidden_units), BF),
    )
    square = (features, features)
    near = (count,)
    scratch = dict(
        weights=((8,) + square, BF),
        gate_quarter=((features, quarter), BF),
        linear_quarter=((features, quarter), BF),
        down_quarter=((quarter, features), BF),
        all_gains=((2 * count,) + gains.shape, BF),
        gain_rows=((16, features), F32),
        strip=((mine, tokens, length), F32),
        strip_sum=((tokens, length), F32),
        h1=((tokens, features), BF),
        h2=((tokens, features), BF),
        qkv_t=((3, features, tokens), BF),
        qkv_h=((3, width, length), BF),
        attn_h=((width, length), BF),
        attn_t=((features, tokens), BF),
        attn=((tokens, features), BF),
        lse=((mine, 1, length), F32),
        cross_kv=((2, states, features), BF),
        cross_t=((2, features, states), BF),
        cq_t=((features, tokens), BF),
        cattn_t=((features, tokens), BF),
        clse=((heads, 1, tokens), F32),
        x1=((tokens, features), F32),
        x2=((tokens, features), F32),
        gx=((tokens, features), F32),
        up=((tokens, features), F32),
        rounded=((tokens, features), BF),
        h3=((4, tokens, features), BF),
        grads_in=((4, tokens, features), BF),
        middle=((4 * tokens, quarter), BF),
        grad_gate=((4 * tokens, quarter), BF),
        grad_linear=((4 * tokens, quarter), BF),
        gh3=((4, tokens, features), BF),
        gh3_in=((3, tokens, features), BF),
        lout=((4, tokens, features), BF),
        lout_in=((3, tokens, features), BF),
        down_terms=((quarter, features), BF),
        gate_terms=((features, quarter), BF),
        linear_terms=((features, quarter), BF),
        down_y=((count, tall, features), BF),
        gate_y=((count, rows, quarter), BF),
        linear_y=((count, rows, quarter), BF),
        down_z=(near + (tall, features), BF),
        gate_z=(near + (rows, quarter), BF),
        linear_z=(near + (rows, quarter), BF),
        out_gate=((4, rows, quarter), BF),
        out_linear=((4, rows, quarter), BF),
        grad_t=((features, tokens), BF),
        gq_t=((features, tokens), BF),
        gq=((tokens, features), BF),
        cross_terms_t=((2, features, states), F32),
        cross_terms=((2, states, features), BF),
        cross_in=((count, 2, enc, features), BF),
        cross_sum=((2, enc, features), BF),
        terms=((2,) + square, BF),
        left=((2, 4, tokens, features), BF),
        right=((2, 4, tokens, features), BF),
        rounded_one=((tokens, features), BF),
        cattn=((tokens, features), BF),
        terms_y=((2, count, rows, features), BF),
        terms_z=((2,) + near + (rows, features), BF),
        grad_h=((width, length), BF),
        dkv=((2, head, length), F32),
        dqkv_h=((3, width, length), BF),
        dqkv_t=((3, features, tokens), BF),
        dqkv=((3, tokens, features), BF),
        small=((3,) + small, F32),
        small_in=((3,) + small, F32),
        small_depth=((count,) + small, F32),
    )
    names = list(inputs) + list(outputs) + list(scratch) + ["local", "sends", "recvs"]
    return pl.pallas_call(
        partial(layer_kernel, (count, tokens, features, enc, heads, quarter, rows, tall), names),
        out_shape=tuple(jax.ShapeDtypeStruct(shape, kind) for shape, kind in outputs.values()),
        in_specs=[spec for _, spec in inputs.values()],
        out_specs=[vmem] * len(outputs),
        scratch_shapes=[
            *(pltpu.VMEM(shape, kind) for shape, kind in scratch.values()),
            pltpu.SemaphoreType.DMA((9,)),
            pltpu.SemaphoreType.DMA((used,)),
            pltpu.SemaphoreType.DMA((used,)),
        ],
        compiler_params=pltpu.CompilerParams(
            collective_id=0, has_side_effects=True, vmem_limit_bytes=60 << 20
        ),
        cost_estimate=pl.CostEstimate(flops=8 * 10**9, bytes_accessed=10**7, transcendentals=10**6),
        name="layer",
    )(*(member for member, _ in inputs.values()))


def per_device_whole(
    hidden_in,
    encoder_states,
    out_grad,
    bucket_index,
    bias_table,
    self_gain,
    self_query,
    self_key,
    self_value,
    self_output,
    cross_gain,
    cross_query,
    cross_key,
    cross_value,
    cross_output,
    feed_gain,
    gate_weight,
    linear_weight,
    down_weight,
):
    count = lax.axis_size("ctx")
    rows, features = self_query.shape
    buckets, heads = bias_table.shape
    length = bucket_index.shape[0]
    mine = heads // count
    onehot = (bucket_index[:, None] == jnp.arange(buckets, dtype=jnp.int32)[None, :]).astype(jnp.float32)
    own_table = lax.dynamic_slice_in_dim(bias_table, lax.axis_index("ctx") * mine, mine, 1)
    own_table = jnp.pad(own_table, ((0, 0), (0, -mine % 8)))
    bias = jnp.dot(onehot, own_table, precision=HIGHEST).T
    gains = jnp.pad(jnp.stack([self_gain, cross_gain, feed_gain]), ((0, 13), (0, LANES - rows)))
    layer_out, input_grad, encoder_grad, small, squares, down, gate, linear = run_layer(
        hidden_in[0],
        encoder_states[0],
        out_grad[0],
        bias,
        (self_query, self_key, self_value, cross_key, cross_value, self_output, cross_query, cross_output),
        gate_weight,
        linear_weight,
        down_weight,
        gains,
    )
    grad_table = jnp.dot(onehot.T, small[:heads, :length].T, precision=HIGHEST)
    shard = lax.axis_index(("ctx", "fsdp"))
    gain_sums = lax.dynamic_slice_in_dim(small[heads : heads + 3], shard * rows, rows, 1)
    squares = squares.astype(jnp.float32)
    return (
        layer_out[None],
        input_grad[None],
        encoder_grad[None],
        grad_table,
        gain_sums[0],
        squares[0],
        squares[1],
        squares[2],
        squares[5],
        gain_sums[1],
        squares[6],
        squares[3],
        squares[4],
        squares[7],
        gain_sums[2],
        gate.astype(jnp.float32),
        linear.astype(jnp.float32),
        down.reshape(-1, features).astype(jnp.float32),
    )


def fits(mesh):
    return mesh.shape["seq"] == 4 and mesh.shape["fsdp"] == 2 and mesh.shape["ctx"] <= 4


def solution(mesh):
    return jax.shard_map(
        per_device_whole if fits(mesh) else per_device,
        mesh=mesh,
        in_specs=(
            P(("seq", "fsdp"), "ctx", None),
            P(("seq", "fsdp"), "ctx", None),
            P(("seq", "fsdp"), "ctx", None),
            P(),
            P(),
            P(("ctx", "fsdp")),
            P(("ctx", "fsdp"), None),
            P(("ctx", "fsdp"), None),
            P(("ctx", "fsdp"), None),
            P(("ctx", "fsdp"), None),
            P(("ctx", "fsdp")),
            P(("ctx", "fsdp"), None),
            P(("ctx", "fsdp"), None),
            P(("ctx", "fsdp"), None),
            P(("ctx", "fsdp"), None),
            P(("ctx", "fsdp")),
            P(("ctx", "fsdp"), None),
            P(("ctx", "fsdp"), None),
            P(("ctx", "fsdp"), None),
        ),
        out_specs=(
            P(("seq", "fsdp"), "ctx", None),
            P(("seq", "fsdp"), "ctx", None),
            P(("seq", "fsdp"), "ctx", None),
            P(),
            P(("ctx", "fsdp")),
            P(("ctx", "fsdp"), None),
            P(("ctx", "fsdp"), None),
            P(("ctx", "fsdp"), None),
            P(("ctx", "fsdp"), None),
            P(("ctx", "fsdp")),
            P(("ctx", "fsdp"), None),
            P(("ctx", "fsdp"), None),
            P(("ctx", "fsdp"), None),
            P(("ctx", "fsdp"), None),
            P(("ctx", "fsdp")),
            P(("ctx", "fsdp"), None),
            P(("ctx", "fsdp"), None),
            P(("ctx", "fsdp"), None),
        ),
        check_vma=False,
    )
```
